512 devices in a mesh: patch: 4 (over x), shot: 128 (over z, y, core).
Axes of the slice: x: 4, y: 8, z: 8, core: 2. Of those that a mesh axis runs over, the one named last changes fastest.
Arguments:
- estimate: bfloat16 [256, 512, 1024], P('shot', 'patch'), may hold values from -6 to 6
- observed: bfloat16 [256, 512, 1024], P('shot', 'patch'), may hold values from -6 to 6
- random_source_delays: int32 [256], replicated, may hold values from 0 to 255
- thresholds: float32 [512], replicated, may hold values from 0.5 to 3
Outputs:
- updated: float32 [256, 512, 1024], P('shot', 'patch')
- misfit: float32 [256], P('shot')
The draws below stay inside these ranges and needn't reach their ends.
All inputs are finite; a program needn't handle non-finite values.
Results may differ from the reference program's by a relative error of at most 0.0084.
Values may be sent and summed in bfloat16 or wider, within the bound.
A program may use at most 64 MiB of HBM per device.

```python
import math
import jax
import jax.numpy as jnp
from jax import lax

S = 256
R = 512
NT = 1024
F = 512
SOURCE_SPACING = 512
JITTER = 256


def plant(drawn, key, smallest, high):
    shape = drawn.shape
    spot = [jax.random.randint(jax.random.fold_in(key, axis), (), 0, shape[axis]) for axis in range(len(shape))]
    drawn = drawn.at[tuple(spot)].set(smallest)
    longest = shape.index(max(shape))
    spot[longest] = (spot[longest] + 1) % shape[longest]
    return drawn.at[tuple(spot)].set(high)


def levels(key, dims, shards, low, high):
    def one(position, blocks):
        steps = jax.random.uniform(jax.random.fold_in(jax.random.fold_in(key, 6), position), (blocks,), jnp.float32, low / len(shards), high / len(shards))
        return jnp.repeat(jnp.exp(steps), dims[position] // blocks).reshape((-1,) + (1,) * (len(dims) - position - 1))

    loudness = one(*shards[0])
    for cut in shards[1:]:
        loudness = loudness * one(*cut)
    return loudness


def bell_draw(own_key, extent, scale, reach, split=(), held_as=jnp.bfloat16):
    entries = jax.random.normal(own_key, extent, jnp.float32) * scale
    if len(split) > 0:
        entries = levels(own_key, extent, split, -0.22, 0.18) * entries
    return jnp.clip(entries, min=-reach, max=reach).astype(held_as)


def setup_inputs(seed: int = 0) -> dict:
    key_of = jax.random.split(jax.random.key(seed), 5)
    estimate = bell_draw(key_of[0], (S, R, NT), 1.0, 6.0, ((0, 128), (1, 4)))
    observed = bell_draw(key_of[1], (S, R, NT), 1.0, 6.0, ((0, 128), (1, 4)))
    random_source_delays = plant(jax.random.randint(key_of[2], (S,), 0, JITTER), jax.random.fold_in(key_of[2], 1), 0, JITTER - 1).astype(jnp.int32)
    thresholds = jnp.clip(jnp.exp(jax.random.uniform(key_of[3], (F,), jnp.float32, math.log(0.5), math.log(3.0))), 0.5, 3.0)
    return {"estimate": estimate, "observed": observed, "random_source_delays": random_source_delays, "thresholds": thresholds}


correction_step_length = 0.5

def delayed(traces, offset):
    length = traces.shape[-1]
    padded = jnp.pad(traces, ((0, 0), (length, length)))
    return lax.dynamic_slice_in_dim(padded, (length - offset).astype(jnp.int32), length, 1)

def combined_data_panel(field, random_source_delays):
    source_panels = field.shape[0]
    source_onset_moments = (jnp.arange(source_panels, dtype=jnp.int32) * SOURCE_SPACING + random_source_delays).astype(jnp.int32)
    padded = jnp.pad(field, ((1, 1), (0, 0), (0, 0)))

    def one_shot(source_position):
        before = lax.dynamic_index_in_dim(padded, source_position, 0, keepdims=False)
        center = lax.dynamic_index_in_dim(padded, source_position + 1, 0, keepdims=False)
        after = lax.dynamic_index_in_dim(padded, source_position + 2, 0, keepdims=False)
        subsequent_source_position = jnp.minimum(source_position + 1, source_panels - 1).astype(jnp.int32)
        prior_source_position = jnp.maximum(source_position - 1, 0).astype(jnp.int32)
        subsequent_source_panel = source_onset_moments[subsequent_source_position] - source_onset_moments[source_position]
        prior_source_panel = source_onset_moments[source_position] - source_onset_moments[prior_source_position]
        return center + delayed(after, subsequent_source_panel) + delayed(before, -prior_source_panel)
    return lax.map(one_shot, jnp.arange(source_panels, dtype=jnp.int32))

def time_tables():
    freq = jnp.arange(F, dtype=jnp.int32)
    sample = jnp.arange(NT, dtype=jnp.int32)
    phase = (freq[:, None] * sample[None, :] % NT).astype(jnp.float32)
    angle = 2.0 * jnp.pi * phase / NT
    root = jnp.sqrt(jnp.float32(NT))
    forward = jnp.stack([jnp.cos(angle) / root, -jnp.sin(angle) / root]).astype(jnp.bfloat16)
    weight = jnp.where(freq == 0, 1.0, 2.0).astype(jnp.float32)[:, None] / root
    inverse = jnp.stack([weight * jnp.cos(angle), -weight * jnp.sin(angle)]).astype(jnp.bfloat16)
    return (forward, inverse)

def shot_tables(source_panels):
    index = jnp.arange(source_panels, dtype=jnp.int32)
    phase = (index[:, None] * index[None, :] % source_panels).astype(jnp.float32)
    angle = 2.0 * jnp.pi * phase / source_panels
    root = jnp.sqrt(jnp.float32(source_panels))
    cosine = jnp.cos(angle) / root
    sine = jnp.sin(angle) / root
    across = jnp.stack([jnp.stack([cosine, sine]), jnp.stack([-sine, cosine])]).astype(jnp.bfloat16)
    back = jnp.stack([jnp.stack([cosine, -sine]), jnp.stack([sine, cosine])]).astype(jnp.bfloat16)
    return (across, back)

def shrink(wavenum, level):
    magnitude = jnp.sqrt(wavenum[0] * wavenum[0] + wavenum[1] * wavenum[1])
    factor = jnp.maximum(magnitude - level, 0.0) / jnp.maximum(magnitude, level)
    return (wavenum * factor[None]).astype(jnp.bfloat16)

def reference(estimate, observed, random_source_delays, thresholds):
    present_gather = estimate.astype(jnp.float32)
    resid = observed.astype(jnp.float32) - combined_data_panel(present_gather, random_source_delays)
    misfit = lax.optimization_barrier(jnp.sum(resid * resid, axis=(1, 2))) / (R * NT)
    advanced_estimate = (present_gather + correction_step_length * combined_data_panel(resid, random_source_delays)).astype(jnp.bfloat16)
    forward, inverse = time_tables()
    spectra = jnp.einsum('srt,pft->pfsr', advanced_estimate.astype(jnp.float32), forward.astype(jnp.float32)).astype(jnp.bfloat16)
    across, back = shot_tables(S)
    wavenum = jnp.einsum('pqks,qfsr->pfkr', across.astype(jnp.float32), spectra.astype(jnp.float32))
    shrunk = shrink(wavenum, thresholds[:, None, None])
    restored = jnp.einsum('pqks,qfsr->pfkr', back.astype(jnp.float32), shrunk.astype(jnp.float32)).astype(jnp.bfloat16)
    updated = jnp.einsum('pft,pfsr->srt', inverse.astype(jnp.float32), restored.astype(jnp.float32))
    return (updated, misfit)
```

```python
import functools
import math

import jax
import jax.numpy as jnp
import ml_dtypes
import numpy as np
from jax import lax
from jax.experimental import pallas as pl
from jax.experimental.pallas import tpu as pltpu
from jax.sharding import PartitionSpec as P

SOURCE_SPACING = 512
LONGEST = 768
ROWS = 16
MESH = pl.DeviceIdType.MESH


def time_table(frequencies, samples):
    phase = np.arange(frequencies)[:, None] * np.arange(samples)[None, :] % samples
    angle = 2.0 * math.pi * phase / samples
    table = np.stack([np.cos(angle), -np.sin(angle)], axis=1) / math.sqrt(samples)
    return table.reshape(2 * frequencies, samples).astype(np.float32).astype(ml_dtypes.bfloat16)


def shot_table(shots, here):
    index = np.arange(shots).reshape(shots // here, here).T.reshape(-1)
    angle = 2.0 * math.pi * (index[:, None] * index[None, :] % shots) / shots
    table = np.concatenate([np.cos(angle), np.sin(angle)]) / math.sqrt(shots)
    return table.astype(np.float32).astype(ml_dtypes.bfloat16)


def shift_left(x, lane, offset):
    length = x.shape[1]
    return jnp.where(lane < length - offset, pltpu.roll(x, length - offset, 1), 0.0)


def shift_right(x, lane, offset):
    return jnp.where(lane >= offset, pltpu.roll(x, offset, 1), 0.0)


def kernel(
    dims,
    est_hbm, obs_hbm, delay_hbm, level_hbm, table_hbm, cn_hbm,
    out_hbm, misfit_ref,
    est, obs, delay, level, table, cn,
    halo_out, halo_in, partial, stepped, energy, energies,
    send1, recv1, wide1, wide2, send2, recv2, out,
    load_sem, store_sem, halo_send, halo_recv, plane_sem,
    send1_sem, recv1_sem, send2_sem, recv2_sem, energy_send, energy_recv,
):
    patches, n, rings, ring = dims
    shots, receivers, length = est.shape
    bands = wide1.shape[0] // n // 4
    me, x = lax.axis_index("shot"), lax.axis_index("patch")
    z, place = me // ring, me % ring
    right, left = (me + 1) % n, (me + n - 1) % n
    last = n * shots - 1

    loads = [
        pltpu.make_async_copy(src, dst, load_sem.at[i])
        for i, (src, dst) in enumerate(
            [(delay_hbm, delay), (est_hbm, est), (obs_hbm, obs), (level_hbm, level), (table_hbm, table), (cn_hbm, cn)]
        )
    ]
    for load in loads:
        load.start()

    barrier = pltpu.get_barrier_semaphore()

    def greet_ring(i, carry):
        pl.semaphore_signal(barrier, 1, device_id={"shot": z * ring + (place + i) % ring}, device_id_type=MESH)
        return carry

    def greet_planes(i, carry):
        pl.semaphore_signal(barrier, 1, device_id={"shot": (z + i) % rings * ring + place}, device_id_type=MESH)
        return carry

    def greet_patches(i, carry):
        pl.semaphore_signal(barrier, 1, device_id={"patch": (x + i) % patches}, device_id_type=MESH)
        return carry

    pl.semaphore_signal(barrier, 1, device_id={"shot": right}, device_id_type=MESH)
    pl.semaphore_signal(barrier, 1, device_id={"shot": left}, device_id_type=MESH)
    lax.fori_loop(1, ring, greet_ring, 0)
    lax.fori_loop(1, rings, greet_planes, 0)
    lax.fori_loop(1, patches, greet_patches, 0)

    loads[0].wait()
    first = me * shots
    d_before = delay[jnp.maximum(first - 1, 0)]
    d_0 = delay[first]
    d_1 = delay[first + 1]
    d_after = delay[jnp.minimum(first + 2, last)]
    a_before = SOURCE_SPACING + d_0 - d_before
    a_here = SOURCE_SPACING + d_1 - d_0
    a_after = SOURCE_SPACING + d_after - d_1
    lane = lax.broadcasted_iota(jnp.int32, (ROWS, length), 1)
    loads[1].wait()
    loads[2].wait()

    def before_halo(i, carry):
        rows = pl.ds(i * ROWS, ROWS)
        e0 = est[0, rows, :].astype(jnp.float32)
        e1 = est[1, rows, :].astype(jnp.float32)
        p0 = obs[0, rows, :].astype(jnp.float32) - e0 - shift_right(e1, lane, a_here)
        p1 = obs[1, rows, :].astype(jnp.float32) - e1 - shift_left(e0, lane, a_here)
        partial[0, rows, :] = p0
        partial[1, rows, :] = p1
        halo_out[0, 0, rows, :] = shift_left(e1, lane, a_after)[:, :LONGEST].astype(jnp.bfloat16)
        halo_out[0, 1, rows, :] = shift_left(p1, lane, a_after)[:, :LONGEST].astype(jnp.bfloat16)
        halo_out[1, 0, rows, :] = shift_right(e0, lane, a_before)[:, length - LONGEST :].astype(jnp.bfloat16)
        halo_out[1, 1, rows, :] = shift_right(p0, lane, a_before)[:, length - LONGEST :].astype(jnp.bfloat16)
        return carry

    lax.fori_loop(0, receivers // ROWS, before_halo, 0)

    pl.semaphore_wait(barrier, ring - 1 + rings - 1 + patches - 1 + 2)

    halos = [
        pltpu.make_async_remote_copy(
            halo_out.at[side], halo_in.at[side], halo_send.at[side], halo_recv.at[side],
            device_id={"shot": peer}, device_id_type=MESH,
        )
        for side, peer in enumerate([right, left])
    ]
    for halo in halos:
        halo.start()

    def plane_ready(i, carry):
        pl.semaphore_signal(plane_sem, 1, device_id={"shot": (z + i) % rings * ring + place}, device_id_type=MESH)
        return carry

    lax.fori_loop(1, rings, plane_ready, 0)
    for load in loads[3:]:
        load.wait()
    for halo in halos:
        halo.wait_recv()

    def after_halo(i, carry):
        rows = pl.ds(i * ROWS, ROWS)
        e0 = est[0, rows, :].astype(jnp.float32)
        e1 = est[1, rows, :].astype(jnp.float32)
        blank = jnp.zeros((ROWS, length - LONGEST), jnp.float32)
        has_left = me > 0
        has_right = me < n - 1

        def from_left(kind):
            got = halo_in[0, kind, rows, :].astype(jnp.float32)
            return jnp.concatenate([jnp.where(has_left, got, 0.0), blank], axis=1)

        def from_right(kind):
            got = halo_in[1, kind, rows, :].astype(jnp.float32)
            return jnp.concatenate([blank, jnp.where(has_right, got, 0.0)], axis=1)

        r0 = partial[0, rows, :] - from_left(0)
        r1 = partial[1, rows, :] - from_right(0)
        own0 = jnp.where(lane < jnp.where(has_left, length - a_before, 0), e0, 0.0)
        own1 = jnp.where(lane >= jnp.where(has_right, a_after, length), e1, 0.0)
        s0 = e0 + 0.5 * (r0 + shift_right(r1, lane, a_here) + (from_left(1) - own0))
        s1 = e1 + 0.5 * (r1 + shift_left(r0, lane, a_here) + (from_right(1) - own1))
        stepped[rows, :] = s0.astype(jnp.bfloat16)
        stepped[pl.ds(receivers + i * ROWS, ROWS), :] = s1.astype(jnp.bfloat16)

        def squares(r):
            total = jnp.zeros((8, 128), jnp.float32)
            for a in range(0, ROWS, 8):
                for b in range(0, length, 128):
                    piece = r[a : a + 8, b : b + 128]
                    total = total + piece * piece
            return total

        return carry[0] + squares(r0), carry[1] + squares(r1)

    zero = jnp.zeros((8, 128), jnp.float32)
    e_0, e_1 = lax.fori_loop(0, receivers // ROWS, after_halo, (zero, zero))
    energy[0] = e_0
    energy[1] = e_1

    pl.semaphore_wait(plane_sem, rings - 1)

    def planes(offsets):
        field = stepped[...]
        for dz in offsets:
            zz = (z + dz) % rings
            rows = table[pl.ds(pl.multiple_of(zz * (ring * 8), ring * 8), ring * 8), :]
            got = lax.dot_general(rows, field, (((1,), (1,)), ((), ())), preferred_element_type=jnp.float32)
            tiles = [got[:, s * receivers : (s + 1) * receivers].reshape(ring, 8, receivers) for s in range(shots)]
            send1[pl.ds(zz * ring, ring)] = jnp.concatenate(tiles, axis=1).astype(jnp.bfloat16)

    def send_planes(offsets, src, dst, ssem, rsem):
        def one(i, carry):
            for dz in offsets:
                peer = (z + dz) % rings * ring + (place + i) % ring
                pltpu.make_async_remote_copy(
                    src(peer), dst(me), ssem, rsem, device_id={"shot": peer}, device_id_type=MESH
                ).start()
            return carry

        if 0 in offsets:
            far = tuple(dz for dz in offsets if dz)
            for dz in far:
                peer = (z + dz) % rings * ring + place
                pltpu.make_async_remote_copy(
                    src(peer), dst(me), ssem, rsem, device_id={"shot": peer}, device_id_type=MESH
                ).start()
            pltpu.make_async_copy(src(me), dst(me), rsem).start()
            lax.fori_loop(1, ring, one, 0)
        else:
            lax.fori_loop(0, ring, one, 0)

    half = rings // 2
    groups = [(half, 0)] + [(dz, rings - dz) for dz in range(half - 1, 0, -1)]
    for offsets in groups:
        planes(offsets)
        send_planes(offsets, lambda d: send1.at[d], lambda d: recv1.at[d], send1_sem, recv1_sem)

    for i in range(1, patches):
        pltpu.make_async_remote_copy(
            energy, energies.at[x], energy_send.at[i], energy_recv,
            device_id={"patch": (x + i) % patches}, device_id_type=MESH,
        ).start()
    pltpu.make_async_copy(energy, energies.at[x], energy_recv).start()

    pltpu.make_async_copy(recv1, recv1, recv1_sem).wait()

    wide1[...] = recv1[...].astype(jnp.float32).reshape(wide1.shape)
    wave = cn[...]
    k = n * shots
    for band in range(bands):
        columns = []
        for q in range(2):
            parts = [wide1[pl.ds(s * 8 + band * 2 + q, n, stride=16), :] for s in range(shots)]
            columns.append(jnp.concatenate(parts, axis=0))
        field = jnp.concatenate(columns, axis=1).astype(jnp.bfloat16)
        got = jnp.dot(wave, field, preferred_element_type=jnp.float32)
        real = got[:k, :receivers] + got[k:, receivers:]
        imag = got[:k, receivers:] - got[k:, :receivers]
        f = me * bands + band
        limit = level[f]
        weight = jnp.where(f == 0, 1.0, 2.0)
        magnitude = jnp.sqrt(real * real + imag * imag)
        factor = jnp.maximum(magnitude - limit, 0.0) / jnp.maximum(magnitude, limit) * weight
        shrunk = jnp.concatenate([real * factor, imag * factor], axis=1).astype(jnp.bfloat16)
        got = jnp.dot(wave, shrunk, preferred_element_type=jnp.float32)
        real = got[:k, :receivers] - got[k:, receivers:]
        imag = got[:k, receivers:] + got[k:, :receivers]
        for s in range(shots):
            wide2[pl.ds(s * 8 + band * 2, n, stride=16), :] = real[s * n : (s + 1) * n]
            wide2[pl.ds(s * 8 + band * 2 + 1, n, stride=16), :] = imag[s * n : (s + 1) * n]
    tiles = wide2[...].reshape(n, 16, receivers)
    for s in range(shots):
        send2[s] = tiles[:, s * 8 : (s + 1) * 8, :].astype(jnp.bfloat16)
    for offsets in groups:
        send_planes(offsets, lambda d: send2.at[:, d], lambda d: recv2.at[:, d], send2_sem, recv2_sem)

    pltpu.make_async_copy(energies, energies, energy_recv).wait()
    total = energies[0]
    for i in range(1, patches):
        total = total + energies[i]
    for s in range(shots):
        misfit_ref[s] = jnp.sum(total[s]) / (patches * receivers * length)

    pltpu.make_async_copy(recv2, recv2, recv2_sem).wait()

    stores = []
    for s in range(shots):
        field = recv2[s].astype(jnp.float32).reshape(n * 8, receivers).astype(jnp.bfloat16)
        out[s] = lax.dot_general(field, table[...], (((0,), (0,)), ((), ())), preferred_element_type=jnp.float32)
        stores.append(pltpu.make_async_copy(out.at[s], out_hbm.at[s], store_sem.at[s]))
        stores[-1].start()

    for halo in halos:
        halo.wait_send()
    for i in range(1, patches):
        pltpu.make_async_remote_copy(
            energy, energies.at[x], energy_send.at[i], energy_recv,
            device_id={"patch": (x + i) % patches}, device_id_type=MESH,
        ).wait_send()
    rest = pl.ds(0, n - 1)
    pltpu.make_async_copy(send1.at[rest], send1.at[rest], send1_sem).wait()
    pltpu.make_async_copy(send2.at[:, rest], send2.at[:, rest], send2_sem).wait()
    for store in stores:
        store.wait()


def local(dims, estimate, observed, delays, thresholds):
    shots, receivers, length = estimate.shape
    n = dims[1]
    frequencies = thresholds.shape[0]
    bf16, f32 = jnp.bfloat16, jnp.float32
    table = jnp.asarray(time_table(frequencies, length))
    cn = jnp.asarray(shot_table(n * shots, shots))
    bands = frequencies // n
    sem = pltpu.SemaphoreType.DMA
    return pl.pallas_call(
        functools.partial(kernel, dims),
        out_shape=(
            jax.ShapeDtypeStruct((shots, receivers, length), f32),
            jax.ShapeDtypeStruct((shots,), f32),
        ),
        in_specs=[pl.BlockSpec(memory_space=pl.ANY)] * 6,
        out_specs=(pl.BlockSpec(memory_space=pl.ANY), pl.BlockSpec(memory_space=pltpu.SMEM)),
        scratch_shapes=[
            pltpu.VMEM(estimate.shape, bf16),
            pltpu.VMEM(estimate.shape, bf16),
            pltpu.SMEM(delays.shape, jnp.int32),
            pltpu.SMEM(thresholds.shape, f32),
            pltpu.VMEM(table.shape, bf16),
            pltpu.VMEM(cn.shape, bf16),
            pltpu.VMEM((2, 2, receivers, LONGEST), bf16),
            pltpu.VMEM((2, 2, receivers, LONGEST), bf16),
            pltpu.VMEM(estimate.shape, f32),
            pltpu.VMEM((shots * receivers, length), bf16),
            pltpu.VMEM((shots, 8, 128), f32),
            pltpu.VMEM((dims[0], shots, 8, 128), f32),
            pltpu.VMEM((n, 16, receivers), bf16),
            pltpu.VMEM((n, 16, receivers), bf16),
            pltpu.VMEM((n * 4 * bands, receivers), f32),
            pltpu.VMEM((n * 4 * bands, receivers), f32),
            pltpu.VMEM((shots, n, 8, receivers), bf16),
            pltpu.VMEM((shots, n, 8, receivers), bf16),
            pltpu.VMEM(estimate.shape, f32),
            sem((6,)),
            sem((shots,)),
            sem((2,)),
            sem((2,)),
            pltpu.SemaphoreType.REGULAR,
            sem,
            sem,
            sem,
            sem,
            sem((dims[0],)),
            sem,
        ],
        compiler_params=pltpu.CompilerParams(
            collective_id=0, has_side_effects=True, vmem_limit_bytes=48 * 2**20
        ),
    )(estimate, observed, delays, thresholds, table, cn)


def solution(mesh):
    patches, n = mesh.shape["patch"], mesh.shape["shot"]
    rings = 8
    dims = (patches, n, rings, n // rings)
    in_specs = (P("shot", "patch", None), P("shot", "patch", None), P(), P())
    out_specs = (P("shot", "patch", None), P("shot"))
    return jax.shard_map(
        functools.partial(local, dims), mesh=mesh, in_specs=in_specs, out_specs=out_specs, check_vma=False
    )
```

```python
import functools
import math

import jax
import jax.numpy as jnp
import ml_dtypes
import numpy as np
from jax import lax
from jax.experimental import pallas as pl
from jax.experimental.pallas import tpu as pltpu
from jax.sharding import PartitionSpec as P

SOURCE_SPACING = 512
LONGEST = 768
ROWS = 16
MESH = pl.DeviceIdType.MESH


def time_table(frequencies, samples):
    phase = np.arange(frequencies)[:, None] * np.arange(samples)[None, :] % samples
    angle = 2.0 * math.pi * phase / samples
    table = np.stack([np.cos(angle), -np.sin(angle)], axis=1) / math.sqrt(samples)
    return table.reshape(2 * frequencies, samples).astype(np.float32).astype(ml_dtypes.bfloat16)


def shot_table(shots, here):
    index = np.arange(shots).reshape(shots // here, here).T.reshape(-1)
    angle = 2.0 * math.pi * (index[:, None] * index[None, :] % shots) / shots
    table = np.concatenate([np.cos(angle), np.sin(angle)]) / math.sqrt(shots)
    return table.astype(np.float32).astype(ml_dtypes.bfloat16)


def shift_left(x, lane, offset):
    length = x.shape[1]
    return jnp.where(lane < length - offset, pltpu.roll(x, length - offset, 1), 0.0)


def shift_right(x, lane, offset):
    return jnp.where(lane >= offset, pltpu.roll(x, offset, 1), 0.0)


def kernel(
    dims,
    est_hbm, obs_hbm, delay_hbm, level_hbm, table_hbm, cn_hbm,
    out_hbm, misfit_ref,
    est, obs, delay, level, table, cn,
    halo_out, halo_in, partial, stepped, energy, energies,
    send1, recv1, wide1, wide2, send2, recv2, out,
    load_sem, store_sem, halo_send, halo_recv, plane_sem,
    send1_sem, recv1_sem, send2_sem, recv2_sem, energy_send, energy_recv,
):
    patches, n, rings, ring = dims
    shots, receivers, length = est.shape
    bands = wide1.shape[0] // n // 4
    me, x = lax.axis_index("shot"), lax.axis_index("patch")
    z, place = me // ring, me % ring
    right, left = (me + 1) % n, (me + n - 1) % n
    last = n * shots - 1

    loads = [
        pltpu.make_async_copy(src, dst, load_sem.at[i])
        for i, (src, dst) in enumerate(
            [(delay_hbm, delay), (est_hbm, est), (obs_hbm, obs), (level_hbm, level), (table_hbm, table), (cn_hbm, cn)]
        )
    ]
    for load in loads:
        load.start()

    barrier = pltpu.get_barrier_semaphore()

    def greet_ring(i, carry):
        pl.semaphore_signal(barrier, 1, device_id={"shot": z * ring + (place + i) % ring}, device_id_type=MESH)
        return carry

    def greet_planes(i, carry):
        pl.semaphore_signal(barrier, 1, device_id={"shot": (z + i) % rings * ring + place}, device_id_type=MESH)
        return carry

    def greet_patches(i, carry):
        pl.semaphore_signal(barrier, 1, device_id={"patch": (x + i) % patches}, device_id_type=MESH)
        return carry

    pl.semaphore_signal(barrier, 1, device_id={"shot": right}, device_id_type=MESH)
    pl.semaphore_signal(barrier, 1, device_id={"shot": left}, device_id_type=MESH)
    lax.fori_loop(1, ring, greet_ring, 0)
    lax.fori_loop(1, rings, greet_planes, 0)
    lax.fori_loop(1, patches, greet_patches, 0)

    loads[0].wait()
    first = me * shots
    d_before = delay[jnp.maximum(first - 1, 0)]
    d_0 = delay[first]
    d_1 = delay[first + 1]
    d_after = delay[jnp.minimum(first + 2, last)]
    a_before = SOURCE_SPACING + d_0 - d_before
    a_here = SOURCE_SPACING + d_1 - d_0
    a_after = SOURCE_SPACING + d_after - d_1
    lane = lax.broadcasted_iota(jnp.int32, (ROWS, length), 1)
    loads[1].wait()
    loads[2].wait()

    def before_halo(i, carry):
        rows = pl.ds(i * ROWS, ROWS)
        e0 = est[0, rows, :].astype(jnp.float32)
        e1 = est[1, rows, :].astype(jnp.float32)
        p0 = obs[0, rows, :].astype(jnp.float32) - e0 - shift_right(e1, lane, a_here)
        p1 = obs[1, rows, :].astype(jnp.float32) - e1 - shift_left(e0, lane, a_here)
        partial[0, rows, :] = p0
        partial[1, rows, :] = p1
        halo_out[0, 0, rows, :] = shift_left(e1, lane, a_after)[:, :LONGEST].astype(jnp.bfloat16)
        halo_out[0, 1, rows, :] = shift_left(p1, lane, a_after)[:, :LONGEST].astype(jnp.bfloat16)
        halo_out[1, 0, rows, :] = shift_right(e0, lane, a_before)[:, length - LONGEST :].astype(jnp.bfloat16)
        halo_out[1, 1, rows, :] = shift_right(p0, lane, a_before)[:, length - LONGEST :].astype(jnp.bfloat16)
        return carry

    lax.fori_loop(0, receivers // ROWS, before_halo, 0)

    pl.semaphore_wait(barrier, ring - 1 + rings - 1 + patches - 1 + 2)

    halos = [
        pltpu.make_async_remote_copy(
            halo_out.at[side], halo_in.at[side], halo_send.at[side], halo_recv.at[side],
            device_id={"shot": peer}, device_id_type=MESH,
        )
        for side, peer in enumerate([right, left])
    ]
    for halo in halos:
        halo.start()

    def plane_ready(i, carry):
        pl.semaphore_signal(plane_sem, 1, device_id={"shot": (z + i) % rings * ring + place}, device_id_type=MESH)
        return carry

    lax.fori_loop(1, rings, plane_ready, 0)
    for load in loads[3:]:
        load.wait()
    for halo in halos:
        halo.wait_recv()

    def after_halo(i, carry):
        rows = pl.ds(i * ROWS, ROWS)
        e0 = est[0, rows, :].astype(jnp.float32)
        e1 = est[1, rows, :].astype(jnp.float32)
        blank = jnp.zeros((ROWS, length - LONGEST), jnp.float32)
        has_left = me > 0
        has_right = me < n - 1

        def from_left(kind):
            got = halo_in[0, kind, rows, :].astype(jnp.float32)
            return jnp.concatenate([jnp.where(has_left, got, 0.0), blank], axis=1)

        def from_right(kind):
            got = halo_in[1, kind, rows, :].astype(jnp.float32)
            return jnp.concatenate([blank, jnp.where(has_right, got, 0.0)], axis=1)

        r0 = partial[0, rows, :] - from_left(0)
        r1 = partial[1, rows, :] - from_right(0)
        own0 = jnp.where(lane < jnp.where(has_left, length - a_before, 0), e0, 0.0)
        own1 = jnp.where(lane >= jnp.where(has_right, a_after, length), e1, 0.0)
        s0 = e0 + 0.5 * (r0 + shift_right(r1, lane, a_here) + (from_left(1) - own0))
        s1 = e1 + 0.5 * (r1 + shift_left(r0, lane, a_here) + (from_right(1) - own1))
        stepped[rows, :] = s0.astype(jnp.bfloat16)
        stepped[pl.ds(receivers + i * ROWS, ROWS), :] = s1.astype(jnp.bfloat16)

        def squares(r):
            total = jnp.zeros((8, 128), jnp.float32)
            for a in range(0, ROWS, 8):
                for b in range(0, length, 128):
                    piece = r[a : a + 8, b : b + 128]
                    total = total + piece * piece
            return total

        return carry[0] + squares(r0), carry[1] + squares(r1)

    zero = jnp.zeros((8, 128), jnp.float32)
    e_0, e_1 = lax.fori_loop(0, receivers // ROWS, after_halo, (zero, zero))
    energy[0] = e_0
    energy[1] = e_1

    pl.semaphore_wait(plane_sem, rings - 1)

    def planes(offsets):
        field = stepped[...]
        for dz in offsets:
            zz = (z + dz) % rings
            rows = table[pl.ds(pl.multiple_of(zz * (ring * 8), ring * 8), ring * 8), :]
            got = lax.dot_general(rows, field, (((1,), (1,)), ((), ())), preferred_element_type=jnp.float32)
            tiles = [got[:, s * receivers : (s + 1) * receivers].reshape(ring, 8, receivers) for s in range(shots)]
            send1[pl.ds(zz * ring, ring)] = jnp.concatenate(tiles, axis=1).astype(jnp.bfloat16)

    def send_planes(offsets, src, dst, ssem, rsem):
        def one(i, carry):
            for dz in offsets:
                peer = (z + dz) % rings * ring + (place + i) % ring
                pltpu.make_async_remote_copy(
                    src(peer), dst(me), ssem, rsem, device_id={"shot": peer}, device_id_type=MESH
                ).start()
            return carry

        if 0 in offsets:
            far = tuple(dz for dz in offsets if dz)
            for dz in far:
                peer = (z + dz) % rings * ring + place
                pltpu.make_async_remote_copy(
                    src(peer), dst(me), ssem, rsem, device_id={"shot": peer}, device_id_type=MESH
                ).start()
            pltpu.make_async_copy(src(me), dst(me), rsem).start()
            lax.fori_loop(1, ring, one, 0)
        else:
            lax.fori_loop(0, ring, one, 0)

    half = rings // 2
    groups = [(half, 0)] + [(dz, rings - dz) for dz in range(half - 1, 0, -1)]
    for offsets in groups:
        planes(offsets)
        send_planes(offsets, lambda d: send1.at[d], lambda d: recv1.at[d], send1_sem, recv1_sem)

    for i in range(1, patches):
        pltpu.make_async_remote_copy(
            energy, energies.at[x], energy_send.at[i], energy_recv,
            device_id={"patch": (x + i) % patches}, device_id_type=MESH,
        ).start()
    pltpu.make_async_copy(energy, energies.at[x], energy_recv).start()

    pltpu.make_async_copy(recv1, recv1, recv1_sem).wait()

    wide1[...] = recv1[...].astype(jnp.float32).reshape(wide1.shape)
    wave = cn[...]
    k = n * shots
    for band in range(bands):
        columns = []
        for q in range(2):
            parts = [wide1[pl.ds(s * 8 + band * 2 + q, n, stride=16), :] for s in range(shots)]
            columns.append(jnp.concatenate(parts, axis=0))
        field = jnp.concatenate(columns, axis=1).astype(jnp.bfloat16)
        got = jnp.dot(wave, field, preferred_element_type=jnp.float32)
        real = got[:k, :receivers] + got[k:, receivers:]
        imag = got[:k, receivers:] - got[k:, :receivers]
        f = me * bands + band
        limit = level[f]
        weight = jnp.where(f == 0, 1.0, 2.0)
        magnitude = jnp.sqrt(real * real + imag * imag)
        factor = jnp.maximum(magnitude - limit, 0.0) / jnp.maximum(magnitude, limit) * weight
        shrunk = jnp.concatenate([real * factor, imag * factor], axis=1).astype(jnp.bfloat16)
        got = jnp.dot(wave, shrunk, preferred_element_type=jnp.float32)
        real = got[:k, :receivers] - got[k:, receivers:]
        imag = got[:k, receivers:] + got[k:, :receivers]
        for s in range(shots):
            wide2[pl.ds(s * 8 + band * 2, n, stride=16), :] = real[s * n : (s + 1) * n]
            wide2[pl.ds(s * 8 + band * 2 + 1, n, stride=16), :] = imag[s * n : (s + 1) * n]
    tiles = wide2[...].reshape(n, 16, receivers)
    for s in range(shots):
        send2[s] = tiles[:, s * 8 : (s + 1) * 8, :].astype(jnp.bfloat16)
    for offsets in groups:
        send_planes(offsets, lambda d: send2.at[:, d], lambda d: recv2.at[:, d], send2_sem, recv2_sem)

    pltpu.make_async_copy(energies, energies, energy_recv).wait()
    total = energies[0]
    for i in range(1, patches):
        total = total + energies[i]
    for s in range(shots):
        misfit_ref[s] = jnp.sum(total[s]) / (patches * receivers * length)

    pltpu.make_async_copy(recv2, recv2, recv2_sem).wait()

    stores = []
    for s in range(shots):
        field = recv2[s].astype(jnp.float32).reshape(n * 8, receivers).astype(jnp.bfloat16)
        out[s] = lax.dot_general(field, table[...], (((0,), (0,)), ((), ())), preferred_element_type=jnp.float32)
        stores.append(pltpu.make_async_copy(out.at[s], out_hbm.at[s], store_sem.at[s]))
        stores[-1].start()

    for halo in halos:
        halo.wait_send()
    for i in range(1, patches):
        pltpu.make_async_remote_copy(
            energy, energies.at[x], energy_send.at[i], energy_recv,
            device_id={"patch": (x + i) % patches}, device_id_type=MESH,
        ).wait_send()
    rest = pl.ds(0, n - 1)
    pltpu.make_async_copy(send1.at[rest], send1.at[rest], send1_sem).wait()
    pltpu.make_async_copy(send2.at[:, rest], send2.at[:, rest], send2_sem).wait()
    for store in stores:
        store.wait()


def local(dims, estimate, observed, delays, thresholds):
    shots, receivers, length = estimate.shape
    n = dims[1]
    frequencies = thresholds.shape[0]
    bf16, f32 = jnp.bfloat16, jnp.float32
    table = jnp.asarray(time_table(frequencies, length))
    cn = jnp.asarray(shot_table(n * shots, shots))
    bands = frequencies // n
    sem = pltpu.SemaphoreType.DMA
    return pl.pallas_call(
        functools.partial(kernel, dims),
        out_shape=(
            jax.ShapeDtypeStruct((shots, receivers, length), f32),
            jax.ShapeDtypeStruct((shots,), f32),
        ),
        in_specs=[pl.BlockSpec(memory_space=pl.ANY)] * 6,
        out_specs=(pl.BlockSpec(memory_space=pl.ANY), pl.BlockSpec(memory_space=pltpu.SMEM)),
        scratch_shapes=[
            pltpu.VMEM(estimate.shape, bf16),
            pltpu.VMEM(estimate.shape, bf16),
            pltpu.SMEM(delays.shape, jnp.int32),
            pltpu.SMEM(thresholds.shape, f32),
            pltpu.VMEM(table.shape, bf16),
            pltpu.VMEM(cn.shape, bf16),
            pltpu.VMEM((2, 2, receivers, LONGEST), bf16),
            pltpu.VMEM((2, 2, receivers, LONGEST), bf16),
            pltpu.VMEM(estimate.shape, f32),
            pltpu.VMEM((shots * receivers, length), bf16),
            pltpu.VMEM((shots, 8, 128), f32),
            pltpu.VMEM((dims[0], shots, 8, 128), f32),
            pltpu.VMEM((n, 16, receivers), bf16),
            pltpu.VMEM((n, 16, receivers), bf16),
            pltpu.VMEM((n * 4 * bands, receivers), f32),
            pltpu.VMEM((n * 4 * bands, receivers), f32),
            pltpu.VMEM((shots, n, 8, receivers), bf16),
            pltpu.VMEM((shots, n, 8, receivers), bf16),
            pltpu.VMEM(estimate.shape, f32),
            sem((6,)),
            sem((shots,)),
            sem((2,)),
            sem((2,)),
            pltpu.SemaphoreType.REGULAR,
            sem,
            sem,
            sem,
            sem,
            sem((dims[0],)),
            sem,
        ],
        compiler_params=pltpu.CompilerParams(
            collective_id=0, has_side_effects=True, vmem_limit_bytes=67_043_328
        ),
    )(estimate, observed, delays, thresholds, table, cn)


def solution(mesh):
    patches, n = mesh.shape["patch"], mesh.shape["shot"]
    rings = 8
    dims = (patches, n, rings, n // rings)
    in_specs = (P("shot", "patch", None), P("shot", "patch", None), P(), P())
    out_specs = (P("shot", "patch", None), P("shot"))
    return jax.shard_map(
        functools.partial(local, dims), mesh=mesh, in_specs=in_specs, out_specs=out_specs, check_vma=False
    )
```

```python
import functools
import math

import jax
import jax.numpy as jnp
import ml_dtypes
import numpy as np
from jax import lax
from jax.experimental import pallas as pl
from jax.experimental.pallas import tpu as pltpu
from jax.sharding import PartitionSpec as P

SOURCE_SPACING = 512
LONGEST = 768
ROWS = 16
MESH = pl.DeviceIdType.MESH


def time_table(frequencies, samples):
    phase = np.arange(frequencies)[:, None] * np.arange(samples)[None, :] % samples
    angle = 2.0 * math.pi * phase / samples
    table = np.stack([np.cos(angle), -np.sin(angle)], axis=1) / math.sqrt(samples)
    return table.reshape(2 * frequencies, samples).astype(np.float32).astype(ml_dtypes.bfloat16)


def shot_table(shots, here):
    index = np.arange(shots).reshape(shots // here, here).T.reshape(-1)
    angle = 2.0 * math.pi * (index[:, None] * index[None, :] % shots) / shots
    table = np.concatenate([np.cos(angle), np.sin(angle)]) / math.sqrt(shots)
    return table.astype(np.float32).astype(ml_dtypes.bfloat16)


def shift_left(x, lane, offset):
    length = x.shape[1]
    return jnp.where(lane < length - offset, pltpu.roll(x, (2 * length - offset) % length, 1), 0.0)


def shift_right(x, lane, offset):
    return jnp.where(lane >= offset, pltpu.roll(x, offset % x.shape[1], 1), 0.0)


def kernel(
    dims,
    est_hbm, obs_hbm, delay_hbm, level_hbm, table_hbm, cn_hbm,
    out, total,
    est, obs, delay, level, table, cn,
    halo_out, halo_in, est_in, partial, base, stepped, energy, energies,
    send1, recv1, wide1, wide2, send2, recv2,
    load_sem, halo_send, halo_recv, est_send, est_recv, plane_sem,
    send1_sem, recv1_sem, send2_sem, recv2_sem, energy_send, energy_recv,
):
    patches, n, rings, ring = dims
    shots, receivers, length = est.shape
    rest = length - LONGEST
    bands = wide1.shape[0] // n // 4
    me, x = lax.axis_index("shot"), lax.axis_index("patch")
    z, place = me // ring, me % ring
    right, left = (me + 1) % n, (me + n - 1) % n
    last = n * shots - 1

    loads = [
        pltpu.make_async_copy(src, dst, load_sem.at[i])
        for i, (src, dst) in enumerate(
            [(delay_hbm, delay), (est_hbm, est), (obs_hbm, obs), (level_hbm, level), (table_hbm, table), (cn_hbm, cn)]
        )
    ]
    for load in loads:
        load.start()

    barrier = pltpu.get_barrier_semaphore()

    def greet_ring(i, carry):
        pl.semaphore_signal(barrier, 1, device_id={"shot": z * ring + (place + i) % ring}, device_id_type=MESH)
        return carry

    def greet_planes(i, carry):
        pl.semaphore_signal(barrier, 1, device_id={"shot": (z + i) % rings * ring + place}, device_id_type=MESH)
        return carry

    def greet_patches(i, carry):
        pl.semaphore_signal(barrier, 1, device_id={"patch": (x + i) % patches}, device_id_type=MESH)
        return carry

    pl.semaphore_signal(barrier, 1, device_id={"shot": right}, device_id_type=MESH)
    pl.semaphore_signal(barrier, 1, device_id={"shot": left}, device_id_type=MESH)
    lax.fori_loop(1, ring, greet_ring, 0)
    lax.fori_loop(1, rings, greet_planes, 0)
    lax.fori_loop(1, patches, greet_patches, 0)

    loads[0].wait()
    first = me * shots
    delays = [delay[jnp.clip(first + i, 0, last)] for i in range(-2, 4)]
    a_prev, a_before, a_here, a_after, a_next = [SOURCE_SPACING + b - a for a, b in zip(delays, delays[1:])]
    has_left = me > 0
    has_right = me < n - 1
    lane = lax.broadcasted_iota(jnp.int32, (ROWS, length), 1)
    lane_rest = lax.broadcasted_iota(jnp.int32, (ROWS, rest), 1)
    loads[1].wait()
    loads[2].wait()

    def before_halo(i, carry):
        rows = pl.ds(i * ROWS, ROWS)
        e0 = est[0, rows, :].astype(jnp.float32)
        e1 = est[1, rows, :].astype(jnp.float32)
        p0 = obs[0, rows, :].astype(jnp.float32) - e0 - shift_right(e1, lane, a_here)
        p1 = obs[1, rows, :].astype(jnp.float32) - e1 - shift_left(e0, lane, a_here)
        partial[0, rows, :] = p0
        partial[1, rows, :] = p1
        once = shift_left(p1 - e1, lane, a_after)[:, :LONGEST]
        twice = shift_left(e1[:, LONGEST:], lane_rest, a_after + a_next - LONGEST)
        halo_out[0, rows, :] = jnp.concatenate([once, twice], axis=1).astype(jnp.bfloat16)
        once = shift_right(p0 - e0, lane, a_before)[:, rest:]
        twice = shift_right(e0[:, :rest], lane_rest, a_before + a_prev - LONGEST)
        halo_out[1, rows, :] = jnp.concatenate([once, twice], axis=1).astype(jnp.bfloat16)
        return carry

    lax.fori_loop(0, receivers // ROWS, before_halo, 0)

    pl.semaphore_wait(barrier, ring - 1 + rings - 1 + patches - 1 + 2)

    halos = [
        pltpu.make_async_remote_copy(
            halo_out.at[side], halo_in.at[side], halo_send.at[side], halo_recv.at[side],
            device_id={"shot": peer}, device_id_type=MESH,
        )
        for side, peer in enumerate([right, left])
    ]
    raw_halos = [
        pltpu.make_async_remote_copy(
            est.at[1 - side, :, pl.ds(rest * (1 - side), LONGEST)], est_in.at[side], est_send.at[side], est_recv.at[side],
            device_id={"shot": peer}, device_id_type=MESH,
        )
        for side, peer in enumerate([right, left])
    ]
    for halo in halos + raw_halos:
        halo.start()

    def plane_ready(i, carry):
        pl.semaphore_signal(plane_sem, 1, device_id={"shot": (z + i) % rings * ring + place}, device_id_type=MESH)
        return carry

    lax.fori_loop(1, rings, plane_ready, 0)

    def own_part(i, carry):
        rows = pl.ds(i * ROWS, ROWS)
        e0 = est[0, rows, :].astype(jnp.float32)
        e1 = est[1, rows, :].astype(jnp.float32)
        p0 = partial[0, rows, :]
        p1 = partial[1, rows, :]
        own0 = jnp.where(lane < jnp.where(has_left, length - a_before, 0), e0, 0.0)
        own1 = jnp.where(lane >= jnp.where(has_right, a_after, length), e1, 0.0)
        base[0, rows, :] = e0 + 0.5 * (p0 + shift_right(p1, lane, a_here) - own0)
        base[1, rows, :] = e1 + 0.5 * (p1 + shift_left(p0, lane, a_here) - own1)
        return carry

    lax.fori_loop(0, receivers // ROWS, own_part, 0)
    for load in loads[3:]:
        load.wait()
    for halo in halos:
        halo.wait_recv()

    def after_halo(i, carry):
        rows = pl.ds(i * ROWS, ROWS)
        from_left = jnp.where(has_left, halo_in[0, rows, :].astype(jnp.float32), 0.0)
        from_right = jnp.where(has_right, halo_in[1, rows, :].astype(jnp.float32), 0.0)
        h0 = jnp.concatenate([from_left[:, :LONGEST], -from_right[:, LONGEST:]], axis=1)
        h1 = jnp.concatenate([-from_left[:, LONGEST:], from_right[:, :LONGEST]], axis=1)
        stepped[rows, :] = (base[0, rows, :] + 0.5 * h0).astype(jnp.bfloat16)
        stepped[pl.ds(receivers + i * ROWS, ROWS), :] = (base[1, rows, :] + 0.5 * h1).astype(jnp.bfloat16)
        return carry

    lax.fori_loop(0, receivers // ROWS, after_halo, 0)

    pl.semaphore_wait(plane_sem, rings - 1)

    def planes(offsets):
        field = stepped[...]
        for dz in offsets:
            zz = (z + dz) % rings
            rows = table[pl.ds(pl.multiple_of(zz * (ring * 8), ring * 8), ring * 8), :]
            got = lax.dot_general(rows, field, (((1,), (1,)), ((), ())), preferred_element_type=jnp.float32)
            tiles = [got[:, s * receivers : (s + 1) * receivers].reshape(ring, 8, receivers) for s in range(shots)]
            send1[pl.ds(zz * ring, ring)] = jnp.concatenate(tiles, axis=1).astype(jnp.bfloat16)

    def send_planes(offsets, src, dst, ssem, rsem):
        def one(i, carry):
            for dz in offsets:
                peer = (z + dz) % rings * ring + (place + i) % ring
                pltpu.make_async_remote_copy(
                    src(peer), dst(me), ssem, rsem, device_id={"shot": peer}, device_id_type=MESH
                ).start()
            return carry

        if 0 in offsets:
            far = tuple(dz for dz in offsets if dz)
            for dz in far:
                peer = (z + dz) % rings * ring + place
                pltpu.make_async_remote_copy(
                    src(peer), dst(me), ssem, rsem, device_id={"shot": peer}, device_id_type=MESH
                ).start()
            pltpu.make_async_copy(src(me), dst(me), rsem).start()
            lax.fori_loop(1, ring, one, 0)
        else:
            lax.fori_loop(0, ring, one, 0)

    half = rings // 2
    groups = [(half, 0)] + [(dz, rings - dz) for dz in range(half - 1, 0, -1)]
    for offsets in groups:
        planes(offsets)
        send_planes(offsets, lambda d: send1.at[d], lambda d: recv1.at[d], send1_sem, recv1_sem)

    for halo in raw_halos:
        halo.wait_recv()

    def misfit_part(i, carry):
        rows = pl.ds(i * ROWS, ROWS)
        blank = jnp.zeros((ROWS, rest), jnp.float32)
        from_left = jnp.concatenate([blank, est_in[0, rows, :].astype(jnp.float32)], axis=1)
        from_right = jnp.concatenate([est_in[1, rows, :].astype(jnp.float32), blank], axis=1)
        r0 = partial[0, rows, :] - jnp.where(has_left, shift_left(from_left, lane, a_before), 0.0)
        r1 = partial[1, rows, :] - jnp.where(has_right, shift_right(from_right, lane, a_after), 0.0)

        def squares(r):
            parts = jnp.zeros((8, 128), jnp.float32)
            for a in range(0, ROWS, 8):
                for b in range(0, length, 128):
                    piece = r[a : a + 8, b : b + 128]
                    parts = parts + piece * piece
            return parts

        return carry[0] + squares(r0), carry[1] + squares(r1)

    zero = jnp.zeros((8, 128), jnp.float32)
    e_0, e_1 = lax.fori_loop(0, receivers // ROWS, misfit_part, (zero, zero))
    energy[0] = e_0
    energy[1] = e_1
    for i in range(1, patches):
        pltpu.make_async_remote_copy(
            energy, energies.at[x], energy_send.at[i], energy_recv,
            device_id={"patch": (x + i) % patches}, device_id_type=MESH,
        ).start()
    pltpu.make_async_copy(energy, energies.at[x], energy_recv).start()

    pltpu.make_async_copy(recv1, recv1, recv1_sem).wait()

    wide1[...] = recv1[...].astype(jnp.float32).reshape(wide1.shape)
    wave = cn[...]
    k = n * shots
    for band in range(bands):
        columns = []
        for q in range(2):
            parts = [wide1[pl.ds(s * 8 + band * 2 + q, n, stride=16), :] for s in range(shots)]
            columns.append(jnp.concatenate(parts, axis=0))
        field = jnp.concatenate(columns, axis=1).astype(jnp.bfloat16)
        got = jnp.dot(wave, field, preferred_element_type=jnp.float32)
        real = got[:k, :receivers] + got[k:, receivers:]
        imag = got[:k, receivers:] - got[k:, :receivers]
        f = me * bands + band
        limit = level[f]
        weight = jnp.where(f == 0, 1.0, 2.0)
        magnitude = jnp.sqrt(real * real + imag * imag)
        factor = jnp.maximum(magnitude - limit, 0.0) / jnp.maximum(magnitude, limit) * weight
        shrunk = jnp.concatenate([real * factor, imag * factor], axis=1).astype(jnp.bfloat16)
        got = jnp.dot(wave, shrunk, preferred_element_type=jnp.float32)
        real = got[:k, :receivers] - got[k:, receivers:]
        imag = got[:k, receivers:] + got[k:, :receivers]
        for s in range(shots):
            wide2[pl.ds(s * 8 + band * 2, n, stride=16), :] = real[s * n : (s + 1) * n]
            wide2[pl.ds(s * 8 + band * 2 + 1, n, stride=16), :] = imag[s * n : (s + 1) * n]
    tiles = wide2[...].reshape(n, 16, receivers)
    for s in range(shots):
        send2[s] = tiles[:, s * 8 : (s + 1) * 8, :].astype(jnp.bfloat16)
    for offsets in groups:
        send_planes(offsets, lambda d: send2.at[:, d], lambda d: recv2.at[:, d], send2_sem, recv2_sem)

    pltpu.make_async_copy(energies, energies, energy_recv).wait()
    total[...] = sum(energies[i] for i in range(patches))

    for halo in halos + raw_halos:
        halo.wait_send()
    for i in range(1, patches):
        pltpu.make_async_remote_copy(
            energy, energies.at[x], energy_send.at[i], energy_recv,
            device_id={"patch": (x + i) % patches}, device_id_type=MESH,
        ).wait_send()
    others = pl.ds(0, n - 1)
    pltpu.make_async_copy(send1.at[others], send1.at[others], send1_sem).wait()

    pltpu.make_async_copy(recv2, recv2, recv2_sem).wait()

    for s in range(shots):
        field = recv2[s].astype(jnp.float32).reshape(n * 8, receivers).astype(jnp.bfloat16)
        out[s] = lax.dot_general(field, table[...], (((0,), (0,)), ((), ())), preferred_element_type=jnp.float32)

    pltpu.make_async_copy(send2.at[:, others], send2.at[:, others], send2_sem).wait()


def finish(count, field, total, out, misfit, sems):
    shots = field.shape[0]
    copies = [pltpu.make_async_copy(field.at[s], out.at[s], sems.at[s]) for s in range(shots)]
    for copy in copies:
        copy.start()
    for s in range(shots):
        misfit[s] = jnp.sum(total[s]) / count
    for copy in copies:
        copy.wait()


def local(dims, estimate, observed, delays, thresholds):
    shots, receivers, length = estimate.shape
    n = dims[1]
    frequencies = thresholds.shape[0]
    bf16, f32 = jnp.bfloat16, jnp.float32
    table = jnp.asarray(time_table(frequencies, length))
    cn = jnp.asarray(shot_table(n * shots, shots))
    bands = frequencies // n
    sem = pltpu.SemaphoreType.DMA
    vmem = pl.BlockSpec(memory_space=pltpu.VMEM)
    operands = (estimate, observed, delays, thresholds, table, cn)
    field, total = pl.pallas_call(
        functools.partial(kernel, dims),
        out_shape=(
            jax.ShapeDtypeStruct((shots, receivers, length), f32),
            jax.ShapeDtypeStruct((shots, 8, 128), f32),
        ),
        in_specs=[pl.BlockSpec(memory_space=pltpu.HBM)] * 6,
        out_specs=(vmem, vmem),
        scratch_shapes=[
            pltpu.VMEM(estimate.shape, bf16),
            pltpu.VMEM(estimate.shape, bf16),
            pltpu.SMEM(delays.shape, jnp.int32),
            pltpu.SMEM(thresholds.shape, f32),
            pltpu.VMEM(table.shape, bf16),
            pltpu.VMEM(cn.shape, bf16),
            pltpu.VMEM((2, receivers, length), bf16),
            pltpu.VMEM((2, receivers, length), bf16),
            pltpu.VMEM((2, receivers, LONGEST), bf16),
            pltpu.VMEM(estimate.shape, f32),
            pltpu.VMEM(estimate.shape, f32),
            pltpu.VMEM((shots * receivers, length), bf16),
            pltpu.VMEM((shots, 8, 128), f32),
            pltpu.VMEM((dims[0], shots, 8, 128), f32),
            pltpu.VMEM((n, 16, receivers), bf16),
            pltpu.VMEM((n, 16, receivers), bf16),
            pltpu.VMEM((n * 4 * bands, receivers), f32),
            pltpu.VMEM((n * 4 * bands, receivers), f32),
            pltpu.VMEM((shots, n, 8, receivers), bf16),
            pltpu.VMEM((shots, n, 8, receivers), bf16),
            sem((6,)),
            sem((2,)),
            sem((2,)),
            sem((2,)),
            sem((2,)),
            pltpu.SemaphoreType.REGULAR,
            sem,
            sem,
            sem,
            sem,
            sem((dims[0],)),
            sem,
        ],
        compiler_params=pltpu.CompilerParams(
            collective_id=0, has_side_effects=True, vmem_limit_bytes=48 * 2**20
        ),
    )(*[pltpu.with_memory_space_constraint(v, pltpu.HBM) for v in operands])
    return pl.pallas_call(
        functools.partial(finish, dims[0] * receivers * length),
        out_shape=(jax.ShapeDtypeStruct(field.shape, f32), jax.ShapeDtypeStruct((shots,), f32)),
        in_specs=[vmem, vmem],
        out_specs=(pl.BlockSpec(memory_space=pltpu.HBM), pl.BlockSpec(memory_space=pltpu.SMEM)),
        scratch_shapes=[sem((shots,))],
        compiler_params=pltpu.CompilerParams(vmem_limit_bytes=8 * 2**20),
    )(field, total)


def solution(mesh):
    patches, n = mesh.shape["patch"], mesh.shape["shot"]
    rings = 8
    dims = (patches, n, rings, n // rings)
    in_specs = (P("shot", "patch", None), P("shot", "patch", None), P(), P())
    out_specs = (P("shot", "patch", None), P("shot"))
    return jax.shard_map(
        functools.partial(local, dims), mesh=mesh, in_specs=in_specs, out_specs=out_specs, check_vma=False
    )
```

```python
import functools
import math

import jax
import jax.numpy as jnp
import ml_dtypes
import numpy as np
from jax import lax
from jax.experimental import pallas as pl
from jax.experimental.pallas import tpu as pltpu
from jax.sharding import PartitionSpec as P

SOURCE_SPACING = 512
LONGEST = 768
ROWS = 16
MESH = pl.DeviceIdType.MESH


def time_table(frequencies, samples, n, halves):
    phase = np.arange(frequencies)[:, None] * np.arange(samples)[None, :] % samples
    angle = 2.0 * math.pi * phase / samples
    table = np.stack([np.cos(angle), -np.sin(angle)], axis=1) / math.sqrt(samples)
    table = table.reshape(n, halves, -1, samples).swapaxes(0, 1)
    return table.reshape(2 * frequencies, samples).astype(np.float32).astype(ml_dtypes.bfloat16)


def shot_table(shots, here):
    index = np.arange(shots).reshape(shots // here, here).T.reshape(-1)
    angle = 2.0 * math.pi * (index[:, None] * index[None, :] % shots) / shots
    table = np.concatenate([np.cos(angle), np.sin(angle)]) / math.sqrt(shots)
    return table.astype(np.float32).astype(ml_dtypes.bfloat16)


def shift_left(x, lane, offset):
    length = x.shape[1]
    return jnp.where(lane < length - offset, pltpu.roll(x, (2 * length - offset) % length, 1), 0.0)


def shift_right(x, lane, offset):
    return jnp.where(lane >= offset, pltpu.roll(x, offset % x.shape[1], 1), 0.0)


def kernel(
    dims,
    est_hbm, obs_hbm, delay_hbm, level_hbm, table_hbm, cn_hbm,
    out, total,
    est, obs, delay, level, table, cn,
    halo_out, halo_in, est_in, partial, base, stepped, energy, energies,
    send1, recv1, wide1, wide2, send2, recv2,
    load_sem, halo_send, halo_recv, est_send, est_recv, plane_sem,
    send1_sem, recv1_sem, send2_sem, recv2_sem, energy_send, energy_recv,
):
    patches, n, rings, ring = dims
    shots, receivers, length = est.shape
    rest = length - LONGEST
    halves = wide1.shape[0]
    bands = 2 * halves
    me, x = lax.axis_index("shot"), lax.axis_index("patch")
    z, place = me // ring, me % ring
    right, left = (me + 1) % n, (me + n - 1) % n
    last = n * shots - 1

    loads = [
        pltpu.make_async_copy(src, dst, load_sem.at[i])
        for i, (src, dst) in enumerate(
            [(delay_hbm, delay), (est_hbm, est), (obs_hbm, obs), (level_hbm, level), (table_hbm, table), (cn_hbm, cn)]
        )
    ]
    for load in loads:
        load.start()

    barrier = pltpu.get_barrier_semaphore()

    def greet_ring(i, carry):
        pl.semaphore_signal(barrier, 1, device_id={"shot": z * ring + (place + i) % ring}, device_id_type=MESH)
        return carry

    def greet_planes(i, carry):
        pl.semaphore_signal(barrier, 1, device_id={"shot": (z + i) % rings * ring + place}, device_id_type=MESH)
        return carry

    def greet_patches(i, carry):
        pl.semaphore_signal(barrier, 1, device_id={"patch": (x + i) % patches}, device_id_type=MESH)
        return carry

    pl.semaphore_signal(barrier, 1, device_id={"shot": right}, device_id_type=MESH)
    pl.semaphore_signal(barrier, 1, device_id={"shot": left}, device_id_type=MESH)
    lax.fori_loop(1, ring, greet_ring, 0)
    lax.fori_loop(1, rings, greet_planes, 0)
    lax.fori_loop(1, patches, greet_patches, 0)

    loads[0].wait()
    first = me * shots
    delays = [delay[jnp.clip(first + i, 0, last)] for i in range(-2, 4)]
    a_prev, a_before, a_here, a_after, a_next = [SOURCE_SPACING + b - a for a, b in zip(delays, delays[1:])]
    has_left = me > 0
    has_right = me < n - 1
    lane = lax.broadcasted_iota(jnp.int32, (ROWS, length), 1)
    lane_rest = lax.broadcasted_iota(jnp.int32, (ROWS, rest), 1)
    loads[1].wait()
    loads[2].wait()

    def before_halo(i, carry):
        rows = pl.ds(i * ROWS, ROWS)
        e0 = est[0, rows, :].astype(jnp.float32)
        e1 = est[1, rows, :].astype(jnp.float32)
        p0 = obs[0, rows, :].astype(jnp.float32) - e0 - shift_right(e1, lane, a_here)
        p1 = obs[1, rows, :].astype(jnp.float32) - e1 - shift_left(e0, lane, a_here)
        partial[0, rows, :] = p0
        partial[1, rows, :] = p1
        once = shift_left(p1 - e1, lane, a_after)[:, :LONGEST]
        twice = shift_left(e1[:, LONGEST:], lane_rest, a_after + a_next - LONGEST)
        halo_out[0, rows, :] = jnp.concatenate([once, twice], axis=1).astype(jnp.bfloat16)
        once = shift_right(p0 - e0, lane, a_before)[:, rest:]
        twice = shift_right(e0[:, :rest], lane_rest, a_before + a_prev - LONGEST)
        halo_out[1, rows, :] = jnp.concatenate([once, twice], axis=1).astype(jnp.bfloat16)
        return carry

    lax.fori_loop(0, receivers // ROWS, before_halo, 0)

    pl.semaphore_wait(barrier, ring - 1 + rings - 1 + patches - 1 + 2)

    halos = [
        pltpu.make_async_remote_copy(
            halo_out.at[side], halo_in.at[side], halo_send.at[side], halo_recv.at[side],
            device_id={"shot": peer}, device_id_type=MESH,
        )
        for side, peer in enumerate([right, left])
    ]
    raw_halos = [
        pltpu.make_async_remote_copy(
            est.at[1 - side, :, pl.ds(rest * (1 - side), LONGEST)], est_in.at[side], est_send.at[side], est_recv.at[side],
            device_id={"shot": peer}, device_id_type=MESH,
        )
        for side, peer in enumerate([right, left])
    ]
    for halo in halos + raw_halos:
        halo.start()

    def plane_ready(i, carry):
        pl.semaphore_signal(plane_sem, 1, device_id={"shot": (z + i) % rings * ring + place}, device_id_type=MESH)
        return carry

    lax.fori_loop(1, rings, plane_ready, 0)

    def own_part(i, carry):
        rows = pl.ds(i * ROWS, ROWS)
        e0 = est[0, rows, :].astype(jnp.float32)
        e1 = est[1, rows, :].astype(jnp.float32)
        p0 = partial[0, rows, :]
        p1 = partial[1, rows, :]
        own0 = jnp.where(lane < jnp.where(has_left, length - a_before, 0), e0, 0.0)
        own1 = jnp.where(lane >= jnp.where(has_right, a_after, length), e1, 0.0)
        base[0, rows, :] = e0 + 0.5 * (p0 + shift_right(p1, lane, a_here) - own0)
        base[1, rows, :] = e1 + 0.5 * (p1 + shift_left(p0, lane, a_here) - own1)
        return carry

    lax.fori_loop(0, receivers // ROWS, own_part, 0)
    for load in loads[3:]:
        load.wait()
    for halo in halos:
        halo.wait_recv()

    def after_halo(i, carry):
        rows = pl.ds(i * ROWS, ROWS)
        from_left = jnp.where(has_left, halo_in[0, rows, :].astype(jnp.float32), 0.0)
        from_right = jnp.where(has_right, halo_in[1, rows, :].astype(jnp.float32), 0.0)
        h0 = jnp.concatenate([from_left[:, :LONGEST], -from_right[:, LONGEST:]], axis=1)
        h1 = jnp.concatenate([-from_left[:, LONGEST:], from_right[:, :LONGEST]], axis=1)
        stepped[rows, :] = (base[0, rows, :] + 0.5 * h0).astype(jnp.bfloat16)
        stepped[pl.ds(receivers + i * ROWS, ROWS), :] = (base[1, rows, :] + 0.5 * h1).astype(jnp.bfloat16)
        return carry

    lax.fori_loop(0, receivers // ROWS, after_halo, 0)

    pl.semaphore_wait(plane_sem, rings - 1)

    upper = lax.broadcasted_iota(jnp.int32, (ring // 2, 8, receivers), 1) < 4

    def planes(h, offsets):
        field = stepped[...]
        starts = [pl.multiple_of((h * n + (z + dz) % rings * ring) * 4, 4 * ring) for dz in offsets]
        rows = jnp.concatenate([table[pl.ds(start, 4 * ring), :] for start in starts], axis=0)
        got = lax.dot_general(rows, field, (((1,), (1,)), ((), ())), preferred_element_type=jnp.float32)
        for j, dz in enumerate(offsets):
            pairs = got[j * 4 * ring : (j + 1) * 4 * ring].reshape(ring // 2, 8, shots * receivers)
            g0, g1 = pairs[:, :, :receivers], pairs[:, :, receivers:]
            even = jnp.where(upper, g0, pltpu.roll(g1, 4, 1))
            odd = jnp.where(upper, pltpu.roll(g0, 4, 1), g1)
            tiles = jnp.stack([even, odd], axis=1).reshape(ring, 8, receivers)
            send1[h, pl.ds((z + dz) % rings * ring, ring)] = tiles.astype(jnp.bfloat16)

    def send_planes(offsets, src, dst, ssem, rsem):
        def one(i, carry):
            for dz in offsets:
                peer = (z + dz) % rings * ring + (place + i) % ring
                pltpu.make_async_remote_copy(
                    src(peer), dst(me), ssem, rsem, device_id={"shot": peer}, device_id_type=MESH
                ).start()
            return carry

        if 0 in offsets:
            far = tuple(dz for dz in offsets if dz)
            for dz in far:
                peer = (z + dz) % rings * ring + place
                pltpu.make_async_remote_copy(
                    src(peer), dst(me), ssem, rsem, device_id={"shot": peer}, device_id_type=MESH
                ).start()
            pltpu.make_async_copy(src(me), dst(me), rsem).start()
            lax.fori_loop(1, ring, one, 0)
        else:
            lax.fori_loop(0, ring, one, 0)

    half = rings // 2
    groups = [(half, 0)] + [(dz, rings - dz) for dz in range(half - 1, 0, -1)]
    for h in range(halves):
        for offsets in groups:
            planes(h, offsets)
            send_planes(offsets, lambda d: send1.at[h, d], lambda d: recv1.at[h, d], send1_sem.at[h], recv1_sem.at[h])

    for halo in raw_halos:
        halo.wait_recv()

    def misfit_part(i, carry):
        rows = pl.ds(i * ROWS, ROWS)
        blank = jnp.zeros((ROWS, rest), jnp.float32)
        from_left = jnp.concatenate([blank, est_in[0, rows, :].astype(jnp.float32)], axis=1)
        from_right = jnp.concatenate([est_in[1, rows, :].astype(jnp.float32), blank], axis=1)
        r0 = partial[0, rows, :] - jnp.where(has_left, shift_left(from_left, lane, a_before), 0.0)
        r1 = partial[1, rows, :] - jnp.where(has_right, shift_right(from_right, lane, a_after), 0.0)

        def squares(r):
            parts = jnp.zeros((8, 128), jnp.float32)
            for a in range(0, ROWS, 8):
                for b in range(0, length, 128):
                    piece = r[a : a + 8, b : b + 128]
                    parts = parts + piece * piece
            return parts

        return carry[0] + squares(r0), carry[1] + squares(r1)

    zero = jnp.zeros((8, 128), jnp.float32)
    e_0, e_1 = lax.fori_loop(0, receivers // ROWS, misfit_part, (zero, zero))
    energy[0] = e_0
    energy[1] = e_1
    for i in range(1, patches):
        pltpu.make_async_remote_copy(
            energy, energies.at[x], energy_send.at[i], energy_recv,
            device_id={"patch": (x + i) % patches}, device_id_type=MESH,
        ).start()
    pltpu.make_async_copy(energy, energies.at[x], energy_recv).start()

    wave = cn[...]
    k = n * shots

    def shrink(h):
        w1, w2 = wide1.at[h], wide2.at[h]
        w1[...] = recv1[h].astype(jnp.float32).reshape(8 * n, receivers)
        for b in range(bands // halves):
            columns = []
            for q in range(2):
                parts = [w1[pl.ds(s * 4 + b * 2 + q, n, stride=8), :] for s in range(shots)]
                columns.append(jnp.concatenate(parts, axis=0))
            field = jnp.concatenate(columns, axis=1).astype(jnp.bfloat16)
            got = jnp.dot(wave, field, preferred_element_type=jnp.float32)
            real = got[:k, :receivers] + got[k:, receivers:]
            imag = got[:k, receivers:] - got[k:, :receivers]
            f = me * bands + h * (bands // halves) + b
            limit = level[f]
            weight = jnp.where(f == 0, 1.0, 2.0)
            magnitude = jnp.sqrt(real * real + imag * imag)
            factor = jnp.maximum(magnitude - limit, 0.0) / jnp.maximum(magnitude, limit) * weight
            shrunk = jnp.concatenate([real * factor, imag * factor], axis=1).astype(jnp.bfloat16)
            got = jnp.dot(wave, shrunk, preferred_element_type=jnp.float32)
            real = got[:k, :receivers] - got[k:, receivers:]
            imag = got[:k, receivers:] + got[k:, :receivers]
            for s in range(shots):
                w2[pl.ds(s * 4 + b * 2, n, stride=8), :] = real[s * n : (s + 1) * n]
                w2[pl.ds(s * 4 + b * 2 + 1, n, stride=8), :] = imag[s * n : (s + 1) * n]
        send2[h] = w2[...].reshape(n, 8, receivers).astype(jnp.bfloat16)

    for h in range(halves):
        pltpu.make_async_copy(recv1.at[h], recv1.at[h], recv1_sem.at[h]).wait()
        shrink(h)
        for offsets in groups:
            send_planes(offsets, lambda d: send2.at[h, d], lambda d: recv2.at[h, d], send2_sem.at[h], recv2_sem.at[h])

    pltpu.make_async_copy(energies, energies, energy_recv).wait()
    total[...] = sum(energies[i] for i in range(patches))

    for halo in halos + raw_halos:
        halo.wait_send()
    for i in range(1, patches):
        pltpu.make_async_remote_copy(
            energy, energies.at[x], energy_send.at[i], energy_recv,
            device_id={"patch": (x + i) % patches}, device_id_type=MESH,
        ).wait_send()
    others = pl.ds(0, n - 1)
    for h in range(halves):
        pltpu.make_async_copy(send1.at[h, others], send1.at[h, others], send1_sem.at[h]).wait()

    first_rows = lax.broadcasted_iota(jnp.int32, (n // 2, 8, receivers), 1) < 4
    for h in range(halves):
        pltpu.make_async_copy(recv2.at[h], recv2.at[h], recv2_sem.at[h]).wait()
        pairs = recv2[h].astype(jnp.float32).reshape(n // 2, 2, 8, receivers)
        even, odd = pairs[:, 0], pairs[:, 1]
        fields = [
            jnp.where(first_rows, even, pltpu.roll(odd, 4, 1)),
            jnp.where(first_rows, pltpu.roll(even, 4, 1), odd),
        ]
        rows = table[h * 4 * n : (h + 1) * 4 * n, :]
        for s in range(shots):
            field = fields[s].reshape(4 * n, receivers).astype(jnp.bfloat16)
            got = lax.dot_general(field, rows, (((0,), (0,)), ((), ())), preferred_element_type=jnp.float32)
            out[s] = got if h == 0 else out[s] + got

    for h in range(halves):
        pltpu.make_async_copy(send2.at[h, others], send2.at[h, others], send2_sem.at[h]).wait()


def finish(count, field, total, out, misfit, sems):
    shots = field.shape[0]
    copies = [pltpu.make_async_copy(field.at[s], out.at[s], sems.at[s]) for s in range(shots)]
    for copy in copies:
        copy.start()
    for s in range(shots):
        misfit[s] = jnp.sum(total[s]) / count
    for copy in copies:
        copy.wait()


def local(dims, estimate, observed, delays, thresholds):
    shots, receivers, length = estimate.shape
    n = dims[1]
    frequencies = thresholds.shape[0]
    bf16, f32 = jnp.bfloat16, jnp.float32
    bands = frequencies // n
    halves = bands // 2
    table = jnp.asarray(time_table(frequencies, length, n, halves))
    cn = jnp.asarray(shot_table(n * shots, shots))
    sem = pltpu.SemaphoreType.DMA
    vmem = pl.BlockSpec(memory_space=pltpu.VMEM)
    operands = (estimate, observed, delays, thresholds, table, cn)
    field, total = pl.pallas_call(
        functools.partial(kernel, dims),
        out_shape=(
            jax.ShapeDtypeStruct((shots, receivers, length), f32),
            jax.ShapeDtypeStruct((shots, 8, 128), f32),
        ),
        in_specs=[pl.BlockSpec(memory_space=pltpu.HBM)] * 6,
        out_specs=(vmem, vmem),
        scratch_shapes=[
            pltpu.VMEM(estimate.shape, bf16),
            pltpu.VMEM(estimate.shape, bf16),
            pltpu.SMEM(delays.shape, jnp.int32),
            pltpu.SMEM(thresholds.shape, f32),
            pltpu.VMEM(table.shape, bf16),
            pltpu.VMEM(cn.shape, bf16),
            pltpu.VMEM((2, receivers, length), bf16),
            pltpu.VMEM((2, receivers, length), bf16),
            pltpu.VMEM((2, receivers, LONGEST), bf16),
            pltpu.VMEM(estimate.shape, f32),
            pltpu.VMEM(estimate.shape, f32),
            pltpu.VMEM((shots * receivers, length), bf16),
            pltpu.VMEM((shots, 8, 128), f32),
            pltpu.VMEM((dims[0], shots, 8, 128), f32),
            pltpu.VMEM((halves, n, 8, receivers), bf16),
            pltpu.VMEM((halves, n, 8, receivers), bf16),
            pltpu.VMEM((halves, n * 8, receivers), f32),
            pltpu.VMEM((halves, n * 8, receivers), f32),
            pltpu.VMEM((halves, n, 8, receivers), bf16),
            pltpu.VMEM((halves, n, 8, receivers), bf16),
            sem((6,)),
            sem((2,)),
            sem((2,)),
            sem((2,)),
            sem((2,)),
            pltpu.SemaphoreType.REGULAR,
            sem((halves,)),
            sem((halves,)),
            sem((halves,)),
            sem((halves,)),
            sem((dims[0],)),
            sem,
        ],
        compiler_params=pltpu.CompilerParams(
            collective_id=0, has_side_effects=True, vmem_limit_bytes=48 * 2**20
        ),
    )(*[pltpu.with_memory_space_constraint(v, pltpu.HBM) for v in operands])
    return pl.pallas_call(
        functools.partial(finish, dims[0] * receivers * length),
        out_shape=(jax.ShapeDtypeStruct(field.shape, f32), jax.ShapeDtypeStruct((shots,), f32)),
        in_specs=[vmem, vmem],
        out_specs=(pl.BlockSpec(memory_space=pltpu.HBM), pl.BlockSpec(memory_space=pltpu.SMEM)),
        scratch_shapes=[sem((shots,))],
        compiler_params=pltpu.CompilerParams(vmem_limit_bytes=8 * 2**20),
    )(field, total)


def solution(mesh):
    patches, n = mesh.shape["patch"], mesh.shape["shot"]
    rings = 8
    dims = (patches, n, rings, n // rings)
    in_specs = (P("shot", "patch", None), P("shot", "patch", None), P(), P())
    out_specs = (P("shot", "patch", None), P("shot"))
    return jax.shard_map(
        functools.partial(local, dims), mesh=mesh, in_specs=in_specs, out_specs=out_specs, check_vma=False
    )
```

```python
import functools
import math

import jax
import jax.numpy as jnp
import ml_dtypes
import numpy as np
from jax import lax
from jax.experimental import pallas as pl
from jax.experimental.pallas import tpu as pltpu
from jax.sharding import PartitionSpec as P

SOURCE_SPACING = 512
LONGEST = 768
ROWS = 16
BLOCKS = 4
MESH = pl.DeviceIdType.MESH


def time_table(frequencies, samples, n, halves):
    phase = np.arange(frequencies)[:, None] * np.arange(samples)[None, :] % samples
    angle = 2.0 * math.pi * phase / samples
    table = np.stack([np.cos(angle), -np.sin(angle)], axis=1) / math.sqrt(samples)
    table = table.reshape(n, halves, -1, samples).swapaxes(0, 1)
    return table.reshape(2 * frequencies, samples).astype(np.float32).astype(ml_dtypes.bfloat16)


def shot_table(shots, here):
    index = np.arange(shots).reshape(shots // here, here).T.reshape(-1)
    angle = 2.0 * math.pi * (index[:, None] * index[None, :] % shots) / shots
    table = np.concatenate([np.cos(angle), np.sin(angle)]) / math.sqrt(shots)
    return table.astype(np.float32).astype(ml_dtypes.bfloat16)


def shift_left(x, lane, offset):
    length = x.shape[1]
    return jnp.where(lane < length - offset, pltpu.roll(x, (2 * length - offset) % length, 1), 0.0)


def shift_right(x, lane, offset):
    return jnp.where(lane >= offset, pltpu.roll(x, offset % x.shape[1], 1), 0.0)


def kernel(
    dims,
    est_hbm, obs_hbm, delay_hbm, level_hbm, table_hbm, cn_hbm,
    out, total,
    est, obs, delay, level, table, cn,
    halo_out, halo_in, est_in, partial, base, stepped, energy, energies,
    send1, recv1, wide1, wide2, send2, recv2,
    load_sem, record_sem, halo_send, halo_recv, est_send, est_recv, plane_sem,
    send1_sem, recv1_sem, send2_sem, recv2_sem, energy_send, energy_recv,
):
    patches, n, rings, ring = dims
    shots, receivers, length = est.shape
    rest = length - LONGEST
    halves = wide1.shape[0]
    bands = 2 * halves
    me, x = lax.axis_index("shot"), lax.axis_index("patch")
    z, place = me // ring, me % ring
    right, left = (me + 1) % n, (me + n - 1) % n
    last = n * shots - 1

    loads = [
        pltpu.make_async_copy(src, dst, load_sem.at[i])
        for i, (src, dst) in enumerate([(delay_hbm, delay), (level_hbm, level), (table_hbm, table), (cn_hbm, cn)])
    ]

    def record_loads(block):
        rows = pl.ds(block * (receivers // BLOCKS), receivers // BLOCKS)
        return [
            pltpu.make_async_copy(src.at[:, rows], dst.at[:, rows], record_sem.at[i, block])
            for i, (src, dst) in enumerate([(est_hbm, est), (obs_hbm, obs)])
        ]

    loads[0].start()
    for block in range(BLOCKS):
        for load in record_loads(block):
            load.start()
    for load in loads[1:]:
        load.start()

    barrier = pltpu.get_barrier_semaphore()

    def greet_ring(i, carry):
        pl.semaphore_signal(barrier, 1, device_id={"shot": z * ring + (place + i) % ring}, device_id_type=MESH)
        return carry

    def greet_planes(i, carry):
        pl.semaphore_signal(barrier, 1, device_id={"shot": (z + i) % rings * ring + place}, device_id_type=MESH)
        return carry

    def greet_patches(i, carry):
        pl.semaphore_signal(barrier, 1, device_id={"patch": (x + i) % patches}, device_id_type=MESH)
        return carry

    pl.semaphore_signal(barrier, 1, device_id={"shot": right}, device_id_type=MESH)
    pl.semaphore_signal(barrier, 1, device_id={"shot": left}, device_id_type=MESH)
    lax.fori_loop(1, ring, greet_ring, 0)
    lax.fori_loop(1, rings, greet_planes, 0)
    lax.fori_loop(1, patches, greet_patches, 0)

    loads[0].wait()
    first = me * shots
    delays = [delay[jnp.clip(first + i, 0, last)] for i in range(-2, 4)]
    a_prev, a_before, a_here, a_after, a_next = [SOURCE_SPACING + b - a for a, b in zip(delays, delays[1:])]
    has_left = me > 0
    has_right = me < n - 1
    lane = lax.broadcasted_iota(jnp.int32, (ROWS, length), 1)
    lane_rest = lax.broadcasted_iota(jnp.int32, (ROWS, rest), 1)

    def before_halo(i, carry):
        rows = pl.ds(i * ROWS, ROWS)
        e0 = est[0, rows, :].astype(jnp.float32)
        e1 = est[1, rows, :].astype(jnp.float32)
        p0 = obs[0, rows, :].astype(jnp.float32) - e0 - shift_right(e1, lane, a_here)
        p1 = obs[1, rows, :].astype(jnp.float32) - e1 - shift_left(e0, lane, a_here)
        partial[0, rows, :] = p0
        partial[1, rows, :] = p1
        once = shift_left(p1 - e1, lane, a_after)[:, :LONGEST]
        twice = shift_left(e1[:, LONGEST:], lane_rest, a_after + a_next - LONGEST)
        halo_out[0, rows, :] = jnp.concatenate([once, twice], axis=1).astype(jnp.bfloat16)
        once = shift_right(p0 - e0, lane, a_before)[:, rest:]
        twice = shift_right(e0[:, :rest], lane_rest, a_before + a_prev - LONGEST)
        halo_out[1, rows, :] = jnp.concatenate([once, twice], axis=1).astype(jnp.bfloat16)
        return carry

    def halo_copies(block):
        rows = pl.ds(block * (receivers // BLOCKS), receivers // BLOCKS)
        return [
            pltpu.make_async_remote_copy(
                halo_out.at[side, rows], halo_in.at[side, rows], halo_send.at[side, block], halo_recv.at[side, block],
                device_id={"shot": peer}, device_id_type=MESH,
            )
            for side, peer in enumerate([right, left])
        ]

    steps = receivers // ROWS // BLOCKS
    for block in range(BLOCKS):
        for load in record_loads(block):
            load.wait()
        lax.fori_loop(block * steps, (block + 1) * steps, before_halo, 0)
        if block == 0:
            pl.semaphore_wait(barrier, ring - 1 + rings - 1 + patches - 1 + 2)
        for halo in halo_copies(block):
            halo.start()

    raw_halos = [
        pltpu.make_async_remote_copy(
            est.at[1 - side, :, pl.ds(rest * (1 - side), LONGEST)], est_in.at[side], est_send.at[side], est_recv.at[side],
            device_id={"shot": peer}, device_id_type=MESH,
        )
        for side, peer in enumerate([right, left])
    ]
    for halo in raw_halos:
        halo.start()

    def plane_ready(i, carry):
        pl.semaphore_signal(plane_sem, 1, device_id={"shot": (z + i) % rings * ring + place}, device_id_type=MESH)
        return carry

    lax.fori_loop(1, rings, plane_ready, 0)

    def own_part(i, carry):
        rows = pl.ds(i * ROWS, ROWS)
        e0 = est[0, rows, :].astype(jnp.float32)
        e1 = est[1, rows, :].astype(jnp.float32)
        p0 = partial[0, rows, :]
        p1 = partial[1, rows, :]
        own0 = jnp.where(lane < jnp.where(has_left, length - a_before, 0), e0, 0.0)
        own1 = jnp.where(lane >= jnp.where(has_right, a_after, length), e1, 0.0)
        base[0, rows, :] = e0 + 0.5 * (p0 + shift_right(p1, lane, a_here) - own0)
        base[1, rows, :] = e1 + 0.5 * (p1 + shift_left(p0, lane, a_here) - own1)
        return carry

    lax.fori_loop(0, receivers // ROWS, own_part, 0)
    for load in loads[1:]:
        load.wait()

    def after_halo(i, carry):
        rows = pl.ds(i * ROWS, ROWS)
        from_left = jnp.where(has_left, halo_in[0, rows, :].astype(jnp.float32), 0.0)
        from_right = jnp.where(has_right, halo_in[1, rows, :].astype(jnp.float32), 0.0)
        h0 = jnp.concatenate([from_left[:, :LONGEST], -from_right[:, LONGEST:]], axis=1)
        h1 = jnp.concatenate([-from_left[:, LONGEST:], from_right[:, :LONGEST]], axis=1)
        stepped[rows, :] = (base[0, rows, :] + 0.5 * h0).astype(jnp.bfloat16)
        stepped[pl.ds(receivers + i * ROWS, ROWS), :] = (base[1, rows, :] + 0.5 * h1).astype(jnp.bfloat16)
        return carry

    for block in range(BLOCKS):
        for halo in halo_copies(block):
            halo.wait_recv()
        lax.fori_loop(block * steps, (block + 1) * steps, after_halo, 0)

    pl.semaphore_wait(plane_sem, rings - 1)

    upper = lax.broadcasted_iota(jnp.int32, (ring // 2, 8, receivers), 1) < 4

    def planes(h, offsets):
        field = stepped[...]
        starts = [pl.multiple_of((h * n + (z + dz) % rings * ring) * 4, 4 * ring) for dz in offsets]
        rows = jnp.concatenate([table[pl.ds(start, 4 * ring), :] for start in starts], axis=0)
        got = lax.dot_general(rows, field, (((1,), (1,)), ((), ())), preferred_element_type=jnp.float32)
        for j, dz in enumerate(offsets):
            pairs = got[j * 4 * ring : (j + 1) * 4 * ring].reshape(ring // 2, 8, shots * receivers)
            g0, g1 = pairs[:, :, :receivers], pairs[:, :, receivers:]
            even = jnp.where(upper, g0, pltpu.roll(g1, 4, 1))
            odd = jnp.where(upper, pltpu.roll(g0, 4, 1), g1)
            tiles = jnp.stack([even, odd], axis=1).reshape(ring, 8, receivers)
            send1[h, pl.ds((z + dz) % rings * ring, ring)] = tiles.astype(jnp.bfloat16)

    def send_shell(hops, src, dst, ssem, rsem):
        for far_z in range(half + 1):
            far_y = hops - far_z
            if not 0 <= far_y <= half:
                continue
            both_z, both_y = far_z % half > 0, far_y % half > 0

            def one(i, carry):
                dz, dy = far_z, far_y
                rest_of = i // 2
                if both_y:
                    dy = far_y + lax.rem(rest_of, 2) * (rings - 2 * far_y)
                    rest_of = rest_of // 2
                if both_z:
                    dz = far_z + rest_of * (rings - 2 * far_z)
                peer = lax.rem(z + dz, rings) * ring + lax.rem(place // 2 + dy, rings) * 2 + lax.rem(place + i, 2)
                pltpu.make_async_remote_copy(
                    src(peer), dst(me), ssem, rsem, device_id={"shot": peer}, device_id_type=MESH
                ).start()
                return carry

            if hops == 0:
                pltpu.make_async_copy(src(me), dst(me), rsem).start()
            lax.fori_loop(1 if hops == 0 else 0, 2 * (1 + both_z) * (1 + both_y), one, 0)

    half = rings // 2
    for h in range(halves):
        for hops in range(2 * half, -1, -1):
            near = hops - half
            if near >= 0:
                planes(h, sorted({near, (rings - near) % rings}))
            send_shell(hops, lambda d: send1.at[h, d], lambda d: recv1.at[h, d], send1_sem.at[h], recv1_sem.at[h])

    for halo in raw_halos:
        halo.wait_recv()

    def misfit_part(i, carry):
        rows = pl.ds(i * ROWS, ROWS)
        blank = jnp.zeros((ROWS, rest), jnp.float32)
        from_left = jnp.concatenate([blank, est_in[0, rows, :].astype(jnp.float32)], axis=1)
        from_right = jnp.concatenate([est_in[1, rows, :].astype(jnp.float32), blank], axis=1)
        r0 = partial[0, rows, :] - jnp.where(has_left, shift_left(from_left, lane, a_before), 0.0)
        r1 = partial[1, rows, :] - jnp.where(has_right, shift_right(from_right, lane, a_after), 0.0)

        def squares(r):
            parts = jnp.zeros((8, 128), jnp.float32)
            for a in range(0, ROWS, 8):
                for b in range(0, length, 128):
                    piece = r[a : a + 8, b : b + 128]
                    parts = parts + piece * piece
            return parts

        return carry[0] + squares(r0), carry[1] + squares(r1)

    zero = jnp.zeros((8, 128), jnp.float32)
    e_0, e_1 = lax.fori_loop(0, receivers // ROWS, misfit_part, (zero, zero))
    energy[0] = e_0
    energy[1] = e_1
    for i in range(1, patches):
        pltpu.make_async_remote_copy(
            energy, energies.at[x], energy_send.at[i], energy_recv,
            device_id={"patch": (x + i) % patches}, device_id_type=MESH,
        ).start()
    pltpu.make_async_copy(energy, energies.at[x], energy_recv).start()

    wave = cn[...]
    k = n * shots

    def shrink(h):
        w1, w2 = wide1.at[h], wide2.at[h]
        w1[...] = recv1[h].astype(jnp.float32).reshape(8 * n, receivers)
        for b in range(bands // halves):
            columns = []
            for q in range(2):
                parts = [w1[pl.ds(s * 4 + b * 2 + q, n, stride=8), :] for s in range(shots)]
                columns.append(jnp.concatenate(parts, axis=0))
            field = jnp.concatenate(columns, axis=1).astype(jnp.bfloat16)
            got = jnp.dot(wave, field, preferred_element_type=jnp.float32)
            real = got[:k, :receivers] + got[k:, receivers:]
            imag = got[:k, receivers:] - got[k:, :receivers]
            f = me * bands + h * (bands // halves) + b
            limit = level[f]
            weight = jnp.where(f == 0, 1.0, 2.0)
            magnitude = jnp.sqrt(real * real + imag * imag)
            factor = jnp.maximum(magnitude - limit, 0.0) / jnp.maximum(magnitude, limit) * weight
            shrunk = jnp.concatenate([real * factor, imag * factor], axis=1).astype(jnp.bfloat16)
            got = jnp.dot(wave, shrunk, preferred_element_type=jnp.float32)
            real = got[:k, :receivers] - got[k:, receivers:]
            imag = got[:k, receivers:] + got[k:, :receivers]
            for s in range(shots):
                w2[pl.ds(s * 4 + b * 2, n, stride=8), :] = real[s * n : (s + 1) * n]
                w2[pl.ds(s * 4 + b * 2 + 1, n, stride=8), :] = imag[s * n : (s + 1) * n]
        send2[h] = w2[...].reshape(n, 8, receivers).astype(jnp.bfloat16)

    for h in range(halves):
        pltpu.make_async_copy(recv1.at[h], recv1.at[h], recv1_sem.at[h]).wait()
        shrink(h)
        for hops in range(2 * half, -1, -1):
            send_shell(hops, lambda d: send2.at[h, d], lambda d: recv2.at[h, d], send2_sem.at[h], recv2_sem.at[h])

    pltpu.make_async_copy(energies, energies, energy_recv).wait()
    total[...] = sum(energies[i] for i in range(patches))

    for block in range(BLOCKS):
        for halo in halo_copies(block):
            halo.wait_send()
    for halo in raw_halos:
        halo.wait_send()
    for i in range(1, patches):
        pltpu.make_async_remote_copy(
            energy, energies.at[x], energy_send.at[i], energy_recv,
            device_id={"patch": (x + i) % patches}, device_id_type=MESH,
        ).wait_send()
    others = pl.ds(0, n - 1)
    for h in range(halves):
        pltpu.make_async_copy(send1.at[h, others], send1.at[h, others], send1_sem.at[h]).wait()

    first_rows = lax.broadcasted_iota(jnp.int32, (n // 2, 8, receivers), 1) < 4
    for h in range(halves):
        pltpu.make_async_copy(recv2.at[h], recv2.at[h], recv2_sem.at[h]).wait()
        pairs = recv2[h].astype(jnp.float32).reshape(n // 2, 2, 8, receivers)
        even, odd = pairs[:, 0], pairs[:, 1]
        fields = [
            jnp.where(first_rows, even, pltpu.roll(odd, 4, 1)),
            jnp.where(first_rows, pltpu.roll(even, 4, 1), odd),
        ]
        rows = table[h * 4 * n : (h + 1) * 4 * n, :]
        for s in range(shots):
            field = fields[s].reshape(4 * n, receivers).astype(jnp.bfloat16)
            got = lax.dot_general(field, rows, (((0,), (0,)), ((), ())), preferred_element_type=jnp.float32)
            out[s] = got if h == 0 else out[s] + got

    for h in range(halves):
        pltpu.make_async_copy(send2.at[h, others], send2.at[h, others], send2_sem.at[h]).wait()


def finish(count, field, total, out, misfit, means, sems):
    shots = field.shape[0]
    copies = [pltpu.make_async_copy(field.at[s], out.at[s], sems.at[s]) for s in range(shots)]
    for copy in copies:
        copy.start()
    for s in range(shots):
        means[s] = jnp.sum(total[s]) / count
    copies.append(pltpu.make_async_copy(means, misfit, sems.at[shots]))
    copies[-1].start()
    for copy in copies:
        copy.wait()


def local(dims, estimate, observed, delays, thresholds):
    shots, receivers, length = estimate.shape
    n = dims[1]
    frequencies = thresholds.shape[0]
    bf16, f32 = jnp.bfloat16, jnp.float32
    bands = frequencies // n
    halves = bands // 2
    table = jnp.asarray(time_table(frequencies, length, n, halves))
    cn = jnp.asarray(shot_table(n * shots, shots))
    sem = pltpu.SemaphoreType.DMA
    vmem = pl.BlockSpec(memory_space=pltpu.VMEM)
    operands = (estimate, observed, delays, thresholds, table, cn)
    field, total = pl.pallas_call(
        functools.partial(kernel, dims),
        out_shape=(
            jax.ShapeDtypeStruct((shots, receivers, length), f32),
            jax.ShapeDtypeStruct((shots, 8, 128), f32),
        ),
        in_specs=[pl.BlockSpec(memory_space=pltpu.HBM)] * 6,
        out_specs=(vmem, vmem),
        scratch_shapes=[
            pltpu.VMEM(estimate.shape, bf16),
            pltpu.VMEM(estimate.shape, bf16),
            pltpu.SMEM(delays.shape, jnp.int32),
            pltpu.SMEM(thresholds.shape, f32),
            pltpu.VMEM(table.shape, bf16),
            pltpu.VMEM(cn.shape, bf16),
            pltpu.VMEM((2, receivers, length), bf16),
            pltpu.VMEM((2, receivers, length), bf16),
            pltpu.VMEM((2, receivers, LONGEST), bf16),
            pltpu.VMEM(estimate.shape, f32),
            pltpu.VMEM(estimate.shape, f32),
            pltpu.VMEM((shots * receivers, length), bf16),
            pltpu.VMEM((shots, 8, 128), f32),
            pltpu.VMEM((dims[0], shots, 8, 128), f32),
            pltpu.VMEM((halves, n, 8, receivers), bf16),
            pltpu.VMEM((halves, n, 8, receivers), bf16),
            pltpu.VMEM((halves, n * 8, receivers), f32),
            pltpu.VMEM((halves, n * 8, receivers), f32),
            pltpu.VMEM((halves, n, 8, receivers), bf16),
            pltpu.VMEM((halves, n, 8, receivers), bf16),
            sem((4,)),
            sem((2, BLOCKS)),
            sem((2, BLOCKS)),
            sem((2, BLOCKS)),
            sem((2,)),
            sem((2,)),
            pltpu.SemaphoreType.REGULAR,
            sem((halves,)),
            sem((halves,)),
            sem((halves,)),
            sem((halves,)),
            sem((dims[0],)),
            sem,
        ],
        compiler_params=pltpu.CompilerParams(
            collective_id=0, has_side_effects=True, vmem_limit_bytes=48 * 2**20
        ),
    )(*[pltpu.with_memory_space_constraint(v, pltpu.HBM) for v in operands])
    return pl.pallas_call(
        functools.partial(finish, dims[0] * receivers * length),
        out_shape=(jax.ShapeDtypeStruct(field.shape, f32), jax.ShapeDtypeStruct((shots,), f32)),
        in_specs=[vmem, vmem],
        out_specs=(pl.BlockSpec(memory_space=pltpu.HBM), pl.BlockSpec(memory_space=pltpu.HBM)),
        scratch_shapes=[pltpu.SMEM((shots,), f32), sem((shots + 1,))],
        compiler_params=pltpu.CompilerParams(vmem_limit_bytes=8 * 2**20),
    )(field, total)


def solution(mesh):
    patches, n = mesh.shape["patch"], mesh.shape["shot"]
    rings = 8
    dims = (patches, n, rings, n // rings)
    in_specs = (P("shot", "patch", None), P("shot", "patch", None), P(), P())
    out_specs = (P("shot", "patch", None), P("shot"))
    return jax.shard_map(
        functools.partial(local, dims), mesh=mesh, in_specs=in_specs, out_specs=out_specs, check_vma=False
    )
```

```python
import functools
import math

import jax
import jax.numpy as jnp
import ml_dtypes
import numpy as np
from jax import lax
from jax.experimental import pallas as pl
from jax.experimental.pallas import tpu as pltpu
from jax.sharding import PartitionSpec as P

SOURCE_SPACING = 512
LONGEST = 768
ROWS = 16
BLOCKS = 4
MESH = pl.DeviceIdType.MESH


def time_table(frequencies, samples, n, halves):
    phase = np.arange(frequencies)[:, None] * np.arange(samples)[None, :] % samples
    angle = 2.0 * math.pi * phase / samples
    table = np.stack([np.cos(angle), -np.sin(angle)], axis=1) / math.sqrt(samples)
    table = table.reshape(n, halves, -1, samples).swapaxes(0, 1)
    return table.reshape(2 * frequencies, samples).astype(np.float32).astype(ml_dtypes.bfloat16)


def shot_table(shots, here):
    index = np.arange(shots).reshape(shots // here, here).T.reshape(-1)
    angle = 2.0 * math.pi * (index[:, None] * index[None, :] % shots) / shots
    table = np.concatenate([np.cos(angle), np.sin(angle)]) / math.sqrt(shots)
    return table.astype(np.float32).astype(ml_dtypes.bfloat16)


def shift_left(x, lane, offset):
    length = x.shape[1]
    return jnp.where(lane < length - offset, pltpu.roll(x, (2 * length - offset) % length, 1), 0.0)


def shift_right(x, lane, offset):
    return jnp.where(lane >= offset, pltpu.roll(x, offset % x.shape[1], 1), 0.0)


def kernel(
    dims,
    est_hbm, obs_hbm, delay_hbm, level_hbm, table_hbm, cn_hbm,
    out, total,
    est, obs, delay, level, table, cn,
    halo_out, halo_in, est_in, partial, base, stepped, energy, energies,
    send1, recv1, wide1, wide2, send2, recv2,
    load_sem, record_sem, halo_send, halo_recv, est_send, est_recv, plane_sem,
    send1_sem, recv1_sem, send2_sem, recv2_sem, energy_send, energy_recv,
):
    patches, n, rings, ring = dims
    shots, receivers, length = est.shape
    rest = length - LONGEST
    halves = wide1.shape[0]
    bands = 2 * halves
    me, x = lax.axis_index("shot"), lax.axis_index("patch")
    z, place = me // ring, me % ring
    right, left = (me + 1) % n, (me + n - 1) % n
    last = n * shots - 1

    loads = [
        pltpu.make_async_copy(src, dst, load_sem.at[i])
        for i, (src, dst) in enumerate([(delay_hbm, delay), (level_hbm, level), (table_hbm, table), (cn_hbm, cn)])
    ]

    def record_loads(block):
        rows = pl.ds(block * (receivers // BLOCKS), receivers // BLOCKS)
        return [
            pltpu.make_async_copy(src.at[:, rows], dst.at[:, rows], record_sem.at[i, block])
            for i, (src, dst) in enumerate([(est_hbm, est), (obs_hbm, obs)])
        ]

    loads[0].start()
    for block in range(BLOCKS):
        for load in record_loads(block):
            load.start()
    for load in loads[1:]:
        load.start()

    barrier = pltpu.get_barrier_semaphore()

    def greet_ring(i, carry):
        pl.semaphore_signal(barrier, 1, device_id={"shot": z * ring + (place + i) % ring}, device_id_type=MESH)
        return carry

    def greet_planes(i, carry):
        pl.semaphore_signal(barrier, 1, device_id={"shot": (z + i) % rings * ring + place}, device_id_type=MESH)
        return carry

    def greet_patches(i, carry):
        pl.semaphore_signal(barrier, 1, device_id={"patch": (x + i) % patches}, device_id_type=MESH)
        return carry

    pl.semaphore_signal(barrier, 1, device_id={"shot": right}, device_id_type=MESH)
    pl.semaphore_signal(barrier, 1, device_id={"shot": left}, device_id_type=MESH)
    lax.fori_loop(1, ring, greet_ring, 0)
    lax.fori_loop(1, rings, greet_planes, 0)
    lax.fori_loop(1, patches, greet_patches, 0)

    loads[0].wait()
    first = me * shots
    delays = [delay[jnp.clip(first + i, 0, last)] for i in range(-2, 4)]
    a_prev, a_before, a_here, a_after, a_next = [SOURCE_SPACING + b - a for a, b in zip(delays, delays[1:])]
    has_left = me > 0
    has_right = me < n - 1
    lane = lax.broadcasted_iota(jnp.int32, (ROWS, length), 1)
    lane_rest = lax.broadcasted_iota(jnp.int32, (ROWS, rest), 1)

    def before_halo(i, carry):
        rows = pl.ds(i * ROWS, ROWS)
        e0 = est[0, rows, :].astype(jnp.float32)
        e1 = est[1, rows, :].astype(jnp.float32)
        p0 = obs[0, rows, :].astype(jnp.float32) - e0 - shift_right(e1, lane, a_here)
        p1 = obs[1, rows, :].astype(jnp.float32) - e1 - shift_left(e0, lane, a_here)
        partial[0, rows, :] = p0
        partial[1, rows, :] = p1
        once = shift_left(p1 - e1, lane, a_after)[:, :LONGEST]
        twice = shift_left(e1[:, LONGEST:], lane_rest, a_after + a_next - LONGEST)
        halo_out[0, rows, :] = jnp.concatenate([once, twice], axis=1).astype(jnp.bfloat16)
        once = shift_right(p0 - e0, lane, a_before)[:, rest:]
        twice = shift_right(e0[:, :rest], lane_rest, a_before + a_prev - LONGEST)
        halo_out[1, rows, :] = jnp.concatenate([once, twice], axis=1).astype(jnp.bfloat16)
        return carry

    def halo_copies(block):
        rows = pl.ds(block * (receivers // BLOCKS), receivers // BLOCKS)
        return [
            pltpu.make_async_remote_copy(
                halo_out.at[side, rows], halo_in.at[side, rows], halo_send.at[side, block], halo_recv.at[side, block],
                device_id={"shot": peer}, device_id_type=MESH,
            )
            for side, peer in enumerate([right, left])
        ]

    steps = receivers // ROWS // BLOCKS
    for block in range(BLOCKS):
        for load in record_loads(block):
            load.wait()
        lax.fori_loop(block * steps, (block + 1) * steps, before_halo, 0)
        if block == 0:
            pl.semaphore_wait(barrier, ring - 1 + rings - 1 + patches - 1 + 2)
        for halo in halo_copies(block):
            halo.start()

    raw_halos = [
        pltpu.make_async_remote_copy(
            est.at[1 - side, :, pl.ds(rest * (1 - side), LONGEST)], est_in.at[side], est_send.at[side], est_recv.at[side],
            device_id={"shot": peer}, device_id_type=MESH,
        )
        for side, peer in enumerate([right, left])
    ]
    for halo in raw_halos:
        halo.start()

    def plane_ready(i, carry):
        pl.semaphore_signal(plane_sem, 1, device_id={"shot": (z + i) % rings * ring + place}, device_id_type=MESH)
        return carry

    lax.fori_loop(1, rings, plane_ready, 0)

    def own_part(i, carry):
        rows = pl.ds(i * ROWS, ROWS)
        e0 = est[0, rows, :].astype(jnp.float32)
        e1 = est[1, rows, :].astype(jnp.float32)
        p0 = partial[0, rows, :]
        p1 = partial[1, rows, :]
        own0 = jnp.where(lane < jnp.where(has_left, length - a_before, 0), e0, 0.0)
        own1 = jnp.where(lane >= jnp.where(has_right, a_after, length), e1, 0.0)
        base[0, rows, :] = e0 + 0.5 * (p0 + shift_right(p1, lane, a_here) - own0)
        base[1, rows, :] = e1 + 0.5 * (p1 + shift_left(p0, lane, a_here) - own1)
        return carry

    lax.fori_loop(0, receivers // ROWS, own_part, 0)
    for load in loads[1:]:
        load.wait()

    def after_halo(i, carry):
        rows = pl.ds(i * ROWS, ROWS)
        from_left = jnp.where(has_left, halo_in[0, rows, :].astype(jnp.float32), 0.0)
        from_right = jnp.where(has_right, halo_in[1, rows, :].astype(jnp.float32), 0.0)
        h0 = jnp.concatenate([from_left[:, :LONGEST], -from_right[:, LONGEST:]], axis=1)
        h1 = jnp.concatenate([-from_left[:, LONGEST:], from_right[:, :LONGEST]], axis=1)
        stepped[rows, :] = (base[0, rows, :] + 0.5 * h0).astype(jnp.bfloat16)
        stepped[pl.ds(receivers + i * ROWS, ROWS), :] = (base[1, rows, :] + 0.5 * h1).astype(jnp.bfloat16)
        return carry

    for block in range(BLOCKS):
        for halo in halo_copies(block):
            halo.wait_recv()
        lax.fori_loop(block * steps, (block + 1) * steps, after_halo, 0)

    pl.semaphore_wait(plane_sem, rings - 1)

    half = rings // 2
    place_y, core = place // 2, place % 2
    at_z = [lax.rem(z + dz, rings) * ring for dz in range(rings)]
    at_y = [lax.rem(place_y + dy, rings) * 2 for dy in range(rings)]
    at_core = [core, 1 - core]
    peers = [
        at_z[dz] + at_y[dy] + at_core[dc]
        for hops in range(2 * half, -1, -1)
        for far_z in range(half + 1)
        for far_y in range(half + 1)
        if far_z + far_y == hops
        for dz in sorted({far_z, (rings - far_z) % rings})
        for dy in sorted({far_y, (rings - far_y) % rings})
        for dc in range(2)
        if dz or dy or dc
    ]

    def exchange(src, dst, ssem, rsem):
        for peer in peers:
            pltpu.make_async_remote_copy(
                src.at[peer], dst.at[me], ssem, rsem, device_id={"shot": peer}, device_id_type=MESH
            ).start()
        pltpu.make_async_copy(src.at[me], dst.at[me], rsem).start()

    upper = lax.broadcasted_iota(jnp.int32, (n // 2, 8, receivers), 1) < 4

    def to_frequencies(h, carry):
        rows = table[pl.ds(pl.multiple_of(h * 4 * n, 4 * n), 4 * n), :]
        got = lax.dot_general(rows, stepped[...], (((1,), (1,)), ((), ())), preferred_element_type=jnp.float32)
        pairs = got.reshape(n // 2, 8, shots * receivers)
        g0, g1 = pairs[:, :, :receivers], pairs[:, :, receivers:]
        even = jnp.where(upper, g0, pltpu.roll(g1, 4, 1))
        odd = jnp.where(upper, pltpu.roll(g0, 4, 1), g1)
        send1[h] = jnp.stack([even, odd], axis=1).reshape(n, 8, receivers).astype(jnp.bfloat16)
        exchange(send1.at[h], recv1.at[h], send1_sem.at[h], recv1_sem.at[h])
        return carry

    lax.fori_loop(0, halves, to_frequencies, 0)

    for halo in raw_halos:
        halo.wait_recv()

    def misfit_part(i, carry):
        rows = pl.ds(i * ROWS, ROWS)
        blank = jnp.zeros((ROWS, rest), jnp.float32)
        from_left = jnp.concatenate([blank, est_in[0, rows, :].astype(jnp.float32)], axis=1)
        from_right = jnp.concatenate([est_in[1, rows, :].astype(jnp.float32), blank], axis=1)
        r0 = partial[0, rows, :] - jnp.where(has_left, shift_left(from_left, lane, a_before), 0.0)
        r1 = partial[1, rows, :] - jnp.where(has_right, shift_right(from_right, lane, a_after), 0.0)

        def squares(r):
            parts = jnp.zeros((8, 128), jnp.float32)
            for a in range(0, ROWS, 8):
                for b in range(0, length, 128):
                    piece = r[a : a + 8, b : b + 128]
                    parts = parts + piece * piece
            return parts

        return carry[0] + squares(r0), carry[1] + squares(r1)

    zero = jnp.zeros((8, 128), jnp.float32)
    e_0, e_1 = lax.fori_loop(0, receivers // ROWS, misfit_part, (zero, zero))
    energy[0] = e_0
    energy[1] = e_1
    for i in range(1, patches):
        pltpu.make_async_remote_copy(
            energy, energies.at[x], energy_send.at[i], energy_recv,
            device_id={"patch": (x + i) % patches}, device_id_type=MESH,
        ).start()
    pltpu.make_async_copy(energy, energies.at[x], energy_recv).start()

    wave = cn[...]
    k = n * shots

    def to_shots(h, carry):
        pltpu.make_async_copy(recv1.at[h], recv1.at[h], recv1_sem.at[h]).wait()
        w1, w2 = wide1.at[h], wide2.at[h]
        w1[...] = recv1[h].astype(jnp.float32).reshape(8 * n, receivers)
        for b in range(bands // halves):
            columns = []
            for q in range(2):
                parts = [w1[pl.ds(s * 4 + b * 2 + q, n, stride=8), :] for s in range(shots)]
                columns.append(jnp.concatenate(parts, axis=0))
            field = jnp.concatenate(columns, axis=1).astype(jnp.bfloat16)
            got = jnp.dot(wave, field, preferred_element_type=jnp.float32)
            real = got[:k, :receivers] + got[k:, receivers:]
            imag = got[:k, receivers:] - got[k:, :receivers]
            f = me * bands + h * (bands // halves) + b
            limit = level[f]
            weight = jnp.where(f == 0, 1.0, 2.0)
            magnitude = jnp.sqrt(real * real + imag * imag)
            factor = jnp.maximum(magnitude - limit, 0.0) / jnp.maximum(magnitude, limit) * weight
            shrunk = jnp.concatenate([real * factor, imag * factor], axis=1).astype(jnp.bfloat16)
            got = jnp.dot(wave, shrunk, preferred_element_type=jnp.float32)
            real = got[:k, :receivers] - got[k:, receivers:]
            imag = got[:k, receivers:] + got[k:, :receivers]
            for s in range(shots):
                w2[pl.ds(s * 4 + b * 2, n, stride=8), :] = real[s * n : (s + 1) * n]
                w2[pl.ds(s * 4 + b * 2 + 1, n, stride=8), :] = imag[s * n : (s + 1) * n]
        send2[h] = w2[...].reshape(n, 8, receivers).astype(jnp.bfloat16)
        exchange(send2.at[h], recv2.at[h], send2_sem.at[h], recv2_sem.at[h])
        return carry

    lax.fori_loop(0, halves, to_shots, 0)

    pltpu.make_async_copy(energies, energies, energy_recv).wait()
    total[...] = sum(energies[i] for i in range(patches))

    for block in range(BLOCKS):
        for halo in halo_copies(block):
            halo.wait_send()
    for halo in raw_halos:
        halo.wait_send()
    for i in range(1, patches):
        pltpu.make_async_remote_copy(
            energy, energies.at[x], energy_send.at[i], energy_recv,
            device_id={"patch": (x + i) % patches}, device_id_type=MESH,
        ).wait_send()
    others = pl.ds(0, n - 1)
    for h in range(halves):
        pltpu.make_async_copy(send1.at[h, others], send1.at[h, others], send1_sem.at[h]).wait()

    for h in range(halves):
        pltpu.make_async_copy(recv2.at[h], recv2.at[h], recv2_sem.at[h]).wait()
        pairs = recv2[h].astype(jnp.float32).reshape(n // 2, 2, 8, receivers)
        even, odd = pairs[:, 0], pairs[:, 1]
        fields = [
            jnp.where(upper, even, pltpu.roll(odd, 4, 1)),
            jnp.where(upper, pltpu.roll(even, 4, 1), odd),
        ]
        rows = table[h * 4 * n : (h + 1) * 4 * n, :]
        for s in range(shots):
            field = fields[s].reshape(4 * n, receivers).astype(jnp.bfloat16)
            got = lax.dot_general(field, rows, (((0,), (0,)), ((), ())), preferred_element_type=jnp.float32)
            out[s] = got if h == 0 else out[s] + got

    for h in range(halves):
        pltpu.make_async_copy(send2.at[h, others], send2.at[h, others], send2_sem.at[h]).wait()


def finish(count, field, total, out, misfit, means, sems):
    shots = field.shape[0]
    copies = [pltpu.make_async_copy(field.at[s], out.at[s], sems.at[s]) for s in range(shots)]
    for copy in copies:
        copy.start()
    for s in range(shots):
        means[s] = jnp.sum(total[s]) / count
    copies.append(pltpu.make_async_copy(means, misfit, sems.at[shots]))
    copies[-1].start()
    for copy in copies:
        copy.wait()


def local(dims, estimate, observed, delays, thresholds):
    shots, receivers, length = estimate.shape
    n = dims[1]
    frequencies = thresholds.shape[0]
    bf16, f32 = jnp.bfloat16, jnp.float32
    bands = frequencies // n
    halves = bands // 2
    table = jnp.asarray(time_table(frequencies, length, n, halves))
    cn = jnp.asarray(shot_table(n * shots, shots))
    sem = pltpu.SemaphoreType.DMA
    vmem = pl.BlockSpec(memory_space=pltpu.VMEM)
    operands = (estimate, observed, delays, thresholds, table, cn)
    field, total = pl.pallas_call(
        functools.partial(kernel, dims),
        out_shape=(
            jax.ShapeDtypeStruct((shots, receivers, length), f32),
            jax.ShapeDtypeStruct((shots, 8, 128), f32),
        ),
        in_specs=[pl.BlockSpec(memory_space=pltpu.HBM)] * 6,
        out_specs=(vmem, vmem),
        scratch_shapes=[
            pltpu.VMEM(estimate.shape, bf16),
            pltpu.VMEM(estimate.shape, bf16),
            pltpu.SMEM(delays.shape, jnp.int32),
            pltpu.SMEM(thresholds.shape, f32),
            pltpu.VMEM(table.shape, bf16),
            pltpu.VMEM(cn.shape, bf16),
            pltpu.VMEM((2, receivers, length), bf16),
            pltpu.VMEM((2, receivers, length), bf16),
            pltpu.VMEM((2, receivers, LONGEST), bf16),
            pltpu.VMEM(estimate.shape, f32),
            pltpu.VMEM(estimate.shape, f32),
            pltpu.VMEM((shots * receivers, length), bf16),
            pltpu.VMEM((shots, 8, 128), f32),
            pltpu.VMEM((dims[0], shots, 8, 128), f32),
            pltpu.VMEM((halves, n, 8, receivers), bf16),
            pltpu.VMEM((halves, n, 8, receivers), bf16),
            pltpu.VMEM((halves, n * 8, receivers), f32),
            pltpu.VMEM((halves, n * 8, receivers), f32),
            pltpu.VMEM((halves, n, 8, receivers), bf16),
            pltpu.VMEM((halves, n, 8, receivers), bf16),
            sem((4,)),
            sem((2, BLOCKS)),
            sem((2, BLOCKS)),
            sem((2, BLOCKS)),
            sem((2,)),
            sem((2,)),
            pltpu.SemaphoreType.REGULAR,
            sem((halves,)),
            sem((halves,)),
            sem((halves,)),
            sem((halves,)),
            sem((dims[0],)),
            sem,
        ],
        compiler_params=pltpu.CompilerParams(
            collective_id=0, has_side_effects=True, vmem_limit_bytes=48 * 2**20
        ),
    )(*[pltpu.with_memory_space_constraint(v, pltpu.HBM) for v in operands])
    return pl.pallas_call(
        functools.partial(finish, dims[0] * receivers * length),
        out_shape=(jax.ShapeDtypeStruct(field.shape, f32), jax.ShapeDtypeStruct((shots,), f32)),
        in_specs=[vmem, vmem],
        out_specs=(pl.BlockSpec(memory_space=pltpu.HBM), pl.BlockSpec(memory_space=pltpu.HBM)),
        scratch_shapes=[pltpu.SMEM((shots,), f32), sem((shots + 1,))],
        compiler_params=pltpu.CompilerParams(vmem_limit_bytes=8 * 2**20),
    )(field, total)


def solution(mesh):
    patches, n = mesh.shape["patch"], mesh.shape["shot"]
    rings = 8
    dims = (patches, n, rings, n // rings)
    in_specs = (P("shot", "patch", None), P("shot", "patch", None), P(), P())
    out_specs = (P("shot", "patch", None), P("shot"))
    return jax.shard_map(
        functools.partial(local, dims), mesh=mesh, in_specs=in_specs, out_specs=out_specs, check_vma=False
    )
```

```python
import functools
import math

import jax
import jax.numpy as jnp
import ml_dtypes
import numpy as np
from jax import lax
from jax.experimental import pallas as pl
from jax.experimental.pallas import tpu as pltpu
from jax.sharding import PartitionSpec as P

SOURCE_SPACING = 512
LONGEST = 768
ROWS = 16
BLOCKS = 4
MESH = pl.DeviceIdType.MESH


def time_table(frequencies, samples):
    phase = np.arange(frequencies)[:, None] * np.arange(samples)[None, :] % samples
    angle = 2.0 * math.pi * phase / samples
    table = np.stack([np.cos(angle), -np.sin(angle)], axis=1) / math.sqrt(samples)
    return table.reshape(2 * frequencies, samples).astype(np.float32).astype(ml_dtypes.bfloat16)


def shot_table(shots, here):
    index = np.arange(shots).reshape(shots // here, here).T.reshape(-1)
    angle = 2.0 * math.pi * (index[:, None] * index[None, :] % shots) / shots
    table = np.concatenate([np.cos(angle), np.sin(angle)]) / math.sqrt(shots)
    return table.astype(np.float32).astype(ml_dtypes.bfloat16)


def shift_left(x, lane, offset):
    length = x.shape[1]
    return jnp.where(lane < length - offset, pltpu.roll(x, (2 * length - offset) % length, 1), 0.0)


def shift_right(x, lane, offset):
    return jnp.where(lane >= offset, pltpu.roll(x, offset % x.shape[1], 1), 0.0)


def kernel(
    dims,
    est_hbm, obs_hbm, delay_hbm, level_hbm, table_hbm, cn_hbm,
    out, total,
    est, obs, delay, level, table, cn,
    halo_out, halo_in, est_in, partial, base, stepped, energy, energies,
    send1, recv1, wide1, wide2, send2, recv2,
    load_sem, record_sem, halo_send, halo_recv, est_send, est_recv, plane_sem,
    send1_sem, recv1_sem, send2_sem, recv2_sem, energy_send, energy_recv,
):
    patches, n, rings, ring = dims
    shots, receivers, length = est.shape
    rest = length - LONGEST
    halves = stepped.shape[0]
    part = receivers // halves
    bands = table.shape[0] // 2 // n
    me, x = lax.axis_index("shot"), lax.axis_index("patch")
    z, place = me // ring, me % ring
    right, left = (me + 1) % n, (me + n - 1) % n
    last = n * shots - 1

    loads = [
        pltpu.make_async_copy(src, dst, load_sem.at[i])
        for i, (src, dst) in enumerate([(delay_hbm, delay), (level_hbm, level), (table_hbm, table), (cn_hbm, cn)])
    ]

    def record_loads(block):
        rows = pl.ds(block * (receivers // BLOCKS), receivers // BLOCKS)
        return [
            pltpu.make_async_copy(src.at[:, rows], dst.at[:, rows], record_sem.at[i, block])
            for i, (src, dst) in enumerate([(est_hbm, est), (obs_hbm, obs)])
        ]

    loads[0].start()
    for block in range(BLOCKS):
        for load in record_loads(block):
            load.start()
    for load in loads[1:]:
        load.start()

    barrier = pltpu.get_barrier_semaphore()

    def greet_ring(i, carry):
        pl.semaphore_signal(barrier, 1, device_id={"shot": z * ring + (place + i) % ring}, device_id_type=MESH)
        return carry

    def greet_planes(i, carry):
        pl.semaphore_signal(barrier, 1, device_id={"shot": (z + i) % rings * ring + place}, device_id_type=MESH)
        return carry

    def greet_patches(i, carry):
        pl.semaphore_signal(barrier, 1, device_id={"patch": (x + i) % patches}, device_id_type=MESH)
        return carry

    pl.semaphore_signal(barrier, 1, device_id={"shot": right}, device_id_type=MESH)
    pl.semaphore_signal(barrier, 1, device_id={"shot": left}, device_id_type=MESH)
    lax.fori_loop(1, ring, greet_ring, 0)
    lax.fori_loop(1, rings, greet_planes, 0)
    lax.fori_loop(1, patches, greet_patches, 0)

    loads[0].wait()
    first = me * shots
    delays = [delay[jnp.clip(first + i, 0, last)] for i in range(-2, 4)]
    a_prev, a_before, a_here, a_after, a_next = [SOURCE_SPACING + b - a for a, b in zip(delays, delays[1:])]
    has_left = me > 0
    has_right = me < n - 1
    lane = lax.broadcasted_iota(jnp.int32, (ROWS, length), 1)
    lane_rest = lax.broadcasted_iota(jnp.int32, (ROWS, rest), 1)

    def before_halo(i, carry):
        rows = pl.ds(i * ROWS, ROWS)
        e0 = est[0, rows, :].astype(jnp.float32)
        e1 = est[1, rows, :].astype(jnp.float32)
        p0 = obs[0, rows, :].astype(jnp.float32) - e0 - shift_right(e1, lane, a_here)
        p1 = obs[1, rows, :].astype(jnp.float32) - e1 - shift_left(e0, lane, a_here)
        partial[0, rows, :] = p0
        partial[1, rows, :] = p1
        once = shift_left(p1 - e1, lane, a_after)[:, :LONGEST]
        twice = shift_left(e1[:, LONGEST:], lane_rest, a_after + a_next - LONGEST)
        halo_out[0, rows, :] = jnp.concatenate([once, twice], axis=1).astype(jnp.bfloat16)
        once = shift_right(p0 - e0, lane, a_before)[:, rest:]
        twice = shift_right(e0[:, :rest], lane_rest, a_before + a_prev - LONGEST)
        halo_out[1, rows, :] = jnp.concatenate([once, twice], axis=1).astype(jnp.bfloat16)
        return carry

    def halo_copies(block):
        rows = pl.ds(block * (receivers // BLOCKS), receivers // BLOCKS)
        return [
            pltpu.make_async_remote_copy(
                halo_out.at[side, rows], halo_in.at[side, rows], halo_send.at[side, block], halo_recv.at[side, block],
                device_id={"shot": peer}, device_id_type=MESH,
            )
            for side, peer in enumerate([right, left])
        ]

    steps = receivers // ROWS // BLOCKS
    for block in range(BLOCKS):
        for load in record_loads(block):
            load.wait()
        lax.fori_loop(block * steps, (block + 1) * steps, before_halo, 0)
        if block == 0:
            pl.semaphore_wait(barrier, ring - 1 + rings - 1 + patches - 1 + 2)
        for halo in halo_copies(block):
            halo.start()

    raw_halos = [
        pltpu.make_async_remote_copy(
            est.at[1 - side, :, pl.ds(rest * (1 - side), LONGEST)], est_in.at[side], est_send.at[side], est_recv.at[side],
            device_id={"shot": peer}, device_id_type=MESH,
        )
        for side, peer in enumerate([right, left])
    ]
    for halo in raw_halos:
        halo.start()

    def plane_ready(i, carry):
        pl.semaphore_signal(plane_sem, 1, device_id={"shot": (z + i) % rings * ring + place}, device_id_type=MESH)
        return carry

    lax.fori_loop(1, rings, plane_ready, 0)

    def own_part(i, carry):
        rows = pl.ds(i * ROWS, ROWS)
        e0 = est[0, rows, :].astype(jnp.float32)
        e1 = est[1, rows, :].astype(jnp.float32)
        p0 = partial[0, rows, :]
        p1 = partial[1, rows, :]
        own0 = jnp.where(lane < jnp.where(has_left, length - a_before, 0), e0, 0.0)
        own1 = jnp.where(lane >= jnp.where(has_right, a_after, length), e1, 0.0)
        base[0, rows, :] = e0 + 0.5 * (p0 + shift_right(p1, lane, a_here) - own0)
        base[1, rows, :] = e1 + 0.5 * (p1 + shift_left(p0, lane, a_here) - own1)
        return carry

    lax.fori_loop(0, receivers // ROWS, own_part, 0)
    for load in loads[1:]:
        load.wait()

    def after_halo(i, carry):
        rows = pl.ds(i * ROWS, ROWS)
        from_left = jnp.where(has_left, halo_in[0, rows, :].astype(jnp.float32), 0.0)
        from_right = jnp.where(has_right, halo_in[1, rows, :].astype(jnp.float32), 0.0)
        h0 = jnp.concatenate([from_left[:, :LONGEST], -from_right[:, LONGEST:]], axis=1)
        h1 = jnp.concatenate([-from_left[:, LONGEST:], from_right[:, :LONGEST]], axis=1)
        h, r = i // (part // ROWS), lax.rem(i, part // ROWS) * ROWS
        stepped[h, pl.ds(r, ROWS), :] = (base[0, rows, :] + 0.5 * h0).astype(jnp.bfloat16)
        stepped[h, pl.ds(part + r, ROWS), :] = (base[1, rows, :] + 0.5 * h1).astype(jnp.bfloat16)
        return carry


    pl.semaphore_wait(plane_sem, rings - 1)

    half = rings // 2
    place_y, core = place // 2, place % 2
    at_z = [lax.rem(z + dz, rings) * ring for dz in range(rings)]
    at_y = [lax.rem(place_y + dy, rings) * 2 for dy in range(rings)]
    at_core = [core, 1 - core]
    peers = [
        at_z[dz] + at_y[dy] + at_core[dc]
        for hops in range(2 * half, -1, -1)
        for far_z in range(half + 1)
        for far_y in range(half + 1)
        if far_z + far_y == hops
        for dz in sorted({far_z, (rings - far_z) % rings})
        for dy in sorted({far_y, (rings - far_y) % rings})
        for dc in range(2)
        if dz or dy or dc
    ]

    def exchange(src, dst, ssem, rsem):
        for peer in peers:
            pltpu.make_async_remote_copy(
                src.at[peer], dst.at[me], ssem, rsem, device_id={"shot": peer}, device_id_type=MESH
            ).start()
        pltpu.make_async_copy(src.at[me], dst.at[me], rsem).start()

    def to_frequencies(h, carry):
        for j in range(BLOCKS // halves):
            block = h * (BLOCKS // halves) + j
            for halo in halo_copies(block):
                halo.wait_recv()
            lax.fori_loop(block * steps, (block + 1) * steps, after_halo, 0)
        got = lax.dot_general(table[...], stepped[h], (((1,), (1,)), ((), ())), preferred_element_type=jnp.float32)
        send1[h] = got.reshape(n, 8, receivers).astype(jnp.bfloat16)
        exchange(send1.at[h], recv1.at[h], send1_sem.at[h], recv1_sem.at[h])
        return carry

    lax.fori_loop(0, halves, to_frequencies, 0)

    for halo in raw_halos:
        halo.wait_recv()

    def misfit_part(i, carry):
        rows = pl.ds(i * ROWS, ROWS)
        blank = jnp.zeros((ROWS, rest), jnp.float32)
        from_left = jnp.concatenate([blank, est_in[0, rows, :].astype(jnp.float32)], axis=1)
        from_right = jnp.concatenate([est_in[1, rows, :].astype(jnp.float32), blank], axis=1)
        r0 = partial[0, rows, :] - jnp.where(has_left, shift_left(from_left, lane, a_before), 0.0)
        r1 = partial[1, rows, :] - jnp.where(has_right, shift_right(from_right, lane, a_after), 0.0)

        def squares(r):
            parts = jnp.zeros((8, 128), jnp.float32)
            for a in range(0, ROWS, 8):
                for b in range(0, length, 128):
                    piece = r[a : a + 8, b : b + 128]
                    parts = parts + piece * piece
            return parts

        return carry[0] + squares(r0), carry[1] + squares(r1)

    zero = jnp.zeros((8, 128), jnp.float32)
    e_0, e_1 = lax.fori_loop(0, receivers // ROWS, misfit_part, (zero, zero))
    energy[0] = e_0
    energy[1] = e_1
    for i in range(1, patches):
        pltpu.make_async_remote_copy(
            energy, energies.at[x], energy_send.at[i], energy_recv,
            device_id={"patch": (x + i) % patches}, device_id_type=MESH,
        ).start()
    pltpu.make_async_copy(energy, energies.at[x], energy_recv).start()

    wave = cn[...]
    k = n * shots

    low = lax.broadcasted_iota(jnp.int32, (n, receivers), 1) < part
    sign = jnp.where(lax.broadcasted_iota(jnp.int32, (k, receivers), 1) < part, 1.0, -1.0)

    def swapped(v):
        return pltpu.roll(v, part, 1)

    def exchanged(v0, v1):
        return jnp.where(low, v0, swapped(v1)), jnp.where(low, swapped(v0), v1)

    def to_shots(h, carry):
        pltpu.make_async_copy(recv1.at[h], recv1.at[h], recv1_sem.at[h]).wait()
        w1, w2 = wide1.at[h], wide2.at[h]
        w1[...] = recv1[h].astype(jnp.float32).reshape(8 * n, receivers)
        for pair in range(0, bands, 2):
            columns = []
            for b in (pair, pair + 1):
                cut = [w1[pl.ds(b * 2 + q, n, stride=8), :] for q in range(2)]
                columns.append(jnp.concatenate(exchanged(*cut), axis=0))
            field = jnp.concatenate(columns, axis=1).astype(jnp.bfloat16)
            got = jnp.dot(wave, field, preferred_element_type=jnp.float32)
            columns = []
            for i, b in enumerate((pair, pair + 1)):
                lanes = slice(i * receivers, (i + 1) * receivers)
                v = got[:k, lanes] + sign * swapped(got[k:, lanes])
                f = me * bands + b
                limit = level[f]
                weight = jnp.where(f == 0, 1.0, 2.0)
                squares = v * v
                magnitude = jnp.sqrt(squares + swapped(squares))
                factor = jnp.maximum(magnitude - limit, 0.0) / jnp.maximum(magnitude, limit) * weight
                columns.append(v * factor)
            shrunk = jnp.concatenate(columns, axis=1).astype(jnp.bfloat16)
            got = jnp.dot(wave, shrunk, preferred_element_type=jnp.float32)
            for i, b in enumerate((pair, pair + 1)):
                lanes = slice(i * receivers, (i + 1) * receivers)
                v = got[:k, lanes] - sign * swapped(got[k:, lanes])
                for p, cut in enumerate(exchanged(v[:n], v[n:])):
                    w2[pl.ds(b * 2 + p, n, stride=8), :] = cut
        send2[h] = w2[...].reshape(n, 8, receivers).astype(jnp.bfloat16)
        exchange(send2.at[h], recv2.at[h], send2_sem.at[h], recv2_sem.at[h])
        return carry

    lax.fori_loop(0, halves, to_shots, 0)

    pltpu.make_async_copy(energies, energies, energy_recv).wait()
    total[...] = sum(energies[i] for i in range(patches))

    for block in range(BLOCKS):
        for halo in halo_copies(block):
            halo.wait_send()
    for halo in raw_halos:
        halo.wait_send()
    for i in range(1, patches):
        pltpu.make_async_remote_copy(
            energy, energies.at[x], energy_send.at[i], energy_recv,
            device_id={"patch": (x + i) % patches}, device_id_type=MESH,
        ).wait_send()
    others = pl.ds(0, n - 1)
    for h in range(halves):
        pltpu.make_async_copy(send1.at[h, others], send1.at[h, others], send1_sem.at[h]).wait()

    def to_samples(h, carry):
        pltpu.make_async_copy(recv2.at[h], recv2.at[h], recv2_sem.at[h]).wait()
        field = recv2[h].astype(jnp.float32).reshape(8 * n, receivers).astype(jnp.bfloat16)
        got = lax.dot_general(field, table[...], (((0,), (0,)), ((), ())), preferred_element_type=jnp.float32)
        for s in range(shots):
            out[s, pl.ds(pl.multiple_of(h * part, part), part), :] = got[s * part : (s + 1) * part]
        return carry

    lax.fori_loop(0, halves, to_samples, 0)

    for h in range(halves):
        pltpu.make_async_copy(send2.at[h, others], send2.at[h, others], send2_sem.at[h]).wait()


def finish(count, field, total, out, misfit, means, sems):
    shots = field.shape[0]
    copies = [pltpu.make_async_copy(field.at[s], out.at[s], sems.at[s]) for s in range(shots)]
    for copy in copies:
        copy.start()
    for s in range(shots):
        means[s] = jnp.sum(total[s]) / count
    copies.append(pltpu.make_async_copy(means, misfit, sems.at[shots]))
    copies[-1].start()
    for copy in copies:
        copy.wait()


def local(dims, estimate, observed, delays, thresholds):
    shots, receivers, length = estimate.shape
    n = dims[1]
    frequencies = thresholds.shape[0]
    bf16, f32 = jnp.bfloat16, jnp.float32
    halves = 2
    table = jnp.asarray(time_table(frequencies, length))
    cn = jnp.asarray(shot_table(n * shots, shots))
    sem = pltpu.SemaphoreType.DMA
    vmem = pl.BlockSpec(memory_space=pltpu.VMEM)
    operands = (estimate, observed, delays, thresholds, table, cn)
    field, total = pl.pallas_call(
        functools.partial(kernel, dims),
        out_shape=(
            jax.ShapeDtypeStruct((shots, receivers, length), f32),
            jax.ShapeDtypeStruct((shots, 8, 128), f32),
        ),
        in_specs=[pl.BlockSpec(memory_space=pltpu.HBM)] * 6,
        out_specs=(vmem, vmem),
        scratch_shapes=[
            pltpu.VMEM(estimate.shape, bf16),
            pltpu.VMEM(estimate.shape, bf16),
            pltpu.SMEM(delays.shape, jnp.int32),
            pltpu.SMEM(thresholds.shape, f32),
            pltpu.VMEM(table.shape, bf16),
            pltpu.VMEM(cn.shape, bf16),
            pltpu.VMEM((2, receivers, length), bf16),
            pltpu.VMEM((2, receivers, length), bf16),
            pltpu.VMEM((2, receivers, LONGEST), bf16),
            pltpu.VMEM(estimate.shape, f32),
            pltpu.VMEM(estimate.shape, f32),
            pltpu.VMEM((halves, shots * receivers // halves, length), bf16),
            pltpu.VMEM((shots, 8, 128), f32),
            pltpu.VMEM((dims[0], shots, 8, 128), f32),
            pltpu.VMEM((halves, n, 8, receivers), bf16),
            pltpu.VMEM((halves, n, 8, receivers), bf16),
            pltpu.VMEM((halves, n * 8, receivers), f32),
            pltpu.VMEM((halves, n * 8, receivers), f32),
            pltpu.VMEM((halves, n, 8, receivers), bf16),
            pltpu.VMEM((halves, n, 8, receivers), bf16),
            sem((4,)),
            sem((2, BLOCKS)),
            sem((2, BLOCKS)),
            sem((2, BLOCKS)),
            sem((2,)),
            sem((2,)),
            pltpu.SemaphoreType.REGULAR,
            sem((halves,)),
            sem((halves,)),
            sem((halves,)),
            sem((halves,)),
            sem((dims[0],)),
            sem,
        ],
        compiler_params=pltpu.CompilerParams(
            collective_id=0, has_side_effects=True, vmem_limit_bytes=48 * 2**20
        ),
    )(*[pltpu.with_memory_space_constraint(v, pltpu.HBM) for v in operands])
    return pl.pallas_call(
        functools.partial(finish, dims[0] * receivers * length),
        out_shape=(jax.ShapeDtypeStruct(field.shape, f32), jax.ShapeDtypeStruct((shots,), f32)),
        in_specs=[vmem, vmem],
        out_specs=(pl.BlockSpec(memory_space=pltpu.HBM), pl.BlockSpec(memory_space=pltpu.HBM)),
        scratch_shapes=[pltpu.SMEM((shots,), f32), sem((shots + 1,))],
        compiler_params=pltpu.CompilerParams(vmem_limit_bytes=8 * 2**20),
    )(field, total)


def solution(mesh):
    patches, n = mesh.shape["patch"], mesh.shape["shot"]
    rings = 8
    dims = (patches, n, rings, n // rings)
    in_specs = (P("shot", "patch", None), P("shot", "patch", None), P(), P())
    out_specs = (P("shot", "patch", None), P("shot"))
    return jax.shard_map(
        functools.partial(local, dims), mesh=mesh, in_specs=in_specs, out_specs=out_specs, check_vma=False
    )
```

```python
import functools
import math

import jax
import jax.numpy as jnp
import ml_dtypes
import numpy as np
from jax import lax
from jax.experimental import pallas as pl
from jax.experimental.pallas import tpu as pltpu
from jax.sharding import PartitionSpec as P

SOURCE_SPACING = 512
LONGEST = 768
ROWS = 16
BLOCKS = 4
MESH = pl.DeviceIdType.MESH


def time_table(frequencies, samples):
    phase = np.arange(frequencies)[:, None] * np.arange(samples)[None, :] % samples
    angle = 2.0 * math.pi * phase / samples
    table = np.stack([np.cos(angle), -np.sin(angle)], axis=1) / math.sqrt(samples)
    return table.reshape(2 * frequencies, samples).astype(np.float32).astype(ml_dtypes.bfloat16)


def shot_table(shots, here):
    index = np.arange(shots).reshape(shots // here, here).T.reshape(-1)
    angle = 2.0 * math.pi * (index[:, None] * index[None, :] % shots) / shots
    table = np.concatenate([np.cos(angle), np.sin(angle)]) / math.sqrt(shots)
    return table.astype(np.float32).astype(ml_dtypes.bfloat16)


def shift_left(x, lane, offset):
    length = x.shape[1]
    return jnp.where(lane < length - offset, pltpu.roll(x, (2 * length - offset) % length, 1), 0.0)


def shift_right(x, lane, offset):
    return jnp.where(lane >= offset, pltpu.roll(x, offset % x.shape[1], 1), 0.0)


def kernel(
    dims,
    est_hbm, obs_hbm, delay_hbm, level_hbm, table_hbm, cn_hbm,
    out, total,
    est, obs, delay, level, table, cn,
    halo_out, halo_in, est_in, partial, base, stepped, energy, energies,
    send1, recv1, wide1, wide2, send2, recv2,
    load_sem, record_sem, halo_send, halo_recv, est_send, est_recv, wave_sem,
    send1_sem, recv1_sem, send2_sem, recv2_sem, energy_send, energy_recv,
):
    patches, n, rings, ring = dims
    shots, receivers, length = est.shape
    rest = length - LONGEST
    halves = stepped.shape[0]
    part = receivers // halves
    bands = table.shape[0] // 2 // n
    me, x = lax.axis_index("shot"), lax.axis_index("patch")
    z, place = me // ring, me % ring
    right, left = (me + 1) % n, (me + n - 1) % n
    last = n * shots - 1

    loads = [
        pltpu.make_async_copy(src, dst, load_sem.at[i])
        for i, (src, dst) in enumerate([(delay_hbm, delay), (level_hbm, level), (table_hbm, table), (cn_hbm, cn)])
    ]

    def record_loads(block):
        rows = pl.ds(block * (receivers // BLOCKS), receivers // BLOCKS)
        return [
            pltpu.make_async_copy(src.at[:, rows], dst.at[:, rows], record_sem.at[i, block])
            for i, (src, dst) in enumerate([(est_hbm, est), (obs_hbm, obs)])
        ]

    loads[0].start()
    for block in range(BLOCKS):
        for load in record_loads(block):
            load.start()
    for load in loads[1:]:
        load.start()

    barrier = pltpu.get_barrier_semaphore()

    def greet_ring(i, carry):
        pl.semaphore_signal(barrier, 1, device_id={"shot": z * ring + (place + i) % ring}, device_id_type=MESH)
        return carry

    def greet_patches(i, carry):
        pl.semaphore_signal(barrier, 1, device_id={"patch": (x + i) % patches}, device_id_type=MESH)
        return carry

    pl.semaphore_signal(barrier, 1, device_id={"shot": right}, device_id_type=MESH)
    pl.semaphore_signal(barrier, 1, device_id={"shot": left}, device_id_type=MESH)
    lax.fori_loop(1, ring, greet_ring, 0)

    def tell(sem, reach):
        for there, inside in [(z + reach, z + reach < rings), (z - reach, z >= reach)]:

            @pl.when(inside)
            def _():
                pl.semaphore_signal(sem, 1, device_id={"shot": there * ring + place}, device_id_type=MESH)

        return jnp.where(z + reach < rings, 1, 0) + jnp.where(z >= reach, 1, 0)

    beside = tell(barrier, 1)
    lax.fori_loop(1, patches, greet_patches, 0)

    loads[0].wait()
    first = me * shots
    delays = [delay[jnp.clip(first + i, 0, last)] for i in range(-2, 4)]
    a_prev, a_before, a_here, a_after, a_next = [SOURCE_SPACING + b - a for a, b in zip(delays, delays[1:])]
    has_left = me > 0
    has_right = me < n - 1
    lane = lax.broadcasted_iota(jnp.int32, (ROWS, length), 1)
    lane_rest = lax.broadcasted_iota(jnp.int32, (ROWS, rest), 1)

    def before_halo(i, carry):
        rows = pl.ds(i * ROWS, ROWS)
        e0 = est[0, rows, :].astype(jnp.float32)
        e1 = est[1, rows, :].astype(jnp.float32)
        p0 = obs[0, rows, :].astype(jnp.float32) - e0 - shift_right(e1, lane, a_here)
        p1 = obs[1, rows, :].astype(jnp.float32) - e1 - shift_left(e0, lane, a_here)
        partial[0, rows, :] = p0
        partial[1, rows, :] = p1
        once = shift_left(p1 - e1, lane, a_after)[:, :LONGEST]
        twice = shift_left(e1[:, LONGEST:], lane_rest, a_after + a_next - LONGEST)
        halo_out[0, rows, :] = jnp.concatenate([once, twice], axis=1).astype(jnp.bfloat16)
        once = shift_right(p0 - e0, lane, a_before)[:, rest:]
        twice = shift_right(e0[:, :rest], lane_rest, a_before + a_prev - LONGEST)
        halo_out[1, rows, :] = jnp.concatenate([once, twice], axis=1).astype(jnp.bfloat16)
        return carry

    def halo_copies(block):
        rows = pl.ds(block * (receivers // BLOCKS), receivers // BLOCKS)
        return [
            pltpu.make_async_remote_copy(
                halo_out.at[side, rows], halo_in.at[side, rows], halo_send.at[side, block], halo_recv.at[side, block],
                device_id={"shot": peer}, device_id_type=MESH,
            )
            for side, peer in enumerate([right, left])
        ]

    steps = receivers // ROWS // BLOCKS
    for block in range(BLOCKS):
        for load in record_loads(block):
            load.wait()
        lax.fori_loop(block * steps, (block + 1) * steps, before_halo, 0)
        if block == 0:
            pl.semaphore_wait(barrier, ring - 1 + patches - 1 + 2 + beside)
            tell(wave_sem.at[0], 1)
        for halo in halo_copies(block):
            halo.start()

    raw_halos = [
        pltpu.make_async_remote_copy(
            est.at[1 - side, :, pl.ds(rest * (1 - side), LONGEST)], est_in.at[side], est_send.at[side], est_recv.at[side],
            device_id={"shot": peer}, device_id_type=MESH,
        )
        for side, peer in enumerate([right, left])
    ]
    for halo in raw_halos:
        halo.start()

    def own_part(i, carry):
        rows = pl.ds(i * ROWS, ROWS)
        e0 = est[0, rows, :].astype(jnp.float32)
        e1 = est[1, rows, :].astype(jnp.float32)
        p0 = partial[0, rows, :]
        p1 = partial[1, rows, :]
        own0 = jnp.where(lane < jnp.where(has_left, length - a_before, 0), e0, 0.0)
        own1 = jnp.where(lane >= jnp.where(has_right, a_after, length), e1, 0.0)
        base[0, rows, :] = e0 + 0.5 * (p0 + shift_right(p1, lane, a_here) - own0)
        base[1, rows, :] = e1 + 0.5 * (p1 + shift_left(p0, lane, a_here) - own1)
        return carry

    lax.fori_loop(0, receivers // ROWS, own_part, 0)
    for load in loads[1:]:
        load.wait()

    def after_halo(i, carry):
        rows = pl.ds(i * ROWS, ROWS)
        from_left = jnp.where(has_left, halo_in[0, rows, :].astype(jnp.float32), 0.0)
        from_right = jnp.where(has_right, halo_in[1, rows, :].astype(jnp.float32), 0.0)
        h0 = jnp.concatenate([from_left[:, :LONGEST], -from_right[:, LONGEST:]], axis=1)
        h1 = jnp.concatenate([-from_left[:, LONGEST:], from_right[:, :LONGEST]], axis=1)
        h, r = i // (part // ROWS), lax.rem(i, part // ROWS) * ROWS
        stepped[h, pl.ds(r, ROWS), :] = (base[0, rows, :] + 0.5 * h0).astype(jnp.bfloat16)
        stepped[h, pl.ds(part + r, ROWS), :] = (base[1, rows, :] + 0.5 * h1).astype(jnp.bfloat16)
        return carry


    pl.semaphore_wait(wave_sem.at[0], beside)
    two_away = tell(wave_sem.at[1], 2)
    pl.semaphore_wait(wave_sem.at[1], two_away)
    four_away = tell(wave_sem.at[2], 4)

    half = rings // 2
    place_y, core = place // 2, place % 2
    at_z = [lax.rem(z + dz, rings) * ring for dz in range(rings)]
    at_y = [lax.rem(place_y + dy, rings) * 2 for dy in range(rings)]
    at_core = [core, 1 - core]
    peers = [
        at_z[dz] + at_y[dy] + at_core[dc]
        for hops in range(2 * half, -1, -1)
        for far_z in range(half + 1)
        for far_y in range(half + 1)
        if far_z + far_y == hops
        for dz in sorted({far_z, (rings - far_z) % rings})
        for dy in sorted({far_y, (rings - far_y) % rings})
        for dc in range(2)
        if dz or dy or dc
    ]

    def exchange(src, dst, ssem, rsem):
        for peer in peers:
            pltpu.make_async_remote_copy(
                src.at[peer], dst.at[me], ssem, rsem, device_id={"shot": peer}, device_id_type=MESH
            ).start()
        pltpu.make_async_copy(src.at[me], dst.at[me], rsem).start()

    def to_frequencies(h):
        for j in range(BLOCKS // halves):
            block = h * (BLOCKS // halves) + j
            for halo in halo_copies(block):
                halo.wait_recv()
            lax.fori_loop(block * steps, (block + 1) * steps, after_halo, 0)
        got = lax.dot_general(table[...], stepped[h], (((1,), (1,)), ((), ())), preferred_element_type=jnp.float32)
        send1[h] = got.reshape(n, 8, receivers).astype(jnp.bfloat16)
        pltpu.make_async_copy(send1.at[h, me], recv1.at[h, me], recv1_sem.at[h]).start()

    def send_planes(h, start, stop):
        def one(zz, carry):
            def send(dy, dc):
                peer = zz * ring + at_y[dy] + at_core[dc]
                pltpu.make_async_remote_copy(
                    send1.at[h, peer], recv1.at[h, me], send1_sem.at[h], recv1_sem.at[h],
                    device_id={"shot": peer}, device_id_type=MESH,
                ).start()

            for dy in sorted(range(rings), key=lambda d: -min(d, rings - d)):
                for dc in range(2):
                    if dy or dc:
                        send(dy, dc)

            @pl.when(zz != z)
            def _():
                send(0, 0)

            return carry

        lax.fori_loop(start, stop, one, 0)

    def send_near(h):
        send_planes(h, jnp.maximum(z - 3, 0), jnp.minimum(z + 4, rings))

    def send_far(h):
        send_planes(h, jnp.where(z < half, z + 4, 0), jnp.where(z < half, rings, z - 3))

    to_frequencies(0)
    send_near(0)

    @pl.when(z >= half)
    def _():
        pl.semaphore_wait(wave_sem.at[2], four_away)
        send_far(0)

    to_frequencies(1)
    send_near(1)

    @pl.when(z < half)
    def _():
        pl.semaphore_wait(wave_sem.at[2], four_away)
        send_far(0)

    send_far(1)

    for halo in raw_halos:
        halo.wait_recv()

    def misfit_part(i, carry):
        rows = pl.ds(i * ROWS, ROWS)
        blank = jnp.zeros((ROWS, rest), jnp.float32)
        from_left = jnp.concatenate([blank, est_in[0, rows, :].astype(jnp.float32)], axis=1)
        from_right = jnp.concatenate([est_in[1, rows, :].astype(jnp.float32), blank], axis=1)
        r0 = partial[0, rows, :] - jnp.where(has_left, shift_left(from_left, lane, a_before), 0.0)
        r1 = partial[1, rows, :] - jnp.where(has_right, shift_right(from_right, lane, a_after), 0.0)

        def squares(r):
            parts = jnp.zeros((8, 128), jnp.float32)
            for a in range(0, ROWS, 8):
                for b in range(0, length, 128):
                    piece = r[a : a + 8, b : b + 128]
                    parts = parts + piece * piece
            return parts

        return carry[0] + squares(r0), carry[1] + squares(r1)

    zero = jnp.zeros((8, 128), jnp.float32)
    e_0, e_1 = lax.fori_loop(0, receivers // ROWS, misfit_part, (zero, zero))
    energy[0] = e_0
    energy[1] = e_1
    for i in range(1, patches):
        pltpu.make_async_remote_copy(
            energy, energies.at[x], energy_send.at[i], energy_recv,
            device_id={"patch": (x + i) % patches}, device_id_type=MESH,
        ).start()
    pltpu.make_async_copy(energy, energies.at[x], energy_recv).start()

    wave = cn[...]
    k = n * shots

    low = lax.broadcasted_iota(jnp.int32, (n, receivers), 1) < part
    low_k = lax.broadcasted_iota(jnp.int32, (k, receivers), 1) < part

    def swapped(v):
        return pltpu.roll(v, part, 1)

    def exchanged(v0, v1):
        return jnp.where(low, v0, swapped(v1)), jnp.where(low, swapped(v0), v1)

    def to_shots(h, carry):
        pltpu.make_async_copy(recv1.at[h], recv1.at[h], recv1_sem.at[h]).wait()
        w1, w2 = wide1.at[h], wide2.at[h]
        w1[...] = recv1[h].astype(jnp.float32).reshape(8 * n, receivers)
        for pair in range(0, bands, 2):
            columns = []
            for q in range(2):
                cut = [w1[pl.ds(b * 2 + q, n, stride=8), :] for b in (pair, pair + 1)]
                columns.append(jnp.concatenate(exchanged(*cut), axis=0))
            field = jnp.concatenate(columns, axis=1).astype(jnp.bfloat16)
            got = jnp.dot(wave, field, preferred_element_type=jnp.float32)
            real = got[:k, :receivers] + got[k:, receivers:]
            imag = got[:k, receivers:] - got[k:, :receivers]
            f = me * bands + pair
            limit = jnp.where(low_k, level[f], level[f + 1])
            weight = jnp.where(low_k, jnp.where(f == 0, 1.0, 2.0), 2.0)
            magnitude = jnp.sqrt(real * real + imag * imag)
            factor = jnp.maximum(magnitude - limit, 0.0) / jnp.maximum(magnitude, limit) * weight
            shrunk = jnp.concatenate([real * factor, imag * factor], axis=1).astype(jnp.bfloat16)
            got = jnp.dot(wave, shrunk, preferred_element_type=jnp.float32)
            real = got[:k, :receivers] - got[k:, receivers:]
            imag = got[:k, receivers:] + got[k:, :receivers]
            for p, v in enumerate([real, imag]):
                for b, cut in zip((pair, pair + 1), exchanged(v[:n], v[n:])):
                    w2[pl.ds(b * 2 + p, n, stride=8), :] = cut
        send2[h] = w2[...].reshape(n, 8, receivers).astype(jnp.bfloat16)
        exchange(send2.at[h], recv2.at[h], send2_sem.at[h], recv2_sem.at[h])
        return carry

    lax.fori_loop(0, halves, to_shots, 0)

    pltpu.make_async_copy(energies, energies, energy_recv).wait()
    total[...] = sum(energies[i] for i in range(patches))

    for block in range(BLOCKS):
        for halo in halo_copies(block):
            halo.wait_send()
    for halo in raw_halos:
        halo.wait_send()
    for i in range(1, patches):
        pltpu.make_async_remote_copy(
            energy, energies.at[x], energy_send.at[i], energy_recv,
            device_id={"patch": (x + i) % patches}, device_id_type=MESH,
        ).wait_send()
    others = pl.ds(0, n - 1)
    for h in range(halves):
        pltpu.make_async_copy(send1.at[h, others], send1.at[h, others], send1_sem.at[h]).wait()

    def to_samples(h, carry):
        pltpu.make_async_copy(recv2.at[h], recv2.at[h], recv2_sem.at[h]).wait()
        field = recv2[h].astype(jnp.float32).reshape(8 * n, receivers).astype(jnp.bfloat16)
        got = lax.dot_general(field, table[...], (((0,), (0,)), ((), ())), preferred_element_type=jnp.float32)
        for s in range(shots):
            out[s, pl.ds(pl.multiple_of(h * part, part), part), :] = got[s * part : (s + 1) * part]
        return carry

    lax.fori_loop(0, halves, to_samples, 0)

    for h in range(halves):
        pltpu.make_async_copy(send2.at[h, others], send2.at[h, others], send2_sem.at[h]).wait()


def finish(count, field, total, out, misfit, means, sems):
    shots = field.shape[0]
    copies = [pltpu.make_async_copy(field.at[s], out.at[s], sems.at[s]) for s in range(shots)]
    for copy in copies:
        copy.start()
    for s in range(shots):
        means[s] = jnp.sum(total[s]) / count
    copies.append(pltpu.make_async_copy(means, misfit, sems.at[shots]))
    copies[-1].start()
    for copy in copies:
        copy.wait()


def local(dims, estimate, observed, delays, thresholds):
    shots, receivers, length = estimate.shape
    n = dims[1]
    frequencies = thresholds.shape[0]
    bf16, f32 = jnp.bfloat16, jnp.float32
    halves = 2
    table = jnp.asarray(time_table(frequencies, length))
    cn = jnp.asarray(shot_table(n * shots, shots))
    sem = pltpu.SemaphoreType.DMA
    vmem = pl.BlockSpec(memory_space=pltpu.VMEM)
    operands = (estimate, observed, delays, thresholds, table, cn)
    field, total = pl.pallas_call(
        functools.partial(kernel, dims),
        out_shape=(
            jax.ShapeDtypeStruct((shots, receivers, length), f32),
            jax.ShapeDtypeStruct((shots, 8, 128), f32),
        ),
        in_specs=[pl.BlockSpec(memory_space=pltpu.HBM)] * 6,
        out_specs=(vmem, vmem),
        scratch_shapes=[
            pltpu.VMEM(estimate.shape, bf16),
            pltpu.VMEM(estimate.shape, bf16),
            pltpu.SMEM(delays.shape, jnp.int32),
            pltpu.SMEM(thresholds.shape, f32),
            pltpu.VMEM(table.shape, bf16),
            pltpu.VMEM(cn.shape, bf16),
            pltpu.VMEM((2, receivers, length), bf16),
            pltpu.VMEM((2, receivers, length), bf16),
            pltpu.VMEM((2, receivers, LONGEST), bf16),
            pltpu.VMEM(estimate.shape, f32),
            pltpu.VMEM(estimate.shape, f32),
            pltpu.VMEM((halves, shots * receivers // halves, length), bf16),
            pltpu.VMEM((shots, 8, 128), f32),
            pltpu.VMEM((dims[0], shots, 8, 128), f32),
            pltpu.VMEM((halves, n, 8, receivers), bf16),
            pltpu.VMEM((halves, n, 8, receivers), bf16),
            pltpu.VMEM((halves, n * 8, receivers), f32),
            pltpu.VMEM((halves, n * 8, receivers), f32),
            pltpu.VMEM((halves, n, 8, receivers), bf16),
            pltpu.VMEM((halves, n, 8, receivers), bf16),
            sem((4,)),
            sem((2, BLOCKS)),
            sem((2, BLOCKS)),
            sem((2, BLOCKS)),
            sem((2,)),
            sem((2,)),
            pltpu.SemaphoreType.REGULAR((3,)),
            sem((halves,)),
            sem((halves,)),
            sem((halves,)),
            sem((halves,)),
            sem((dims[0],)),
            sem,
        ],
        compiler_params=pltpu.CompilerParams(
            collective_id=0, has_side_effects=True, vmem_limit_bytes=48 * 2**20
        ),
    )(*[pltpu.with_memory_space_constraint(v, pltpu.HBM) for v in operands])
    return pl.pallas_call(
        functools.partial(finish, dims[0] * receivers * length),
        out_shape=(jax.ShapeDtypeStruct(field.shape, f32), jax.ShapeDtypeStruct((shots,), f32)),
        in_specs=[vmem, vmem],
        out_specs=(pl.BlockSpec(memory_space=pltpu.HBM), pl.BlockSpec(memory_space=pltpu.HBM)),
        scratch_shapes=[pltpu.SMEM((shots,), f32), sem((shots + 1,))],
        compiler_params=pltpu.CompilerParams(vmem_limit_bytes=8 * 2**20),
    )(field, total)


def solution(mesh):
    patches, n = mesh.shape["patch"], mesh.shape["shot"]
    rings = 8
    dims = (patches, n, rings, n // rings)
    in_specs = (P("shot", "patch", None), P("shot", "patch", None), P(), P())
    out_specs = (P("shot", "patch", None), P("shot"))
    return jax.shard_map(
        functools.partial(local, dims), mesh=mesh, in_specs=in_specs, out_specs=out_specs, check_vma=False
    )
```

```python
import functools
import math

import jax
import jax.numpy as jnp
import ml_dtypes
import numpy as np
from jax import lax
from jax.experimental import pallas as pl
from jax.experimental.pallas import tpu as pltpu
from jax.sharding import PartitionSpec as P

SOURCE_SPACING = 512
LONGEST = 768
ROWS = 16
BLOCKS = 4
MESH = pl.DeviceIdType.MESH


def time_table(frequencies, samples):
    phase = np.arange(frequencies)[:, None] * np.arange(samples)[None, :] % samples
    angle = 2.0 * math.pi * phase / samples
    table = np.stack([np.cos(angle), -np.sin(angle)], axis=1) / math.sqrt(samples)
    return table.reshape(2 * frequencies, samples).astype(np.float32).astype(ml_dtypes.bfloat16)


def shot_table(shots, here):
    index = np.arange(shots).reshape(shots // here, here).T.reshape(-1)
    angle = 2.0 * math.pi * (index[:, None] * index[None, :] % shots) / shots
    table = np.concatenate([np.cos(angle), np.sin(angle)]) / math.sqrt(shots)
    return table.astype(np.float32).astype(ml_dtypes.bfloat16)


def shift_left(x, lane, offset):
    length = x.shape[1]
    return jnp.where(lane < length - offset, pltpu.roll(x, (2 * length - offset) % length, 1), 0.0)


def shift_right(x, lane, offset):
    return jnp.where(lane >= offset, pltpu.roll(x, offset % x.shape[1], 1), 0.0)


def kernel(
    dims,
    est_hbm, obs_hbm, delay_hbm, level_hbm, table_hbm, cn_hbm,
    out, total,
    est, obs, delay, level, table, cn,
    halo_out, halo_in, est_in, partial, base, stepped, energy, energies,
    send1, recv1, wide1, wide2, send2, recv2,
    load_sem, record_sem, halo_send, halo_recv, est_send, est_recv, plane_sem,
    send1_sem, recv1_sem, send2_sem, recv2_sem, energy_send, energy_recv,
):
    patches, n, rings, ring = dims
    shots, receivers, length = est.shape
    rest = length - LONGEST
    halves = stepped.shape[0]
    part = receivers // halves
    bands = table.shape[0] // 2 // n
    me, x = lax.axis_index("shot"), lax.axis_index("patch")
    z, place = me // ring, me % ring
    right, left = (me + 1) % n, (me + n - 1) % n
    last = n * shots - 1

    loads = [
        pltpu.make_async_copy(src, dst, load_sem.at[i])
        for i, (src, dst) in enumerate([(delay_hbm, delay), (level_hbm, level), (table_hbm, table), (cn_hbm, cn)])
    ]

    def record_loads(block):
        rows = pl.ds(block * (receivers // BLOCKS), receivers // BLOCKS)
        return [
            pltpu.make_async_copy(src.at[:, rows], dst.at[:, rows], record_sem.at[i, block])
            for i, (src, dst) in enumerate([(est_hbm, est), (obs_hbm, obs)])
        ]

    loads[0].start()
    for block in range(BLOCKS):
        for load in record_loads(block):
            load.start()
    for load in loads[1:]:
        load.start()

    barrier = pltpu.get_barrier_semaphore()

    def greet_ring(i, carry):
        pl.semaphore_signal(barrier, 1, device_id={"shot": z * ring + (place + i) % ring}, device_id_type=MESH)
        return carry

    def greet_planes(i, carry):
        pl.semaphore_signal(barrier, 1, device_id={"shot": (z + i) % rings * ring + place}, device_id_type=MESH)
        return carry

    def greet_patches(i, carry):
        pl.semaphore_signal(barrier, 1, device_id={"patch": (x + i) % patches}, device_id_type=MESH)
        return carry

    pl.semaphore_signal(barrier, 1, device_id={"shot": right}, device_id_type=MESH)
    pl.semaphore_signal(barrier, 1, device_id={"shot": left}, device_id_type=MESH)
    lax.fori_loop(1, ring, greet_ring, 0)
    lax.fori_loop(1, rings, greet_planes, 0)
    lax.fori_loop(1, patches, greet_patches, 0)

    loads[0].wait()
    first = me * shots
    delays = [delay[jnp.clip(first + i, 0, last)] for i in range(-2, 4)]
    a_prev, a_before, a_here, a_after, a_next = [SOURCE_SPACING + b - a for a, b in zip(delays, delays[1:])]
    has_left = me > 0
    has_right = me < n - 1
    lane = lax.broadcasted_iota(jnp.int32, (ROWS, length), 1)
    lane_rest = lax.broadcasted_iota(jnp.int32, (ROWS, rest), 1)

    def before_halo(i, carry):
        rows = pl.ds(i * ROWS, ROWS)
        e0 = est[0, rows, :].astype(jnp.float32)
        e1 = est[1, rows, :].astype(jnp.float32)
        p0 = obs[0, rows, :].astype(jnp.float32) - e0 - shift_right(e1, lane, a_here)
        p1 = obs[1, rows, :].astype(jnp.float32) - e1 - shift_left(e0, lane, a_here)
        partial[0, rows, :] = p0
        partial[1, rows, :] = p1
        once = shift_left(p1 - e1, lane, a_after)[:, :LONGEST]
        twice = shift_left(e1[:, LONGEST:], lane_rest, a_after + a_next - LONGEST)
        halo_out[0, rows, :] = jnp.concatenate([once, twice], axis=1).astype(jnp.bfloat16)
        once = shift_right(p0 - e0, lane, a_before)[:, rest:]
        twice = shift_right(e0[:, :rest], lane_rest, a_before + a_prev - LONGEST)
        halo_out[1, rows, :] = jnp.concatenate([once, twice], axis=1).astype(jnp.bfloat16)
        return carry

    def halo_copies(block):
        rows = pl.ds(block * (receivers // BLOCKS), receivers // BLOCKS)
        return [
            pltpu.make_async_remote_copy(
                halo_out.at[side, rows], halo_in.at[side, rows], halo_send.at[side, block], halo_recv.at[side, block],
                device_id={"shot": peer}, device_id_type=MESH,
            )
            for side, peer in enumerate([right, left])
        ]

    steps = receivers // ROWS // BLOCKS
    for block in range(BLOCKS):
        for load in record_loads(block):
            load.wait()
        lax.fori_loop(block * steps, (block + 1) * steps, before_halo, 0)
        if block == 0:
            pl.semaphore_wait(barrier, ring - 1 + rings - 1 + patches - 1 + 2)
        for halo in halo_copies(block):
            halo.start()

    raw_halos = [
        pltpu.make_async_remote_copy(
            est.at[1 - side, :, pl.ds(rest * (1 - side), LONGEST)], est_in.at[side], est_send.at[side], est_recv.at[side],
            device_id={"shot": peer}, device_id_type=MESH,
        )
        for side, peer in enumerate([right, left])
    ]
    def plane_ready(i, carry):
        pl.semaphore_signal(plane_sem, 1, device_id={"shot": (z + i) % rings * ring + place}, device_id_type=MESH)
        return carry

    lax.fori_loop(1, rings, plane_ready, 0)

    def own_part(i, carry):
        rows = pl.ds(i * ROWS, ROWS)
        e0 = est[0, rows, :].astype(jnp.float32)
        e1 = est[1, rows, :].astype(jnp.float32)
        p0 = partial[0, rows, :]
        p1 = partial[1, rows, :]
        own0 = jnp.where(lane < jnp.where(has_left, length - a_before, 0), e0, 0.0)
        own1 = jnp.where(lane >= jnp.where(has_right, a_after, length), e1, 0.0)
        base[0, rows, :] = e0 + 0.5 * (p0 + shift_right(p1, lane, a_here) - own0)
        base[1, rows, :] = e1 + 0.5 * (p1 + shift_left(p0, lane, a_here) - own1)
        return carry

    lax.fori_loop(0, receivers // ROWS, own_part, 0)
    for load in loads[1:]:
        load.wait()

    def after_halo(i, carry):
        rows = pl.ds(i * ROWS, ROWS)
        from_left = jnp.where(has_left, halo_in[0, rows, :].astype(jnp.float32), 0.0)
        from_right = jnp.where(has_right, halo_in[1, rows, :].astype(jnp.float32), 0.0)
        h0 = jnp.concatenate([from_left[:, :LONGEST], -from_right[:, LONGEST:]], axis=1)
        h1 = jnp.concatenate([-from_left[:, LONGEST:], from_right[:, :LONGEST]], axis=1)
        h, r = i // (part // ROWS), lax.rem(i, part // ROWS) * ROWS
        stepped[h, pl.ds(r, ROWS), :] = (base[0, rows, :] + 0.5 * h0).astype(jnp.bfloat16)
        stepped[h, pl.ds(part + r, ROWS), :] = (base[1, rows, :] + 0.5 * h1).astype(jnp.bfloat16)
        return carry


    pl.semaphore_wait(plane_sem, rings - 1)

    half = rings // 2
    place_y, core = place // 2, place % 2
    at_z = [lax.rem(z + dz, rings) * ring for dz in range(rings)]
    at_y = [lax.rem(place_y + dy, rings) * 2 for dy in range(rings)]
    at_core = [core, 1 - core]
    peers = [
        at_z[dz] + at_y[dy] + at_core[dc]
        for hops in range(2 * half, -1, -1)
        for far_z in range(half + 1)
        for far_y in range(half + 1)
        if far_z + far_y == hops
        for dz in sorted({far_z, (rings - far_z) % rings})
        for dy in sorted({far_y, (rings - far_y) % rings})
        for dc in range(2)
        if dz or dy or dc
    ]

    def exchange(src, dst, ssem, rsem):
        for peer in peers:
            pltpu.make_async_remote_copy(
                src.at[peer], dst.at[me], ssem, rsem, device_id={"shot": peer}, device_id_type=MESH
            ).start()
        pltpu.make_async_copy(src.at[me], dst.at[me], rsem).start()

    def to_frequencies(h, carry):
        for j in range(BLOCKS // halves):
            block = h * (BLOCKS // halves) + j
            for halo in halo_copies(block):
                halo.wait_recv()
            lax.fori_loop(block * steps, (block + 1) * steps, after_halo, 0)
        got = lax.dot_general(table[...], stepped[h], (((1,), (1,)), ((), ())), preferred_element_type=jnp.float32)
        send1[h] = got.reshape(n, 8, receivers).astype(jnp.bfloat16)
        exchange(send1.at[h], recv1.at[h], send1_sem.at[h], recv1_sem.at[h])

        @pl.when(h == 0)
        def _():
            for halo in raw_halos:
                halo.start()

        return carry

    lax.fori_loop(0, halves, to_frequencies, 0)

    def own_misfit():
        for halo in raw_halos:
            halo.wait_recv()

        def misfit_part(i, carry):
            rows = pl.ds(i * ROWS, ROWS)
            blank = jnp.zeros((ROWS, rest), jnp.float32)
            from_left = jnp.concatenate([blank, est_in[0, rows, :].astype(jnp.float32)], axis=1)
            from_right = jnp.concatenate([est_in[1, rows, :].astype(jnp.float32), blank], axis=1)
            r0 = partial[0, rows, :] - jnp.where(has_left, shift_left(from_left, lane, a_before), 0.0)
            r1 = partial[1, rows, :] - jnp.where(has_right, shift_right(from_right, lane, a_after), 0.0)

            def squares(r):
                parts = jnp.zeros((8, 128), jnp.float32)
                for a in range(0, ROWS, 8):
                    for b in range(0, length, 128):
                        piece = r[a : a + 8, b : b + 128]
                        parts = parts + piece * piece
                return parts

            return carry[0] + squares(r0), carry[1] + squares(r1)

        zero = jnp.zeros((8, 128), jnp.float32)
        e_0, e_1 = lax.fori_loop(0, receivers // ROWS, misfit_part, (zero, zero))
        energy[0] = e_0
        energy[1] = e_1
        for i in range(1, patches):
            pltpu.make_async_remote_copy(
                energy, energies.at[x], energy_send.at[i], energy_recv,
                device_id={"patch": (x + i) % patches}, device_id_type=MESH,
            ).start()
        pltpu.make_async_copy(energy, energies.at[x], energy_recv).start()

    wave = cn[...]
    k = n * shots

    low = lax.broadcasted_iota(jnp.int32, (n, receivers), 1) < part
    low_k = lax.broadcasted_iota(jnp.int32, (k, receivers), 1) < part

    def swapped(v):
        return pltpu.roll(v, part, 1)

    def exchanged(v0, v1):
        return jnp.where(low, v0, swapped(v1)), jnp.where(low, swapped(v0), v1)

    def to_shots(h, carry):
        pltpu.make_async_copy(recv1.at[h], recv1.at[h], recv1_sem.at[h]).wait()
        w1, w2 = wide1.at[h], wide2.at[h]
        w1[...] = recv1[h].astype(jnp.float32).reshape(8 * n, receivers)
        for pair in range(0, bands, 2):
            columns = []
            for q in range(2):
                cut = [w1[pl.ds(b * 2 + q, n, stride=8), :] for b in (pair, pair + 1)]
                columns.append(jnp.concatenate(exchanged(*cut), axis=0))
            field = jnp.concatenate(columns, axis=1).astype(jnp.bfloat16)
            got = jnp.dot(wave, field, preferred_element_type=jnp.float32)
            real = got[:k, :receivers] + got[k:, receivers:]
            imag = got[:k, receivers:] - got[k:, :receivers]
            f = me * bands + pair
            limit = jnp.where(low_k, level[f], level[f + 1])
            weight = jnp.where(low_k, jnp.where(f == 0, 1.0, 2.0), 2.0)
            magnitude = jnp.sqrt(real * real + imag * imag)
            factor = jnp.maximum(magnitude - limit, 0.0) / jnp.maximum(magnitude, limit) * weight
            shrunk = jnp.concatenate([real * factor, imag * factor], axis=1).astype(jnp.bfloat16)
            got = jnp.dot(wave, shrunk, preferred_element_type=jnp.float32)
            real = got[:k, :receivers] - got[k:, receivers:]
            imag = got[:k, receivers:] + got[k:, :receivers]
            for p, v in enumerate([real, imag]):
                for b, cut in zip((pair, pair + 1), exchanged(v[:n], v[n:])):
                    w2[pl.ds(b * 2 + p, n, stride=8), :] = cut
        send2[h] = w2[...].reshape(n, 8, receivers).astype(jnp.bfloat16)
        exchange(send2.at[h], recv2.at[h], send2_sem.at[h], recv2_sem.at[h])
        pl.when(h == 0)(own_misfit)
        return carry

    lax.fori_loop(0, halves, to_shots, 0)

    pltpu.make_async_copy(energies, energies, energy_recv).wait()
    total[...] = sum(energies[i] for i in range(patches))

    for block in range(BLOCKS):
        for halo in halo_copies(block):
            halo.wait_send()
    for halo in raw_halos:
        halo.wait_send()
    for i in range(1, patches):
        pltpu.make_async_remote_copy(
            energy, energies.at[x], energy_send.at[i], energy_recv,
            device_id={"patch": (x + i) % patches}, device_id_type=MESH,
        ).wait_send()
    others = pl.ds(0, n - 1)
    for h in range(halves):
        pltpu.make_async_copy(send1.at[h, others], send1.at[h, others], send1_sem.at[h]).wait()

    def to_samples(h, carry):
        pltpu.make_async_copy(recv2.at[h], recv2.at[h], recv2_sem.at[h]).wait()
        field = recv2[h].astype(jnp.float32).reshape(8 * n, receivers).astype(jnp.bfloat16)
        got = lax.dot_general(field, table[...], (((0,), (0,)), ((), ())), preferred_element_type=jnp.float32)
        for s in range(shots):
            out[s, pl.ds(pl.multiple_of(h * part, part), part), :] = got[s * part : (s + 1) * part]
        return carry

    lax.fori_loop(0, halves, to_samples, 0)

    for h in range(halves):
        pltpu.make_async_copy(send2.at[h, others], send2.at[h, others], send2_sem.at[h]).wait()


def finish(count, field, total, out, misfit, means, sems):
    shots = field.shape[0]
    copies = [pltpu.make_async_copy(field.at[s], out.at[s], sems.at[s]) for s in range(shots)]
    for copy in copies:
        copy.start()
    for s in range(shots):
        means[s] = jnp.sum(total[s]) / count
    copies.append(pltpu.make_async_copy(means, misfit, sems.at[shots]))
    copies[-1].start()
    for copy in copies:
        copy.wait()


def local(dims, estimate, observed, delays, thresholds):
    shots, receivers, length = estimate.shape
    n = dims[1]
    frequencies = thresholds.shape[0]
    bf16, f32 = jnp.bfloat16, jnp.float32
    halves = 2
    table = jnp.asarray(time_table(frequencies, length))
    cn = jnp.asarray(shot_table(n * shots, shots))
    sem = pltpu.SemaphoreType.DMA
    vmem = pl.BlockSpec(memory_space=pltpu.VMEM)
    operands = (estimate, observed, delays, thresholds, table, cn)
    field, total = pl.pallas_call(
        functools.partial(kernel, dims),
        out_shape=(
            jax.ShapeDtypeStruct((shots, receivers, length), f32),
            jax.ShapeDtypeStruct((shots, 8, 128), f32),
        ),
        in_specs=[pl.BlockSpec(memory_space=pltpu.HBM)] * 6,
        out_specs=(vmem, vmem),
        scratch_shapes=[
            pltpu.VMEM(estimate.shape, bf16),
            pltpu.VMEM(estimate.shape, bf16),
            pltpu.SMEM(delays.shape, jnp.int32),
            pltpu.SMEM(thresholds.shape, f32),
            pltpu.VMEM(table.shape, bf16),
            pltpu.VMEM(cn.shape, bf16),
            pltpu.VMEM((2, receivers, length), bf16),
            pltpu.VMEM((2, receivers, length), bf16),
            pltpu.VMEM((2, receivers, LONGEST), bf16),
            pltpu.VMEM(estimate.shape, f32),
            pltpu.VMEM(estimate.shape, f32),
            pltpu.VMEM((halves, shots * receivers // halves, length), bf16),
            pltpu.VMEM((shots, 8, 128), f32),
            pltpu.VMEM((dims[0], shots, 8, 128), f32),
            pltpu.VMEM((halves, n, 8, receivers), bf16),
            pltpu.VMEM((halves, n, 8, receivers), bf16),
            pltpu.VMEM((halves, n * 8, receivers), f32),
            pltpu.VMEM((halves, n * 8, receivers), f32),
            pltpu.VMEM((halves, n, 8, receivers), bf16),
            pltpu.VMEM((halves, n, 8, receivers), bf16),
            sem((4,)),
            sem((2, BLOCKS)),
            sem((2, BLOCKS)),
            sem((2, BLOCKS)),
            sem((2,)),
            sem((2,)),
            pltpu.SemaphoreType.REGULAR,
            sem((halves,)),
            sem((halves,)),
            sem((halves,)),
            sem((halves,)),
            sem((dims[0],)),
            sem,
        ],
        compiler_params=pltpu.CompilerParams(
            collective_id=0, has_side_effects=True, vmem_limit_bytes=48 * 2**20
        ),
    )(*[pltpu.with_memory_space_constraint(v, pltpu.HBM) for v in operands])
    return pl.pallas_call(
        functools.partial(finish, dims[0] * receivers * length),
        out_shape=(jax.ShapeDtypeStruct(field.shape, f32), jax.ShapeDtypeStruct((shots,), f32)),
        in_specs=[vmem, vmem],
        out_specs=(pl.BlockSpec(memory_space=pltpu.HBM), pl.BlockSpec(memory_space=pltpu.HBM)),
        scratch_shapes=[pltpu.SMEM((shots,), f32), sem((shots + 1,))],
        compiler_params=pltpu.CompilerParams(vmem_limit_bytes=8 * 2**20),
    )(field, total)


def solution(mesh):
    patches, n = mesh.shape["patch"], mesh.shape["shot"]
    rings = 8
    dims = (patches, n, rings, n // rings)
    in_specs = (P("shot", "patch", None), P("shot", "patch", None), P(), P())
    out_specs = (P("shot", "patch", None), P("shot"))
    return jax.shard_map(
        functools.partial(local, dims), mesh=mesh, in_specs=in_specs, out_specs=out_specs, check_vma=False
    )
```

```python
import functools
import math

import jax
import jax.numpy as jnp
import ml_dtypes
import numpy as np
from jax import lax
from jax.experimental import pallas as pl
from jax.experimental.pallas import tpu as pltpu
from jax.sharding import PartitionSpec as P

SOURCE_SPACING = 512
LONGEST = 768
ROWS = 16
BLOCKS = 4
MESH = pl.DeviceIdType.MESH


def time_table(frequencies, samples):
    phase = np.arange(frequencies)[:, None] * np.arange(samples)[None, :] % samples
    angle = 2.0 * math.pi * phase / samples
    table = np.stack([np.cos(angle), -np.sin(angle)], axis=1) / math.sqrt(samples)
    return table.reshape(2 * frequencies, samples).astype(np.float32).astype(ml_dtypes.bfloat16)


def shot_table(shots, here):
    index = np.arange(shots).reshape(shots // here, here).T.reshape(-1)
    angle = 2.0 * math.pi * (index[:, None] * index[None, :] % shots) / shots
    table = np.concatenate([np.cos(angle), np.sin(angle)]) / math.sqrt(shots)
    return table.astype(np.float32).astype(ml_dtypes.bfloat16)


def shift_left(x, lane, offset):
    length = x.shape[1]
    return jnp.where(lane < length - offset, pltpu.roll(x, (2 * length - offset) % length, 1), 0.0)


def shift_right(x, lane, offset):
    return jnp.where(lane >= offset, pltpu.roll(x, offset % x.shape[1], 1), 0.0)


def kernel(
    dims,
    est_hbm, obs_hbm, delay_hbm, level_hbm, table_hbm, cn_hbm,
    out, total,
    est, obs, delay, level, table, cn,
    halo_out, halo_in, est_in, partial, base, stepped, energy, energies,
    send1, recv1, wide1, wide2, send2, recv2,
    load_sem, record_sem, halo_send, halo_recv, est_send, est_recv, plane_sem,
    send1_sem, recv1_sem, send2_sem, recv2_sem, energy_send, energy_recv,
):
    patches, n, rings, ring = dims
    shots, receivers, length = est.shape
    rest = length - LONGEST
    halves = stepped.shape[0]
    part = receivers // halves
    bands = table.shape[0] // 2 // n
    me, x = lax.axis_index("shot"), lax.axis_index("patch")
    z, place = me // ring, me % ring
    right, left = (me + 1) % n, (me + n - 1) % n
    last = n * shots - 1

    loads = [
        pltpu.make_async_copy(src, dst, load_sem.at[i])
        for i, (src, dst) in enumerate([(delay_hbm, delay), (level_hbm, level), (table_hbm, table), (cn_hbm, cn)])
    ]

    def record_loads(block):
        rows = pl.ds(block * (receivers // BLOCKS), receivers // BLOCKS)
        return [
            pltpu.make_async_copy(src.at[:, rows], dst.at[:, rows], record_sem.at[i, block])
            for i, (src, dst) in enumerate([(est_hbm, est), (obs_hbm, obs)])
        ]

    loads[0].start()
    for block in range(BLOCKS):
        for load in record_loads(block):
            load.start()
    for load in loads[1:]:
        load.start()

    barrier = pltpu.get_barrier_semaphore()

    def greet_ring(i, carry):
        pl.semaphore_signal(barrier, 1, device_id={"shot": z * ring + (place + i) % ring}, device_id_type=MESH)
        return carry

    def greet_planes(i, carry):
        pl.semaphore_signal(barrier, 1, device_id={"shot": (z + i) % rings * ring + place}, device_id_type=MESH)
        return carry

    def greet_patches(i, carry):
        pl.semaphore_signal(barrier, 1, device_id={"patch": (x + i) % patches}, device_id_type=MESH)
        return carry

    pl.semaphore_signal(barrier, 1, device_id={"shot": right}, device_id_type=MESH)
    pl.semaphore_signal(barrier, 1, device_id={"shot": left}, device_id_type=MESH)
    lax.fori_loop(1, ring, greet_ring, 0)
    lax.fori_loop(1, rings, greet_planes, 0)
    lax.fori_loop(1, patches, greet_patches, 0)

    loads[0].wait()
    first = me * shots
    delays = [delay[jnp.clip(first + i, 0, last)] for i in range(-2, 4)]
    a_prev, a_before, a_here, a_after, a_next = [SOURCE_SPACING + b - a for a, b in zip(delays, delays[1:])]
    has_left = me > 0
    has_right = me < n - 1
    lane = lax.broadcasted_iota(jnp.int32, (ROWS, length), 1)
    lane_rest = lax.broadcasted_iota(jnp.int32, (ROWS, rest), 1)

    def before_halo(i, carry):
        rows = pl.ds(i * ROWS, ROWS)
        e0 = est[0, rows, :].astype(jnp.float32)
        e1 = est[1, rows, :].astype(jnp.float32)
        p0 = obs[0, rows, :].astype(jnp.float32) - e0 - shift_right(e1, lane, a_here)
        p1 = obs[1, rows, :].astype(jnp.float32) - e1 - shift_left(e0, lane, a_here)
        partial[0, rows, :] = p0
        partial[1, rows, :] = p1
        once = shift_left(p1 - e1, lane, a_after)[:, :LONGEST]
        twice = shift_left(e1[:, LONGEST:], lane_rest, a_after + a_next - LONGEST)
        halo_out[0, rows, :] = jnp.concatenate([once, twice], axis=1).astype(jnp.bfloat16)
        once = shift_right(p0 - e0, lane, a_before)[:, rest:]
        twice = shift_right(e0[:, :rest], lane_rest, a_before + a_prev - LONGEST)
        halo_out[1, rows, :] = jnp.concatenate([once, twice], axis=1).astype(jnp.bfloat16)
        return carry

    def halo_copies(block):
        rows = pl.ds(block * (receivers // BLOCKS), receivers // BLOCKS)
        return [
            pltpu.make_async_remote_copy(
                halo_out.at[side, rows], halo_in.at[side, rows], halo_send.at[side, block], halo_recv.at[side, block],
                device_id={"shot": peer}, device_id_type=MESH,
            )
            for side, peer in enumerate([right, left])
        ]

    steps = receivers // ROWS // BLOCKS
    for block in range(BLOCKS):
        for load in record_loads(block):
            load.wait()
        lax.fori_loop(block * steps, (block + 1) * steps, before_halo, 0)
        if block == 0:
            pl.semaphore_wait(barrier, ring - 1 + rings - 1 + patches - 1 + 2)
        for halo in halo_copies(block):
            halo.start()

    raw_halos = [
        pltpu.make_async_remote_copy(
            est.at[1 - side, :, pl.ds(rest * (1 - side), LONGEST)], est_in.at[side], est_send.at[side], est_recv.at[side],
            device_id={"shot": peer}, device_id_type=MESH,
        )
        for side, peer in enumerate([right, left])
    ]
    for halo in raw_halos:
        halo.start()

    def plane_ready(i, carry):
        pl.semaphore_signal(plane_sem, 1, device_id={"shot": (z + i) % rings * ring + place}, device_id_type=MESH)
        return carry

    lax.fori_loop(1, rings, plane_ready, 0)

    def own_part(i, carry):
        rows = pl.ds(i * ROWS, ROWS)
        e0 = est[0, rows, :].astype(jnp.float32)
        e1 = est[1, rows, :].astype(jnp.float32)
        p0 = partial[0, rows, :]
        p1 = partial[1, rows, :]
        own0 = jnp.where(lane < jnp.where(has_left, length - a_before, 0), e0, 0.0)
        own1 = jnp.where(lane >= jnp.where(has_right, a_after, length), e1, 0.0)
        base[0, rows, :] = e0 + 0.5 * (p0 + shift_right(p1, lane, a_here) - own0)
        base[1, rows, :] = e1 + 0.5 * (p1 + shift_left(p0, lane, a_here) - own1)
        return carry

    lax.fori_loop(0, receivers // ROWS, own_part, 0)
    for load in loads[1:]:
        load.wait()

    def after_halo(i, carry):
        rows = pl.ds(i * ROWS, ROWS)
        from_left = jnp.where(has_left, halo_in[0, rows, :].astype(jnp.float32), 0.0)
        from_right = jnp.where(has_right, halo_in[1, rows, :].astype(jnp.float32), 0.0)
        h0 = jnp.concatenate([from_left[:, :LONGEST], -from_right[:, LONGEST:]], axis=1)
        h1 = jnp.concatenate([-from_left[:, LONGEST:], from_right[:, :LONGEST]], axis=1)
        h, r = i // (part // ROWS), lax.rem(i, part // ROWS) * ROWS
        stepped[h, pl.ds(r, ROWS), :] = (base[0, rows, :] + 0.5 * h0).astype(jnp.bfloat16)
        stepped[h, pl.ds(part + r, ROWS), :] = (base[1, rows, :] + 0.5 * h1).astype(jnp.bfloat16)
        return carry


    pl.semaphore_wait(plane_sem, rings - 1)

    half = rings // 2
    place_y, core = place // 2, place % 2
    at_z = [lax.rem(z + dz, rings) * ring for dz in range(rings)]
    at_y = [lax.rem(place_y + dy, rings) * 2 for dy in range(rings)]
    at_core = [core, 1 - core]
    peers = [
        at_z[dz] + at_y[dy] + at_core[dc]
        for hops in range(2 * half, -1, -1)
        for far_z in range(half + 1)
        for far_y in range(half + 1)
        if far_z + far_y == hops
        for dz in sorted({far_z, (rings - far_z) % rings})
        for dy in sorted({far_y, (rings - far_y) % rings})
        for dc in range(2)
        if dz or dy or dc
    ]

    def exchange(src, dst, ssem, rsem):
        for peer in peers:
            pltpu.make_async_remote_copy(
                src.at[peer], dst.at[me], ssem, rsem, device_id={"shot": peer}, device_id_type=MESH
            ).start()
        pltpu.make_async_copy(src.at[me], dst.at[me], rsem).start()

    def to_frequencies(h, carry):
        for j in range(BLOCKS // halves):
            block = h * (BLOCKS // halves) + j
            for halo in halo_copies(block):
                halo.wait_recv()
            lax.fori_loop(block * steps, (block + 1) * steps, after_halo, 0)
        got = lax.dot_general(table[...], stepped[h], (((1,), (1,)), ((), ())), preferred_element_type=jnp.float32)
        send1[h] = got.reshape(n, 8, receivers).astype(jnp.bfloat16)
        exchange(send1.at[h], recv1.at[h], send1_sem.at[h], recv1_sem.at[h])
        return carry

    lax.fori_loop(0, halves, to_frequencies, 0)

    for halo in raw_halos:
        halo.wait_recv()

    def misfit_part(i, carry):
        rows = pl.ds(i * ROWS, ROWS)
        blank = jnp.zeros((ROWS, rest), jnp.float32)
        from_left = jnp.concatenate([blank, est_in[0, rows, :].astype(jnp.float32)], axis=1)
        from_right = jnp.concatenate([est_in[1, rows, :].astype(jnp.float32), blank], axis=1)
        r0 = partial[0, rows, :] - jnp.where(has_left, shift_left(from_left, lane, a_before), 0.0)
        r1 = partial[1, rows, :] - jnp.where(has_right, shift_right(from_right, lane, a_after), 0.0)

        def squares(r):
            parts = jnp.zeros((8, 128), jnp.float32)
            for a in range(0, ROWS, 8):
                for b in range(0, length, 128):
                    piece = r[a : a + 8, b : b + 128]
                    parts = parts + piece * piece
            return parts

        return carry[0] + squares(r0), carry[1] + squares(r1)

    zero = jnp.zeros((8, 128), jnp.float32)
    e_0, e_1 = lax.fori_loop(0, receivers // ROWS, misfit_part, (zero, zero))
    energy[0] = e_0
    energy[1] = e_1
    for i in range(1, patches):
        pltpu.make_async_remote_copy(
            energy, energies.at[x], energy_send.at[i], energy_recv,
            device_id={"patch": (x + i) % patches}, device_id_type=MESH,
        ).start()
    pltpu.make_async_copy(energy, energies.at[x], energy_recv).start()

    wave = cn[...]
    k = n * shots

    low = lax.broadcasted_iota(jnp.int32, (n, receivers), 1) < part
    low_k = lax.broadcasted_iota(jnp.int32, (k, receivers), 1) < part

    def swapped(v):
        return pltpu.roll(v, part, 1)

    def exchanged(v0, v1):
        return jnp.where(low, v0, swapped(v1)), jnp.where(low, swapped(v0), v1)

    def to_shots(h, carry):
        pltpu.make_async_copy(recv1.at[h], recv1.at[h], recv1_sem.at[h]).wait()
        w1, w2 = wide1.at[h], wide2.at[h]
        w1[...] = recv1[h].astype(jnp.float32).reshape(8 * n, receivers)
        for pair in range(0, bands, 2):
            columns = []
            for q in range(2):
                cut = [w1[pl.ds(b * 2 + q, n, stride=8), :] for b in (pair, pair + 1)]
                columns.append(jnp.concatenate(exchanged(*cut), axis=0))
            field = jnp.concatenate(columns, axis=1).astype(jnp.bfloat16)
            got = jnp.dot(wave, field, preferred_element_type=jnp.float32)
            real = got[:k, :receivers] + got[k:, receivers:]
            imag = got[:k, receivers:] - got[k:, :receivers]
            f = me * bands + pair
            limit = jnp.where(low_k, level[f], level[f + 1])
            weight = jnp.where(low_k, jnp.where(f == 0, 1.0, 2.0), 2.0)
            magnitude = jnp.sqrt(real * real + imag * imag)
            factor = jnp.maximum(magnitude - limit, 0.0) / jnp.maximum(magnitude, limit) * weight
            shrunk = jnp.concatenate([real * factor, imag * factor], axis=1).astype(jnp.bfloat16)
            got = jnp.dot(wave, shrunk, preferred_element_type=jnp.float32)
            real = got[:k, :receivers] - got[k:, receivers:]
            imag = got[:k, receivers:] + got[k:, :receivers]
            for p, v in enumerate([real, imag]):
                for b, cut in zip((pair, pair + 1), exchanged(v[:n], v[n:])):
                    w2[pl.ds(b * 2 + p, n, stride=8), :] = cut
        send2[h] = w2[...].reshape(n, 8, receivers).astype(jnp.bfloat16)
        exchange(send2.at[h], recv2.at[h], send2_sem.at[h], recv2_sem.at[h])
        return carry

    lax.fori_loop(0, halves, to_shots, 0)

    pltpu.make_async_copy(energies, energies, energy_recv).wait()
    total[...] = sum(energies[i] for i in range(patches))

    for block in range(BLOCKS):
        for halo in halo_copies(block):
            halo.wait_send()
    for halo in raw_halos:
        halo.wait_send()
    for i in range(1, patches):
        pltpu.make_async_remote_copy(
            energy, energies.at[x], energy_send.at[i], energy_recv,
            device_id={"patch": (x + i) % patches}, device_id_type=MESH,
        ).wait_send()
    others = pl.ds(0, n - 1)
    for h in range(halves):
        pltpu.make_async_copy(send1.at[h, others], send1.at[h, others], send1_sem.at[h]).wait()

    def to_samples(h, carry):
        pltpu.make_async_copy(recv2.at[h], recv2.at[h], recv2_sem.at[h]).wait()
        field = recv2[h].astype(jnp.float32).reshape(8 * n, receivers).astype(jnp.bfloat16)
        got = lax.dot_general(field, table[...], (((0,), (0,)), ((), ())), preferred_element_type=jnp.float32)
        for s in range(shots):
            out[s, pl.ds(pl.multiple_of(h * part, part), part), :] = got[s * part : (s + 1) * part]
        return carry

    lax.fori_loop(0, halves, to_samples, 0)

    for h in range(halves):
        pltpu.make_async_copy(send2.at[h, others], send2.at[h, others], send2_sem.at[h]).wait()


def finish(count, field, total, out, misfit, means, sems):
    shots = field.shape[0]
    copies = [pltpu.make_async_copy(field.at[s], out.at[s], sems.at[s]) for s in range(shots)]
    for copy in copies:
        copy.start()
    for s in range(shots):
        means[s] = jnp.sum(total[s]) / count
    copies.append(pltpu.make_async_copy(means, misfit, sems.at[shots]))
    copies[-1].start()
    for copy in copies:
        copy.wait()


def local(dims, estimate, observed, delays, thresholds):
    shots, receivers, length = estimate.shape
    n = dims[1]
    frequencies = thresholds.shape[0]
    bf16, f32 = jnp.bfloat16, jnp.float32
    halves = 2
    table = jnp.asarray(time_table(frequencies, length))
    cn = jnp.asarray(shot_table(n * shots, shots))
    sem = pltpu.SemaphoreType.DMA
    vmem = pl.BlockSpec(memory_space=pltpu.VMEM)
    operands = (estimate, observed, delays, thresholds, table, cn)
    field, total = pl.pallas_call(
        functools.partial(kernel, dims),
        out_shape=(
            jax.ShapeDtypeStruct((shots, receivers, length), f32),
            jax.ShapeDtypeStruct((shots, 8, 128), f32),
        ),
        in_specs=[pl.BlockSpec(memory_space=pltpu.HBM)] * 6,
        out_specs=(vmem, vmem),
        scratch_shapes=[
            pltpu.VMEM(estimate.shape, bf16),
            pltpu.VMEM(estimate.shape, bf16),
            pltpu.SMEM(delays.shape, jnp.int32),
            pltpu.SMEM(thresholds.shape, f32),
            pltpu.VMEM(table.shape, bf16),
            pltpu.VMEM(cn.shape, bf16),
            pltpu.VMEM((2, receivers, length), bf16),
            pltpu.VMEM((2, receivers, length), bf16),
            pltpu.VMEM((2, receivers, LONGEST), bf16),
            pltpu.VMEM(estimate.shape, f32),
            pltpu.VMEM(estimate.shape, f32),
            pltpu.VMEM((halves, shots * receivers // halves, length), bf16),
            pltpu.VMEM((shots, 8, 128), f32),
            pltpu.VMEM((dims[0], shots, 8, 128), f32),
            pltpu.VMEM((halves, n, 8, receivers), bf16),
            pltpu.VMEM((halves, n, 8, receivers), bf16),
            pltpu.VMEM((halves, n * 8, receivers), f32),
            pltpu.VMEM((halves, n * 8, receivers), f32),
            pltpu.VMEM((halves, n, 8, receivers), bf16),
            pltpu.VMEM((halves, n, 8, receivers), bf16),
            sem((4,)),
            sem((2, BLOCKS)),
            sem((2, BLOCKS)),
            sem((2, BLOCKS)),
            sem((2,)),
            sem((2,)),
            pltpu.SemaphoreType.REGULAR,
            sem((halves,)),
            sem((halves,)),
            sem((halves,)),
            sem((halves,)),
            sem((dims[0],)),
            sem,
        ],
        compiler_params=pltpu.CompilerParams(
            collective_id=0, has_side_effects=True, vmem_limit_bytes=48 * 2**20
        ),
    )(*[pltpu.with_memory_space_constraint(v, pltpu.HBM) for v in operands])
    return pl.pallas_call(
        functools.partial(finish, dims[0] * receivers * length),
        out_shape=(jax.ShapeDtypeStruct(field.shape, f32), jax.ShapeDtypeStruct((shots,), f32)),
        in_specs=[vmem, vmem],
        out_specs=(pl.BlockSpec(memory_space=pltpu.HBM), pl.BlockSpec(memory_space=pltpu.HBM)),
        scratch_shapes=[pltpu.SMEM((shots,), f32), sem((shots + 1,))],
        compiler_params=pltpu.CompilerParams(vmem_limit_bytes=8 * 2**20),
    )(field, total)


def solution(mesh):
    patches, n = mesh.shape["patch"], mesh.shape["shot"]
    rings = 8
    dims = (patches, n, rings, n // rings)
    in_specs = (P("shot", "patch", None), P("shot", "patch", None), P(), P())
    out_specs = (P("shot", "patch", None), P("shot"))
    return jax.shard_map(
        functools.partial(local, dims), mesh=mesh, in_specs=in_specs, out_specs=out_specs, check_vma=False
    )
```

```python
import functools
import math

import jax
import jax.numpy as jnp
import ml_dtypes
import numpy as np
from jax import lax
from jax.experimental import pallas as pl
from jax.experimental.pallas import tpu as pltpu
from jax.sharding import PartitionSpec as P

SOURCE_SPACING = 512
LONGEST = 768
ROWS = 16
BLOCKS = 4
MESH = pl.DeviceIdType.MESH


def time_table(frequencies, samples, n, halves):
    phase = np.arange(frequencies)[:, None] * np.arange(samples)[None, :] % samples
    angle = 2.0 * math.pi * phase / samples
    table = np.stack([np.cos(angle), -np.sin(angle)], axis=1) / math.sqrt(samples)
    table = table.reshape(n, halves, -1, samples).swapaxes(0, 1)
    return table.reshape(2 * frequencies, samples).astype(np.float32).astype(ml_dtypes.bfloat16)


def shot_table(shots, here):
    index = np.arange(shots).reshape(shots // here, here).T.reshape(-1)
    angle = 2.0 * math.pi * (index[:, None] * index[None, :] % shots) / shots
    table = np.concatenate([np.cos(angle), np.sin(angle)]) / math.sqrt(shots)
    return table.astype(np.float32).astype(ml_dtypes.bfloat16)


def shift_left(x, lane, offset):
    length = x.shape[1]
    return jnp.where(lane < length - offset, pltpu.roll(x, (2 * length - offset) % length, 1), 0.0)


def shift_right(x, lane, offset):
    return jnp.where(lane >= offset, pltpu.roll(x, offset % x.shape[1], 1), 0.0)


def kernel(
    dims,
    est_hbm, obs_hbm, delay_hbm, level_hbm, table_hbm, cn_hbm,
    out, total,
    est, obs, delay, level, table, cn,
    halo_out, halo_in, est_in, partial, base, stepped, energy, energies,
    send1, recv1, wide1, wide2, send2, recv2,
    load_sem, record_sem, halo_send, halo_recv, est_send, est_recv, plane_sem,
    send1_sem, recv1_sem, send2_sem, recv2_sem, energy_send, energy_recv,
):
    patches, n, rings, ring = dims
    shots, receivers, length = est.shape
    rest = length - LONGEST
    halves = wide1.shape[0]
    bands = 2 * halves
    me, x = lax.axis_index("shot"), lax.axis_index("patch")
    z, place = me // ring, me % ring
    right, left = (me + 1) % n, (me + n - 1) % n
    last = n * shots - 1

    loads = [
        pltpu.make_async_copy(src, dst, load_sem.at[i])
        for i, (src, dst) in enumerate([(delay_hbm, delay), (level_hbm, level), (table_hbm, table), (cn_hbm, cn)])
    ]

    def record_loads(block):
        rows = pl.ds(block * (receivers // BLOCKS), receivers // BLOCKS)
        return [
            pltpu.make_async_copy(src.at[:, rows], dst.at[:, rows], record_sem.at[i, block])
            for i, (src, dst) in enumerate([(est_hbm, est), (obs_hbm, obs)])
        ]

    loads[0].start()
    for block in range(BLOCKS):
        for load in record_loads(block):
            load.start()
    for load in loads[1:]:
        load.start()

    barrier = pltpu.get_barrier_semaphore()

    def greet_ring(i, carry):
        pl.semaphore_signal(barrier, 1, device_id={"shot": z * ring + (place + i) % ring}, device_id_type=MESH)
        return carry

    def greet_planes(i, carry):
        pl.semaphore_signal(barrier, 1, device_id={"shot": (z + i) % rings * ring + place}, device_id_type=MESH)
        return carry

    def greet_patches(i, carry):
        pl.semaphore_signal(barrier, 1, device_id={"patch": (x + i) % patches}, device_id_type=MESH)
        return carry

    pl.semaphore_signal(barrier, 1, device_id={"shot": right}, device_id_type=MESH)
    pl.semaphore_signal(barrier, 1, device_id={"shot": left}, device_id_type=MESH)
    lax.fori_loop(1, ring, greet_ring, 0)
    lax.fori_loop(1, rings, greet_planes, 0)
    lax.fori_loop(1, patches, greet_patches, 0)

    loads[0].wait()
    first = me * shots
    delays = [delay[jnp.clip(first + i, 0, last)] for i in range(-2, 4)]
    a_prev, a_before, a_here, a_after, a_next = [SOURCE_SPACING + b - a for a, b in zip(delays, delays[1:])]
    has_left = me > 0
    has_right = me < n - 1
    lane = lax.broadcasted_iota(jnp.int32, (ROWS, length), 1)
    lane_rest = lax.broadcasted_iota(jnp.int32, (ROWS, rest), 1)

    def before_halo(i, carry):
        rows = pl.ds(i * ROWS, ROWS)
        e0 = est[0, rows, :].astype(jnp.float32)
        e1 = est[1, rows, :].astype(jnp.float32)
        p0 = obs[0, rows, :].astype(jnp.float32) - e0 - shift_right(e1, lane, a_here)
        p1 = obs[1, rows, :].astype(jnp.float32) - e1 - shift_left(e0, lane, a_here)
        partial[0, rows, :] = p0
        partial[1, rows, :] = p1
        once = shift_left(p1 - e1, lane, a_after)[:, :LONGEST]
        twice = shift_left(e1[:, LONGEST:], lane_rest, a_after + a_next - LONGEST)
        halo_out[0, rows, :] = jnp.concatenate([once, twice], axis=1).astype(jnp.bfloat16)
        once = shift_right(p0 - e0, lane, a_before)[:, rest:]
        twice = shift_right(e0[:, :rest], lane_rest, a_before + a_prev - LONGEST)
        halo_out[1, rows, :] = jnp.concatenate([once, twice], axis=1).astype(jnp.bfloat16)
        return carry

    def halo_copies(block):
        rows = pl.ds(block * (receivers // BLOCKS), receivers // BLOCKS)
        return [
            pltpu.make_async_remote_copy(
                halo_out.at[side, rows], halo_in.at[side, rows], halo_send.at[side, block], halo_recv.at[side, block],
                device_id={"shot": peer}, device_id_type=MESH,
            )
            for side, peer in enumerate([right, left])
        ]

    def plane_ready(i, carry):
        pl.semaphore_signal(plane_sem, 1, device_id={"shot": (z + i) % rings * ring + place}, device_id_type=MESH)
        return carry

    steps = receivers // ROWS // BLOCKS
    for block in range(BLOCKS):
        for load in record_loads(block):
            load.wait()
        lax.fori_loop(block * steps, (block + 1) * steps, before_halo, 0)
        if block == 0:
            pl.semaphore_wait(barrier, ring - 1 + rings - 1 + patches - 1 + 2)
            lax.fori_loop(1, rings, plane_ready, 0)
        for halo in halo_copies(block):
            halo.start()

    raw_halos = [
        pltpu.make_async_remote_copy(
            est.at[1 - side, :, pl.ds(rest * (1 - side), LONGEST)], est_in.at[side], est_send.at[side], est_recv.at[side],
            device_id={"shot": peer}, device_id_type=MESH,
        )
        for side, peer in enumerate([right, left])
    ]
    for halo in raw_halos:
        halo.start()

    def own_part(i, carry):
        rows = pl.ds(i * ROWS, ROWS)
        e0 = est[0, rows, :].astype(jnp.float32)
        e1 = est[1, rows, :].astype(jnp.float32)
        p0 = partial[0, rows, :]
        p1 = partial[1, rows, :]
        own0 = jnp.where(lane < jnp.where(has_left, length - a_before, 0), e0, 0.0)
        own1 = jnp.where(lane >= jnp.where(has_right, a_after, length), e1, 0.0)
        base[0, rows, :] = e0 + 0.5 * (p0 + shift_right(p1, lane, a_here) - own0)
        base[1, rows, :] = e1 + 0.5 * (p1 + shift_left(p0, lane, a_here) - own1)
        return carry

    lax.fori_loop(0, receivers // ROWS, own_part, 0)
    for load in loads[1:]:
        load.wait()

    def after_halo(i, carry):
        rows = pl.ds(i * ROWS, ROWS)
        from_left = jnp.where(has_left, halo_in[0, rows, :].astype(jnp.float32), 0.0)
        from_right = jnp.where(has_right, halo_in[1, rows, :].astype(jnp.float32), 0.0)
        h0 = jnp.concatenate([from_left[:, :LONGEST], -from_right[:, LONGEST:]], axis=1)
        h1 = jnp.concatenate([-from_left[:, LONGEST:], from_right[:, :LONGEST]], axis=1)
        stepped[rows, :] = (base[0, rows, :] + 0.5 * h0).astype(jnp.bfloat16)
        stepped[pl.ds(receivers + i * ROWS, ROWS), :] = (base[1, rows, :] + 0.5 * h1).astype(jnp.bfloat16)
        return carry

    for block in range(BLOCKS):
        for halo in halo_copies(block):
            halo.wait_recv()
        lax.fori_loop(block * steps, (block + 1) * steps, after_halo, 0)


    half = rings // 2
    place_y, core = place // 2, place % 2
    at_z = [lax.rem(z + dz, rings) * ring for dz in range(rings)]
    at_y = [lax.rem(place_y + dy, rings) * 2 for dy in range(rings)]
    at_core = [core, 1 - core]
    peers = [
        at_z[dz] + at_y[dy] + at_core[dc]
        for hops in range(2 * half, -1, -1)
        for far_z in range(half + 1)
        for far_y in range(half + 1)
        if far_z + far_y == hops
        for dz in sorted({far_z, (rings - far_z) % rings})
        for dy in sorted({far_y, (rings - far_y) % rings})
        for dc in range(2)
        if dz or dy or dc
    ]

    def exchange(src, dst, ssem, rsem):
        for peer in peers:
            pltpu.make_async_remote_copy(
                src.at[peer], dst.at[me], ssem, rsem, device_id={"shot": peer}, device_id_type=MESH
            ).start()
        pltpu.make_async_copy(src.at[me], dst.at[me], rsem).start()

    upper = lax.broadcasted_iota(jnp.int32, (n // 2, 8, receivers), 1) < 4

    def to_frequencies(h, carry):
        rows = table[pl.ds(pl.multiple_of(h * 4 * n, 4 * n), 4 * n), :]
        got = lax.dot_general(rows, stepped[...], (((1,), (1,)), ((), ())), preferred_element_type=jnp.float32)
        pairs = got.reshape(n // 2, 8, shots * receivers)
        g0, g1 = pairs[:, :, :receivers], pairs[:, :, receivers:]
        even = jnp.where(upper, g0, pltpu.roll(g1, 4, 1))
        odd = jnp.where(upper, pltpu.roll(g0, 4, 1), g1)
        send1[h] = jnp.stack([even, odd], axis=1).reshape(n, 8, receivers).astype(jnp.bfloat16)

        @pl.when(h == 0)
        def _():
            pl.semaphore_wait(plane_sem, rings - 1)

        exchange(send1.at[h], recv1.at[h], send1_sem.at[h], recv1_sem.at[h])
        return carry

    lax.fori_loop(0, halves, to_frequencies, 0)

    for halo in raw_halos:
        halo.wait_recv()

    def misfit_part(i, carry):
        rows = pl.ds(i * ROWS, ROWS)
        blank = jnp.zeros((ROWS, rest), jnp.float32)
        from_left = jnp.concatenate([blank, est_in[0, rows, :].astype(jnp.float32)], axis=1)
        from_right = jnp.concatenate([est_in[1, rows, :].astype(jnp.float32), blank], axis=1)
        r0 = partial[0, rows, :] - jnp.where(has_left, shift_left(from_left, lane, a_before), 0.0)
        r1 = partial[1, rows, :] - jnp.where(has_right, shift_right(from_right, lane, a_after), 0.0)

        def squares(r):
            parts = jnp.zeros((8, 128), jnp.float32)
            for a in range(0, ROWS, 8):
                for b in range(0, length, 128):
                    piece = r[a : a + 8, b : b + 128]
                    parts = parts + piece * piece
            return parts

        return carry[0] + squares(r0), carry[1] + squares(r1)

    zero = jnp.zeros((8, 128), jnp.float32)
    e_0, e_1 = lax.fori_loop(0, receivers // ROWS, misfit_part, (zero, zero))
    energy[0] = e_0
    energy[1] = e_1
    for i in range(1, patches):
        pltpu.make_async_remote_copy(
            energy, energies.at[x], energy_send.at[i], energy_recv,
            device_id={"patch": (x + i) % patches}, device_id_type=MESH,
        ).start()
    pltpu.make_async_copy(energy, energies.at[x], energy_recv).start()

    wave = cn[...]
    k = n * shots

    def to_shots(h, carry):
        pltpu.make_async_copy(recv1.at[h], recv1.at[h], recv1_sem.at[h]).wait()
        w1, w2 = wide1.at[h], wide2.at[h]
        w1[...] = recv1[h].astype(jnp.float32).reshape(8 * n, receivers)
        for b in range(bands // halves):
            columns = []
            for q in range(2):
                parts = [w1[pl.ds(s * 4 + b * 2 + q, n, stride=8), :] for s in range(shots)]
                columns.append(jnp.concatenate(parts, axis=0))
            field = jnp.concatenate(columns, axis=1).astype(jnp.bfloat16)
            got = jnp.dot(wave, field, preferred_element_type=jnp.float32)
            real = got[:k, :receivers] + got[k:, receivers:]
            imag = got[:k, receivers:] - got[k:, :receivers]
            f = me * bands + h * (bands // halves) + b
            limit = level[f]
            weight = jnp.where(f == 0, 1.0, 2.0)
            magnitude = jnp.sqrt(real * real + imag * imag)
            factor = jnp.maximum(magnitude - limit, 0.0) / jnp.maximum(magnitude, limit) * weight
            shrunk = jnp.concatenate([real * factor, imag * factor], axis=1).astype(jnp.bfloat16)
            got = jnp.dot(wave, shrunk, preferred_element_type=jnp.float32)
            real = got[:k, :receivers] - got[k:, receivers:]
            imag = got[:k, receivers:] + got[k:, :receivers]
            for s in range(shots):
                w2[pl.ds(s * 4 + b * 2, n, stride=8), :] = real[s * n : (s + 1) * n]
                w2[pl.ds(s * 4 + b * 2 + 1, n, stride=8), :] = imag[s * n : (s + 1) * n]
        send2[h] = w2[...].reshape(n, 8, receivers).astype(jnp.bfloat16)
        exchange(send2.at[h], recv2.at[h], send2_sem.at[h], recv2_sem.at[h])
        return carry

    lax.fori_loop(0, halves, to_shots, 0)

    pltpu.make_async_copy(energies, energies, energy_recv).wait()
    total[...] = sum(energies[i] for i in range(patches))

    for block in range(BLOCKS):
        for halo in halo_copies(block):
            halo.wait_send()
    for halo in raw_halos:
        halo.wait_send()
    for i in range(1, patches):
        pltpu.make_async_remote_copy(
            energy, energies.at[x], energy_send.at[i], energy_recv,
            device_id={"patch": (x + i) % patches}, device_id_type=MESH,
        ).wait_send()
    others = pl.ds(0, n - 1)
    for h in range(halves):
        pltpu.make_async_copy(send1.at[h, others], send1.at[h, others], send1_sem.at[h]).wait()

    for h in range(halves):
        pltpu.make_async_copy(recv2.at[h], recv2.at[h], recv2_sem.at[h]).wait()
        pairs = recv2[h].astype(jnp.float32).reshape(n // 2, 2, 8, receivers)
        even, odd = pairs[:, 0], pairs[:, 1]
        fields = [
            jnp.where(upper, even, pltpu.roll(odd, 4, 1)),
            jnp.where(upper, pltpu.roll(even, 4, 1), odd),
        ]
        rows = table[h * 4 * n : (h + 1) * 4 * n, :]
        for s in range(shots):
            field = fields[s].reshape(4 * n, receivers).astype(jnp.bfloat16)
            got = lax.dot_general(field, rows, (((0,), (0,)), ((), ())), preferred_element_type=jnp.float32)
            out[s] = got if h == 0 else out[s] + got

    for h in range(halves):
        pltpu.make_async_copy(send2.at[h, others], send2.at[h, others], send2_sem.at[h]).wait()


def finish(count, field, total, out, misfit, means, sems):
    shots = field.shape[0]
    copies = [pltpu.make_async_copy(field.at[s], out.at[s], sems.at[s]) for s in range(shots)]
    for copy in copies:
        copy.start()
    for s in range(shots):
        means[s] = jnp.sum(total[s]) / count
    copies.append(pltpu.make_async_copy(means, misfit, sems.at[shots]))
    copies[-1].start()
    for copy in copies:
        copy.wait()


def local(dims, estimate, observed, delays, thresholds):
    shots, receivers, length = estimate.shape
    n = dims[1]
    frequencies = thresholds.shape[0]
    bf16, f32 = jnp.bfloat16, jnp.float32
    bands = frequencies // n
    halves = bands // 2
    table = jnp.asarray(time_table(frequencies, length, n, halves))
    cn = jnp.asarray(shot_table(n * shots, shots))
    sem = pltpu.SemaphoreType.DMA
    vmem = pl.BlockSpec(memory_space=pltpu.VMEM)
    operands = (estimate, observed, delays, thresholds, table, cn)
    field, total = pl.pallas_call(
        functools.partial(kernel, dims),
        out_shape=(
            jax.ShapeDtypeStruct((shots, receivers, length), f32),
            jax.ShapeDtypeStruct((shots, 8, 128), f32),
        ),
        in_specs=[pl.BlockSpec(memory_space=pltpu.HBM)] * 6,
        out_specs=(vmem, vmem),
        scratch_shapes=[
            pltpu.VMEM(estimate.shape, bf16),
            pltpu.VMEM(estimate.shape, bf16),
            pltpu.SMEM(delays.shape, jnp.int32),
            pltpu.SMEM(thresholds.shape, f32),
            pltpu.VMEM(table.shape, bf16),
            pltpu.VMEM(cn.shape, bf16),
            pltpu.VMEM((2, receivers, length), bf16),
            pltpu.VMEM((2, receivers, length), bf16),
            pltpu.VMEM((2, receivers, LONGEST), bf16),
            pltpu.VMEM(estimate.shape, f32),
            pltpu.VMEM(estimate.shape, f32),
            pltpu.VMEM((shots * receivers, length), bf16),
            pltpu.VMEM((shots, 8, 128), f32),
            pltpu.VMEM((dims[0], shots, 8, 128), f32),
            pltpu.VMEM((halves, n, 8, receivers), bf16),
            pltpu.VMEM((halves, n, 8, receivers), bf16),
            pltpu.VMEM((halves, n * 8, receivers), f32),
            pltpu.VMEM((halves, n * 8, receivers), f32),
            pltpu.VMEM((halves, n, 8, receivers), bf16),
            pltpu.VMEM((halves, n, 8, receivers), bf16),
            sem((4,)),
            sem((2, BLOCKS)),
            sem((2, BLOCKS)),
            sem((2, BLOCKS)),
            sem((2,)),
            sem((2,)),
            pltpu.SemaphoreType.REGULAR,
            sem((halves,)),
            sem((halves,)),
            sem((halves,)),
            sem((halves,)),
            sem((dims[0],)),
            sem,
        ],
        compiler_params=pltpu.CompilerParams(
            collective_id=0, has_side_effects=True, vmem_limit_bytes=48 * 2**20
        ),
    )(*[pltpu.with_memory_space_constraint(v, pltpu.HBM) for v in operands])
    return pl.pallas_call(
        functools.partial(finish, dims[0] * receivers * length),
        out_shape=(jax.ShapeDtypeStruct(field.shape, f32), jax.ShapeDtypeStruct((shots,), f32)),
        in_specs=[vmem, vmem],
        out_specs=(pl.BlockSpec(memory_space=pltpu.HBM), pl.BlockSpec(memory_space=pltpu.HBM)),
        scratch_shapes=[pltpu.SMEM((shots,), f32), sem((shots + 1,))],
        compiler_params=pltpu.CompilerParams(vmem_limit_bytes=8 * 2**20),
    )(field, total)


def solution(mesh):
    patches, n = mesh.shape["patch"], mesh.shape["shot"]
    rings = 8
    dims = (patches, n, rings, n // rings)
    in_specs = (P("shot", "patch", None), P("shot", "patch", None), P(), P())
    out_specs = (P("shot", "patch", None), P("shot"))
    return jax.shard_map(
        functools.partial(local, dims), mesh=mesh, in_specs=in_specs, out_specs=out_specs, check_vma=False
    )
```

```python
import functools
import math

import jax
import jax.numpy as jnp
import ml_dtypes
import numpy as np
from jax import lax
from jax.experimental import pallas as pl
from jax.experimental.pallas import tpu as pltpu
from jax.sharding import PartitionSpec as P

SOURCE_SPACING = 512
LONGEST = 768
ROWS = 16
BLOCKS = 4
MESH = pl.DeviceIdType.MESH


def time_table(frequencies, samples, n, halves):
    phase = np.arange(frequencies)[:, None] * np.arange(samples)[None, :] % samples
    angle = 2.0 * math.pi * phase / samples
    table = np.stack([np.cos(angle), -np.sin(angle)], axis=1) / math.sqrt(samples)
    table = table.reshape(n, halves, -1, samples).swapaxes(0, 1)
    return table.reshape(2 * frequencies, samples).astype(np.float32).astype(ml_dtypes.bfloat16)


def shot_table(shots, here):
    index = np.arange(shots).reshape(shots // here, here).T.reshape(-1)
    angle = 2.0 * math.pi * (index[:, None] * index[None, :] % shots) / shots
    table = np.concatenate([np.cos(angle), np.sin(angle)]) / math.sqrt(shots)
    return table.astype(np.float32).astype(ml_dtypes.bfloat16)


def shift_left(x, lane, offset):
    length = x.shape[1]
    return jnp.where(lane < length - offset, pltpu.roll(x, (2 * length - offset) % length, 1), 0.0)


def shift_right(x, lane, offset):
    return jnp.where(lane >= offset, pltpu.roll(x, offset % x.shape[1], 1), 0.0)


def kernel(
    dims,
    est_hbm, obs_hbm, delay_hbm, level_hbm, table_hbm, cn_hbm,
    out, total,
    est, obs, delay, level, table, cn,
    halo_out, halo_in, est_in, partial, base, stepped, energy, energies,
    send1, recv1, wide1, wide2, send2, recv2,
    load_sem, record_sem, halo_send, halo_recv, est_send, est_recv, plane_sem,
    send1_sem, recv1_sem, send2_sem, recv2_sem, energy_send, energy_recv,
):
    patches, n, rings, ring = dims
    shots, receivers, length = est.shape
    rest = length - LONGEST
    halves = wide1.shape[0]
    bands = 2 * halves
    me, x = lax.axis_index("shot"), lax.axis_index("patch")
    z, place = me // ring, me % ring
    right, left = (me + 1) % n, (me + n - 1) % n
    last = n * shots - 1

    loads = [
        pltpu.make_async_copy(src, dst, load_sem.at[i])
        for i, (src, dst) in enumerate([(delay_hbm, delay), (level_hbm, level), (table_hbm, table), (cn_hbm, cn)])
    ]

    def record_loads(block):
        rows = pl.ds(block * (receivers // BLOCKS), receivers // BLOCKS)
        return [
            pltpu.make_async_copy(src.at[:, rows], dst.at[:, rows], record_sem.at[i, block])
            for i, (src, dst) in enumerate([(est_hbm, est), (obs_hbm, obs)])
        ]

    loads[0].start()
    for block in range(BLOCKS):
        for load in record_loads(block):
            load.start()

    barrier = pltpu.get_barrier_semaphore()

    def greet(**peer):
        pl.semaphore_signal(barrier, 1, device_id=peer, device_id_type=MESH)

    def far_first(size):
        return sorted(range(1, size), key=lambda i: -min(i, size - i))

    greet(shot=right)
    greet(shot=left)
    for i in far_first(ring):
        greet(shot=z * ring + lax.rem(place + i, ring))
    for i in far_first(rings):
        greet(shot=lax.rem(z + i, rings) * ring + place)
    for i in far_first(patches):
        greet(patch=lax.rem(x + i, patches))
    for load in loads[1:]:
        load.start()

    loads[0].wait()
    first = me * shots
    delays = [delay[jnp.clip(first + i, 0, last)] for i in range(-2, 4)]
    a_prev, a_before, a_here, a_after, a_next = [SOURCE_SPACING + b - a for a, b in zip(delays, delays[1:])]
    has_left = me > 0
    has_right = me < n - 1
    lane = lax.broadcasted_iota(jnp.int32, (ROWS, length), 1)
    lane_rest = lax.broadcasted_iota(jnp.int32, (ROWS, rest), 1)

    def before_halo(i, carry):
        rows = pl.ds(i * ROWS, ROWS)
        e0 = est[0, rows, :].astype(jnp.float32)
        e1 = est[1, rows, :].astype(jnp.float32)
        p0 = obs[0, rows, :].astype(jnp.float32) - e0 - shift_right(e1, lane, a_here)
        p1 = obs[1, rows, :].astype(jnp.float32) - e1 - shift_left(e0, lane, a_here)
        partial[0, rows, :] = p0
        partial[1, rows, :] = p1
        once = shift_left(p1 - e1, lane, a_after)[:, :LONGEST]
        twice = shift_left(e1[:, LONGEST:], lane_rest, a_after + a_next - LONGEST)
        halo_out[0, rows, :] = jnp.concatenate([once, twice], axis=1).astype(jnp.bfloat16)
        once = shift_right(p0 - e0, lane, a_before)[:, rest:]
        twice = shift_right(e0[:, :rest], lane_rest, a_before + a_prev - LONGEST)
        halo_out[1, rows, :] = jnp.concatenate([once, twice], axis=1).astype(jnp.bfloat16)
        return carry

    def halo_copies(block):
        rows = pl.ds(block * (receivers // BLOCKS), receivers // BLOCKS)
        return [
            pltpu.make_async_remote_copy(
                halo_out.at[side, rows], halo_in.at[side, rows], halo_send.at[side, block], halo_recv.at[side, block],
                device_id={"shot": peer}, device_id_type=MESH,
            )
            for side, peer in enumerate([right, left])
        ]

    steps = receivers // ROWS // BLOCKS
    for block in range(BLOCKS):
        for load in record_loads(block):
            load.wait()
        lax.fori_loop(block * steps, (block + 1) * steps, before_halo, 0)
        if block == 0:
            pl.semaphore_wait(barrier, ring - 1 + rings - 1 + patches - 1 + 2)
            for i in far_first(rings):
                peer = lax.rem(z + i, rings) * ring + place
                pl.semaphore_signal(plane_sem, 1, device_id={"shot": peer}, device_id_type=MESH)
        for halo in halo_copies(block):
            halo.start()

    raw_halos = [
        pltpu.make_async_remote_copy(
            est.at[1 - side, :, pl.ds(rest * (1 - side), LONGEST)], est_in.at[side], est_send.at[side], est_recv.at[side],
            device_id={"shot": peer}, device_id_type=MESH,
        )
        for side, peer in enumerate([right, left])
    ]
    for halo in raw_halos:
        halo.start()

    def own_part(i, carry):
        rows = pl.ds(i * ROWS, ROWS)
        e0 = est[0, rows, :].astype(jnp.float32)
        e1 = est[1, rows, :].astype(jnp.float32)
        p0 = partial[0, rows, :]
        p1 = partial[1, rows, :]
        own0 = jnp.where(lane < jnp.where(has_left, length - a_before, 0), e0, 0.0)
        own1 = jnp.where(lane >= jnp.where(has_right, a_after, length), e1, 0.0)
        base[0, rows, :] = e0 + 0.5 * (p0 + shift_right(p1, lane, a_here) - own0)
        base[1, rows, :] = e1 + 0.5 * (p1 + shift_left(p0, lane, a_here) - own1)
        return carry

    lax.fori_loop(0, receivers // ROWS, own_part, 0)
    for load in loads[1:]:
        load.wait()

    def after_halo(i, carry):
        rows = pl.ds(i * ROWS, ROWS)
        from_left = jnp.where(has_left, halo_in[0, rows, :].astype(jnp.float32), 0.0)
        from_right = jnp.where(has_right, halo_in[1, rows, :].astype(jnp.float32), 0.0)
        h0 = jnp.concatenate([from_left[:, :LONGEST], -from_right[:, LONGEST:]], axis=1)
        h1 = jnp.concatenate([-from_left[:, LONGEST:], from_right[:, :LONGEST]], axis=1)
        stepped[rows, :] = (base[0, rows, :] + 0.5 * h0).astype(jnp.bfloat16)
        stepped[pl.ds(receivers + i * ROWS, ROWS), :] = (base[1, rows, :] + 0.5 * h1).astype(jnp.bfloat16)
        return carry

    for block in range(BLOCKS):
        for halo in halo_copies(block):
            halo.wait_recv()
        lax.fori_loop(block * steps, (block + 1) * steps, after_halo, 0)


    half = rings // 2
    place_y, core = place // 2, place % 2
    at_z = [lax.rem(z + dz, rings) * ring for dz in range(rings)]
    at_y = [lax.rem(place_y + dy, rings) * 2 for dy in range(rings)]
    at_core = [core, 1 - core]
    peers = [
        at_z[dz] + at_y[dy] + at_core[dc]
        for hops in range(2 * half, -1, -1)
        for far_z in range(half + 1)
        for far_y in range(half + 1)
        if far_z + far_y == hops
        for dz in sorted({far_z, (rings - far_z) % rings})
        for dy in sorted({far_y, (rings - far_y) % rings})
        for dc in range(2)
        if dz or dy or dc
    ]

    def exchange(src, dst, ssem, rsem):
        for peer in peers:
            pltpu.make_async_remote_copy(
                src.at[peer], dst.at[me], ssem, rsem, device_id={"shot": peer}, device_id_type=MESH
            ).start()
        pltpu.make_async_copy(src.at[me], dst.at[me], rsem).start()

    upper = lax.broadcasted_iota(jnp.int32, (n // 2, 8, receivers), 1) < 4

    def to_frequencies(h, carry):
        rows = table[pl.ds(pl.multiple_of(h * 4 * n, 4 * n), 4 * n), :]
        got = lax.dot_general(rows, stepped[...], (((1,), (1,)), ((), ())), preferred_element_type=jnp.float32)
        pairs = got.reshape(n // 2, 8, shots * receivers)
        g0, g1 = pairs[:, :, :receivers], pairs[:, :, receivers:]
        even = jnp.where(upper, g0, pltpu.roll(g1, 4, 1))
        odd = jnp.where(upper, pltpu.roll(g0, 4, 1), g1)
        send1[h] = jnp.stack([even, odd], axis=1).reshape(n, 8, receivers).astype(jnp.bfloat16)

        @pl.when(h == 0)
        def _():
            pl.semaphore_wait(plane_sem, rings - 1)

        exchange(send1.at[h], recv1.at[h], send1_sem.at[h], recv1_sem.at[h])
        return carry

    lax.fori_loop(0, halves, to_frequencies, 0)

    for halo in raw_halos:
        halo.wait_recv()

    def misfit_part(i, carry):
        rows = pl.ds(i * ROWS, ROWS)
        blank = jnp.zeros((ROWS, rest), jnp.float32)
        from_left = jnp.concatenate([blank, est_in[0, rows, :].astype(jnp.float32)], axis=1)
        from_right = jnp.concatenate([est_in[1, rows, :].astype(jnp.float32), blank], axis=1)
        r0 = partial[0, rows, :] - jnp.where(has_left, shift_left(from_left, lane, a_before), 0.0)
        r1 = partial[1, rows, :] - jnp.where(has_right, shift_right(from_right, lane, a_after), 0.0)

        def squares(r):
            parts = jnp.zeros((8, 128), jnp.float32)
            for a in range(0, ROWS, 8):
                for b in range(0, length, 128):
                    piece = r[a : a + 8, b : b + 128]
                    parts = parts + piece * piece
            return parts

        return carry[0] + squares(r0), carry[1] + squares(r1)

    zero = jnp.zeros((8, 128), jnp.float32)
    e_0, e_1 = lax.fori_loop(0, receivers // ROWS, misfit_part, (zero, zero))
    energy[0] = e_0
    energy[1] = e_1
    for i in range(1, patches):
        pltpu.make_async_remote_copy(
            energy, energies.at[x], energy_send.at[i], energy_recv,
            device_id={"patch": (x + i) % patches}, device_id_type=MESH,
        ).start()
    pltpu.make_async_copy(energy, energies.at[x], energy_recv).start()

    wave = cn[...]
    k = n * shots

    def to_shots(h, carry):
        pltpu.make_async_copy(recv1.at[h], recv1.at[h], recv1_sem.at[h]).wait()
        w1, w2 = wide1.at[h], wide2.at[h]
        w1[...] = recv1[h].astype(jnp.float32).reshape(8 * n, receivers)
        for b in range(bands // halves):
            columns = []
            for q in range(2):
                parts = [w1[pl.ds(s * 4 + b * 2 + q, n, stride=8), :] for s in range(shots)]
                columns.append(jnp.concatenate(parts, axis=0))
            field = jnp.concatenate(columns, axis=1).astype(jnp.bfloat16)
            got = jnp.dot(wave, field, preferred_element_type=jnp.float32)
            real = got[:k, :receivers] + got[k:, receivers:]
            imag = got[:k, receivers:] - got[k:, :receivers]
            f = me * bands + h * (bands // halves) + b
            limit = level[f]
            weight = jnp.where(f == 0, 1.0, 2.0)
            magnitude = jnp.sqrt(real * real + imag * imag)
            factor = jnp.maximum(magnitude - limit, 0.0) / jnp.maximum(magnitude, limit) * weight
            shrunk = jnp.concatenate([real * factor, imag * factor], axis=1).astype(jnp.bfloat16)
            got = jnp.dot(wave, shrunk, preferred_element_type=jnp.float32)
            real = got[:k, :receivers] - got[k:, receivers:]
            imag = got[:k, receivers:] + got[k:, :receivers]
            for s in range(shots):
                w2[pl.ds(s * 4 + b * 2, n, stride=8), :] = real[s * n : (s + 1) * n]
                w2[pl.ds(s * 4 + b * 2 + 1, n, stride=8), :] = imag[s * n : (s + 1) * n]
        send2[h] = w2[...].reshape(n, 8, receivers).astype(jnp.bfloat16)
        exchange(send2.at[h], recv2.at[h], send2_sem.at[h], recv2_sem.at[h])
        return carry

    lax.fori_loop(0, halves, to_shots, 0)

    pltpu.make_async_copy(energies, energies, energy_recv).wait()
    total[...] = sum(energies[i] for i in range(patches))

    for block in range(BLOCKS):
        for halo in halo_copies(block):
            halo.wait_send()
    for halo in raw_halos:
        halo.wait_send()
    for i in range(1, patches):
        pltpu.make_async_remote_copy(
            energy, energies.at[x], energy_send.at[i], energy_recv,
            device_id={"patch": (x + i) % patches}, device_id_type=MESH,
        ).wait_send()
    others = pl.ds(0, n - 1)
    for h in range(halves):
        pltpu.make_async_copy(send1.at[h, others], send1.at[h, others], send1_sem.at[h]).wait()

    for h in range(halves):
        pltpu.make_async_copy(recv2.at[h], recv2.at[h], recv2_sem.at[h]).wait()
        pairs = recv2[h].astype(jnp.float32).reshape(n // 2, 2, 8, receivers)
        even, odd = pairs[:, 0], pairs[:, 1]
        fields = [
            jnp.where(upper, even, pltpu.roll(odd, 4, 1)),
            jnp.where(upper, pltpu.roll(even, 4, 1), odd),
        ]
        rows = table[h * 4 * n : (h + 1) * 4 * n, :]
        for s in range(shots):
            field = fields[s].reshape(4 * n, receivers).astype(jnp.bfloat16)
            got = lax.dot_general(field, rows, (((0,), (0,)), ((), ())), preferred_element_type=jnp.float32)
            out[s] = got if h == 0 else out[s] + got

    for h in range(halves):
        pltpu.make_async_copy(send2.at[h, others], send2.at[h, others], send2_sem.at[h]).wait()


def finish(count, field, total, out, misfit, means, sems):
    shots = field.shape[0]
    copies = [pltpu.make_async_copy(field.at[s], out.at[s], sems.at[s]) for s in range(shots)]
    for copy in copies:
        copy.start()
    for s in range(shots):
        means[s] = jnp.sum(total[s]) / count
    copies.append(pltpu.make_async_copy(means, misfit, sems.at[shots]))
    copies[-1].start()
    for copy in copies:
        copy.wait()


def local(dims, estimate, observed, delays, thresholds):
    shots, receivers, length = estimate.shape
    n = dims[1]
    frequencies = thresholds.shape[0]
    bf16, f32 = jnp.bfloat16, jnp.float32
    bands = frequencies // n
    halves = bands // 2
    table = jnp.asarray(time_table(frequencies, length, n, halves))
    cn = jnp.asarray(shot_table(n * shots, shots))
    sem = pltpu.SemaphoreType.DMA
    vmem = pl.BlockSpec(memory_space=pltpu.VMEM)
    operands = (estimate, observed, delays, thresholds, table, cn)
    field, total = pl.pallas_call(
        functools.partial(kernel, dims),
        out_shape=(
            jax.ShapeDtypeStruct((shots, receivers, length), f32),
            jax.ShapeDtypeStruct((shots, 8, 128), f32),
        ),
        in_specs=[pl.BlockSpec(memory_space=pltpu.HBM)] * 6,
        out_specs=(vmem, vmem),
        scratch_shapes=[
            pltpu.VMEM(estimate.shape, bf16),
            pltpu.VMEM(estimate.shape, bf16),
            pltpu.SMEM(delays.shape, jnp.int32),
            pltpu.SMEM(thresholds.shape, f32),
            pltpu.VMEM(table.shape, bf16),
            pltpu.VMEM(cn.shape, bf16),
            pltpu.VMEM((2, receivers, length), bf16),
            pltpu.VMEM((2, receivers, length), bf16),
            pltpu.VMEM((2, receivers, LONGEST), bf16),
            pltpu.VMEM(estimate.shape, f32),
            pltpu.VMEM(estimate.shape, f32),
            pltpu.VMEM((shots * receivers, length), bf16),
            pltpu.VMEM((shots, 8, 128), f32),
            pltpu.VMEM((dims[0], shots, 8, 128), f32),
            pltpu.VMEM((halves, n, 8, receivers), bf16),
            pltpu.VMEM((halves, n, 8, receivers), bf16),
            pltpu.VMEM((halves, n * 8, receivers), f32),
            pltpu.VMEM((halves, n * 8, receivers), f32),
            pltpu.VMEM((halves, n, 8, receivers), bf16),
            pltpu.VMEM((halves, n, 8, receivers), bf16),
            sem((4,)),
            sem((2, BLOCKS)),
            sem((2, BLOCKS)),
            sem((2, BLOCKS)),
            sem((2,)),
            sem((2,)),
            pltpu.SemaphoreType.REGULAR,
            sem((halves,)),
            sem((halves,)),
            sem((halves,)),
            sem((halves,)),
            sem((dims[0],)),
            sem,
        ],
        compiler_params=pltpu.CompilerParams(
            collective_id=0, has_side_effects=True, vmem_limit_bytes=48 * 2**20
        ),
    )(*[pltpu.with_memory_space_constraint(v, pltpu.HBM) for v in operands])
    return pl.pallas_call(
        functools.partial(finish, dims[0] * receivers * length),
        out_shape=(jax.ShapeDtypeStruct(field.shape, f32), jax.ShapeDtypeStruct((shots,), f32)),
        in_specs=[vmem, vmem],
        out_specs=(pl.BlockSpec(memory_space=pltpu.HBM), pl.BlockSpec(memory_space=pltpu.HBM)),
        scratch_shapes=[pltpu.SMEM((shots,), f32), sem((shots + 1,))],
        compiler_params=pltpu.CompilerParams(vmem_limit_bytes=8 * 2**20),
    )(field, total)


def solution(mesh):
    patches, n = mesh.shape["patch"], mesh.shape["shot"]
    rings = 8
    dims = (patches, n, rings, n // rings)
    in_specs = (P("shot", "patch", None), P("shot", "patch", None), P(), P())
    out_specs = (P("shot", "patch", None), P("shot"))
    return jax.shard_map(
        functools.partial(local, dims), mesh=mesh, in_specs=in_specs, out_specs=out_specs, check_vma=False
    )
```
